32 devices in a mesh: rep: 8 (over y, x, core), shard: 4 (over z).
Axes of the slice: x: 2, y: 2, z: 4, core: 2. Of those that a mesh axis runs over, the one named last changes fastest.
Arguments:
- hidden_in: bfloat16 [2, 8192, 2048], P(None, ('rep', 'shard')), may hold values from -6 to 6
- prefix: int32 [2, 8], P(None, 'rep'), may hold values from 102 to 512
- ln1_gain: bfloat16 [2048], P('shard'), may hold values from 0.5 to 1.5
- ln1_bias: bfloat16 [2048], P('shard'), may hold values from -3 to 3
- qkv_weight: bfloat16 [2048, 6144], P('shard'), may hold values from -0.125 to 0.125
- q_bias: bfloat16 [2048], P('shard'), may hold values from -3 to 3
- v_bias: bfloat16 [2048], P('shard'), may hold values from -3 to 3
- out_weight: bfloat16 [2048, 2048], P('shard'), may hold values from -1.5 to 1.5
- out_bias: bfloat16 [2048], P('shard'), may hold values from -3 to 3
- ln2_gain: bfloat16 [2048], P('shard'), may hold values from 0.5 to 1.5
- ln2_bias: bfloat16 [2048], P('shard'), may hold values from -3 to 3
- fc1_weight: bfloat16 [2048, 8192], P('shard'), may hold values from -0.125 to 0.125
- fc1_bias: bfloat16 [8192], P('shard'), may hold values from -3 to 3
- fc2_weight: bfloat16 [8192, 2048], P('shard'), may hold values from -0.09375 to 0.09375
- fc2_bias: bfloat16 [2048], P('shard'), may hold values from -3 to 3
- grad_out: bfloat16 [2, 8192, 2048], P(None, ('rep', 'shard')), may hold values from -6 to 6
Outputs:
- result: bfloat16 [2, 8192, 2048], P(None, ('rep', 'shard'))
- grad_in: bfloat16 [2, 8192, 2048], P(None, ('rep', 'shard'))
- ln1_gain_grad: float32 [2048], P('shard')
- ln1_bias_grad: float32 [2048], P('shard')
- qkv_weight_grad: float32 [2048, 6144], P('shard')
- q_bias_grad: float32 [2048], P('shard')
- v_bias_grad: float32 [2048], P('shard')
- out_weight_grad: float32 [2048, 2048], P('shard')
- out_bias_grad: float32 [2048], P('shard')
- ln2_gain_grad: float32 [2048], P('shard')
- ln2_bias_grad: float32 [2048], P('shard')
- fc1_weight_grad: float32 [2048, 8192], P('shard')
- fc1_bias_grad: float32 [8192], P('shard')
- fc2_weight_grad: float32 [8192, 2048], P('shard')
- fc2_bias_grad: float32 [2048], P('shard')
The draws below stay inside these ranges and needn't reach their ends.
Inputs may be any that keep to these rules, and one draw needn't show every extreme that they name: One prefix length for each sequence.
All inputs are finite; a program needn't handle non-finite values.
Results may differ from the reference program's by a relative error of at most 0.019.
Values may be sent and summed in bfloat16 or wider, within the bound.
No kernel may reach another device: no remote copies, remote signals or barrier semaphores. Data moves between devices by JAX's collectives and lax.ppermute only.
A program may use at most 576 MiB of HBM per device.

```python
import jax
import jax.numpy as jnp
from jax import lax

D = 2048
HEADS = 16
HEAD_DIM = 128
FF = 8192
SEQ_LEN = 1024
MB = 2
TOKENS = 8192
N_REP = 8


def touch_ends(entries, stream_key, least, high):
    longest = entries.shape.index(max(entries.shape))
    spots = []
    for shift in (0, 1):
        where = [jax.random.randint(jax.random.fold_in(stream_key, axis), (), 0, length) for axis, length in enumerate(entries.shape)]
        where[longest] = (where[longest] + shift) % entries.shape[longest]
        spots.append(tuple(where))
    return entries.at[spots[0]].set(least).at[spots[1]].set(high)


def steps_of(key, extent, shards, low, largest):
    def one(axis_at, parts):
        heights = jax.random.uniform(jax.random.fold_in(jax.random.fold_in(key, 6), axis_at), (parts,), jnp.float32, low / len(shards), largest / len(shards))
        return jnp.repeat(jnp.exp(heights), extent[axis_at] // parts).reshape((-1,) + (1,) * (len(extent) - axis_at - 1))

    loudness = one(*shards[0])
    for cut in shards[1:]:
        loudness = loudness * one(*cut)
    return loudness


def bell_draw(rng, extent, width, reach, shards=(), held_as=jnp.bfloat16):
    entries = jax.random.normal(rng, extent, jnp.float32) * width
    if len(shards) > 0:
        entries = steps_of(rng, extent, shards, -0.22, 0.18) * entries
    return jnp.clip(entries, min=-reach, max=reach).astype(held_as)


def setup_inputs(seed: int = 0) -> dict:
    streams_of = jax.random.split(jax.random.key(seed), 17)
    return {
        "hidden_in": bell_draw(streams_of[0], (MB, TOKENS, D), 1.0, 6.0, ((1, 32),)),
        "prefix": touch_ends(jax.random.randint(streams_of[1], (MB, N_REP), SEQ_LEN // 10, SEQ_LEN // 2 + 1), jax.random.fold_in(streams_of[1], 1), SEQ_LEN // 10, (SEQ_LEN // 2 + 1) - 1).astype(jnp.int32),
        "ln1_gain": jnp.clip(1.0 + 0.1 * jax.random.normal(streams_of[2], (D,), jnp.float32), 0.5, 1.5).astype(jnp.bfloat16),
        "ln1_bias": bell_draw(streams_of[3], (D,), 0.5, 3.0, ((0, 4),)),
        "qkv_weight": bell_draw(streams_of[4], (D, 3 * D), D ** -0.5, 0.125, ((0, 4),)),
        "q_bias": bell_draw(streams_of[5], (D,), 0.5, 3.0, ((0, 4),)),
        "v_bias": bell_draw(streams_of[6], (D,), 0.5, 3.0, ((0, 4),)),
        "out_weight": bell_draw(streams_of[7], (D, D), (max(8 * D // SEQ_LEN, 1)) ** -0.5, 1.5, ((0, 4),)),
        "out_bias": bell_draw(streams_of[8], (D,), 0.5, 3.0, ((0, 4),)),
        "ln2_gain": jnp.clip(1.0 + 0.1 * jax.random.normal(streams_of[9], (D,), jnp.float32), 0.5, 1.5).astype(jnp.bfloat16),
        "ln2_bias": bell_draw(streams_of[10], (D,), 0.5, 3.0, ((0, 4),)),
        "fc1_weight": bell_draw(streams_of[11], (D, FF), D ** -0.5, 0.125, ((0, 4),)),
        "fc1_bias": bell_draw(streams_of[12], (FF,), 0.5, 3.0, ((0, 4),)),
        "fc2_weight": bell_draw(streams_of[13], (FF, D), (FF // 2) ** -0.5, 0.09375, ((0, 4),)),
        "fc2_bias": bell_draw(streams_of[14], (D,), 0.5, 3.0, ((0, 4),)),
        "grad_out": bell_draw(streams_of[15], (MB, TOKENS, D), 1.0, 6.0, ((1, 32),)),
    }


EPSILON = 1e-05
MASKED = -1e+30
HIGHEST = lax.Precision.HIGHEST

@jax.custom_vjp
def low(v):
    return lax.optimization_barrier(v.astype(jnp.bfloat16)).astype(jnp.float32)

@jax.custom_vjp
def low_back(v):
    return v

def low_keep(v):
    return (low(v), None)

def low_pass(kept, grad):
    return (grad,)

def back_keep(v):
    return (v, None)

def back_low(kept, grad):
    return (low(grad),)
low.defvjp(low_keep, low_pass)
low_back.defvjp(back_keep, back_low)

def normalize(values, gain_vec, shift_vec):
    centred = values - lax.optimization_barrier(jnp.mean(values, axis=-1, keepdims=True))
    spread = lax.optimization_barrier(jnp.mean(centred * centred, axis=-1, keepdims=True))
    return centred * lax.rsqrt(spread + EPSILON) * gain_vec + shift_vec

def exact_dot(left_side, right_side):
    return jnp.dot(left_side, right_side, precision=HIGHEST, preferred_element_type=jnp.float32)

def attend(seq_parts):
    queries, keys_seq, values_seq, prefix_len = seq_parts
    query_four = queries.reshape(SEQ_LEN, HEADS, HEAD_DIM)
    keys_four = keys_seq.reshape(SEQ_LEN, HEADS, HEAD_DIM)
    values_four = values_seq.reshape(SEQ_LEN, HEADS, HEAD_DIM)
    raw_scores = low_back(jnp.einsum('qhd,khd->hqk', query_four, keys_four, precision=HIGHEST)) * HEAD_DIM ** (-0.5)
    query_pos = lax.broadcasted_iota(jnp.int32, (SEQ_LEN, SEQ_LEN), 0)
    key_pos = lax.broadcasted_iota(jnp.int32, (SEQ_LEN, SEQ_LEN), 1)
    visible = (key_pos <= query_pos) | (key_pos < prefix_len)
    scores = jnp.where(visible[None], raw_scores, MASKED)
    row_max = lax.optimization_barrier(jnp.max(scores, axis=-1, keepdims=True))
    exp_terms = jnp.exp(scores - row_max)
    soft_low = low(exp_terms / lax.optimization_barrier(jnp.sum(exp_terms, axis=-1, keepdims=True)))
    context = jnp.einsum('hqk,khd->qhd', soft_low, values_four, precision=HIGHEST)
    return context.reshape(SEQ_LEN, D)

def reference(hidden_in, prefix, ln1_gain, ln1_bias, qkv_weight, q_bias, v_bias, out_weight, out_bias, ln2_gain, ln2_bias, fc1_weight, fc1_bias, fc2_weight, fc2_bias, grad_out):
    seq_count = MB * N_REP
    prefix_flat = prefix.reshape(seq_count).astype(jnp.int32)

    def forward(inputs_f, gain_one, shift_one, qkv_w, bias_query, bias_value, out_w, bias_out, gain_two, shift_two, up_w, bias_up, down_w, bias_down):
        all_rows = inputs_f.reshape(-1, D)
        normed_one = low(normalize(all_rows, gain_one, shift_one))
        projected = exact_dot(normed_one, qkv_w) + jnp.concatenate([bias_query, jnp.zeros_like(bias_query), bias_value])
        queries = low(low_back(projected[:, :D]))
        keys_all = low(low_back(projected[:, D:2 * D]))
        values_all = low(low_back(projected[:, 2 * D:]))
        context = lax.map(jax.checkpoint(attend), (queries.reshape(seq_count, SEQ_LEN, D), keys_all.reshape(seq_count, SEQ_LEN, D), values_all.reshape(seq_count, SEQ_LEN, D), prefix_flat))
        context = low(low_back(context.reshape(-1, D)))
        attn_out = low_back(exact_dot(context, out_w) + bias_out)
        middle = all_rows + attn_out
        normed_two = low(normalize(middle, gain_two, shift_two))
        pre_act = low_back(exact_dot(normed_two, up_w) + bias_up)
        activated = low(jax.nn.gelu(pre_act, approximate=False))
        branch_out = low_back(exact_dot(activated, down_w) + bias_down)
        return (middle + branch_out).reshape(MB, TOKENS, D)
    params = [p.astype(jnp.float32) for p in (ln1_gain, ln1_bias, qkv_weight, q_bias, v_bias, out_weight, out_bias, ln2_gain, ln2_bias, fc1_weight, fc1_bias, fc2_weight, fc2_bias)]
    result, pullback = jax.vjp(forward, hidden_in.astype(jnp.float32), *params)
    grads = pullback(grad_out.astype(jnp.float32))
    return (result.astype(jnp.bfloat16), grads[0].astype(jnp.bfloat16), grads[1], grads[2], grads[3], grads[4], grads[5], grads[6], grads[7], grads[8], grads[9], grads[10], grads[11], grads[12], grads[13])
```

```python
import math

import jax
import jax.numpy as jnp
import numpy as np
from jax import lax
from jax.experimental import pallas as pl
from jax.experimental.pallas import tpu as pltpu
from jax.sharding import Mesh
from jax.sharding import PartitionSpec as P

HEADS = 16
HEAD_DIM = 128
CORES = 2
EPSILON = 1e-05
MASKED = -1e30
SCALE = 1.0 / math.sqrt(HEAD_DIM)
ALL = ("ch", "co", "sh")
BF = jnp.bfloat16
F32 = jnp.float32


def normalize(values, gain_vec, shift_vec):
    centred = values - jnp.mean(values, axis=-1, keepdims=True)
    spread = jnp.mean(centred * centred, axis=-1, keepdims=True)
    return centred * lax.rsqrt(spread + EPSILON) * gain_vec + shift_vec


def dot(left_side, right_side):
    return jnp.dot(left_side, right_side, preferred_element_type=F32)


def cross_rows(left_side, right_side):
    return lax.dot_general(left_side, right_side, (((0,), (0,)), ((), ())), preferred_element_type=F32)


def times_rows(left_side, right_side):
    return lax.dot_general(left_side, right_side, (((1,), (1,)), ((), ())), preferred_element_type=F32)


def after(value, other):
    return lax.optimization_barrier((value, other))[0]


def place(sources, steps, dest_rows, dest_cols, block, out_shape, out_dtype):
    count = len(steps)
    spans = []
    table = []
    for which in range(len(sources)):
        mine = [i for i, step in enumerate(steps) if step[0] == which]
        first, last = mine[0], mine[-1]
        spans.append((first, last + 1))
        hold = [steps[min(max(i, first), last)] for i in range(count)]
        table.append([step[1] for step in hold])
        table.append([step[2] for step in hold])
    table = jnp.concatenate(
        [jnp.asarray(np.array(table, np.int32)), dest_rows.astype(jnp.int32)[None], dest_cols.astype(jnp.int32)[None]]
    )
    last_row = 2 * len(sources)

    def body(table_ref, *refs):
        step = pl.program_id(0)
        out_ref = refs[-1]
        for which, (first, stop) in enumerate(spans):

            @pl.when((step >= first) & (step < stop))
            def _():
                out_ref[...] = refs[which][...].astype(out_dtype)

    def in_map(which):
        return lambda i, table_ref: (table_ref[2 * which, i], table_ref[2 * which + 1, i])

    return pl.pallas_call(
        body,
        grid_spec=pltpu.PrefetchScalarGridSpec(
            num_scalar_prefetch=1,
            grid=(count,),
            in_specs=[pl.BlockSpec(block, in_map(which)) for which in range(len(sources))],
            out_specs=pl.BlockSpec(block, lambda i, table_ref: (table_ref[last_row, i], table_ref[last_row + 1, i])),
        ),
        out_shape=jax.ShapeDtypeStruct(out_shape, out_dtype),
    )(table, *sources)


def head_parts(scal_ref, q_ref, k_ref, block, rows):
    half = 2 * rows
    core = scal_ref[0]
    prefix = scal_ref[1]
    side = block // 2
    offsets = [pl.multiple_of(core * half, half), pl.multiple_of((1 - core) * half, half)]
    q_off = pl.multiple_of(offsets[side] + (block % 2) * rows, rows)
    queries = q_ref[pl.ds(q_off, rows), :]
    chunks = [(offsets[0], half, 0)]
    if side == 1:
        chunks.append((offsets[1], (block - 1) * rows, half))
    scores = []
    for k_off, count, first in chunks:
        raw = lax.dot_general(
            queries, k_ref[pl.ds(k_off, count), :], (((1,), (1,)), ((), ())), preferred_element_type=F32
        )
        raw = raw * SCALE
        if first + count > block * rows:
            q_pos = block * rows + lax.broadcasted_iota(jnp.int32, raw.shape, 0)
            k_pos = first + lax.broadcasted_iota(jnp.int32, raw.shape, 1)
            raw = jnp.where((k_pos <= q_pos) | (k_pos < prefix), raw, MASKED)
        scores.append(raw)
    top = scores[0].max(axis=-1, keepdims=True)
    for raw in scores[1:]:
        top = jnp.maximum(top, raw.max(axis=-1, keepdims=True))
    terms = [jnp.exp(raw - top) for raw in scores]
    total = terms[0].sum(axis=-1, keepdims=True)
    for term in terms[1:]:
        total = total + term.sum(axis=-1, keepdims=True)
    inverse = 1.0 / total
    return q_off, queries, [(k_off, count, term * inverse) for (k_off, count, _), term in zip(chunks, terms)]


def attend_forward_body(scal_ref, q_ref, k_ref, v_ref, out_ref):
    rows = q_ref.shape[0] // 4
    for block in range(4):
        q_off, _, parts = head_parts(scal_ref, q_ref, k_ref, block, rows)
        total = None
        for k_off, count, soft in parts:
            term = jnp.dot(soft.astype(BF), v_ref[pl.ds(k_off, count), :], preferred_element_type=F32)
            total = term if total is None else total + term
        out_ref[pl.ds(q_off, rows), :] = total.astype(BF)


def attend_backward_body(scal_ref, q_ref, k_ref, v_ref, d_ref, dq_ref, dk_ref, dv_ref, dk_acc, dv_acc):
    rows = q_ref.shape[0] // 4
    dk_acc[...] = jnp.zeros_like(dk_acc)
    dv_acc[...] = jnp.zeros_like(dv_acc)
    for block in range(4):
        q_off, queries, parts = head_parts(scal_ref, q_ref, k_ref, block, rows)
        d_out = d_ref[pl.ds(q_off, rows), :]
        d_softs = []
        row_sum = None
        for k_off, count, soft in parts:
            dv_acc[pl.ds(k_off, count), :] += lax.dot_general(
                soft.astype(BF), d_out, (((0,), (0,)), ((), ())), preferred_element_type=F32
            )
            d_soft = lax.dot_general(
                d_out, v_ref[pl.ds(k_off, count), :], (((1,), (1,)), ((), ())), preferred_element_type=F32
            )
            d_softs.append(d_soft)
            term = jnp.sum(soft * d_soft, axis=-1, keepdims=True)
            row_sum = term if row_sum is None else row_sum + term
        d_queries = None
        for (k_off, count, soft), d_soft in zip(parts, d_softs):
            d_scores = (soft * (d_soft - row_sum) * SCALE).astype(BF)
            term = jnp.dot(d_scores, k_ref[pl.ds(k_off, count), :], preferred_element_type=F32)
            d_queries = term if d_queries is None else d_queries + term
            dk_acc[pl.ds(k_off, count), :] += lax.dot_general(
                d_scores, queries, (((0,), (0,)), ((), ())), preferred_element_type=F32
            )
        dq_ref[pl.ds(q_off, rows), :] = d_queries.astype(BF)
    dk_ref[...] = dk_acc[...].astype(BF)
    dv_ref[...] = dv_acc[...].astype(BF)


def head_specs(rows, heads):
    return [pl.BlockSpec((rows, HEAD_DIM), lambda h, scal_ref, at=at: (0, at * heads + h)) for at in range(3)]


def attend_forward(projected, scalars):
    rows, width = projected.shape
    heads = width // (3 * HEAD_DIM)
    return pl.pallas_call(
        attend_forward_body,
        grid_spec=pltpu.PrefetchScalarGridSpec(
            num_scalar_prefetch=1,
            grid=(heads,),
            in_specs=head_specs(rows, heads),
            out_specs=head_specs(rows, heads)[0],
        ),
        out_shape=jax.ShapeDtypeStruct((rows, width // 3), BF),
    )(scalars, projected, projected, projected)


def attend_backward(projected, d_context, scalars):
    rows, width = projected.shape
    heads = width // (3 * HEAD_DIM)
    one = head_specs(rows, heads)[0]
    return pl.pallas_call(
        attend_backward_body,
        grid_spec=pltpu.PrefetchScalarGridSpec(
            num_scalar_prefetch=1,
            grid=(heads,),
            in_specs=head_specs(rows, heads) + [one],
            out_specs=[one, one, one],
            scratch_shapes=[pltpu.VMEM((rows, HEAD_DIM), F32), pltpu.VMEM((rows, HEAD_DIM), F32)],
        ),
        out_shape=[jax.ShapeDtypeStruct((rows, width // 3), BF)] * 3,
    )(scalars, projected, projected, projected, d_context)


def spread_softmax(queries, keys, q_pos, k_pos, prefix):
    raw = jnp.einsum("qhd,khd->hqk", queries, keys, preferred_element_type=F32) * SCALE
    visible = (k_pos[None, :] <= q_pos[:, None]) | (k_pos[None, :] < prefix)
    raw = jnp.where(visible[None], raw, MASKED)
    terms = jnp.exp(raw - jnp.max(raw, axis=-1, keepdims=True))
    return terms / jnp.sum(terms, axis=-1, keepdims=True)


def spread_backward(queries, keys, values, d_context, soft):
    d_values = jnp.einsum("hqk,qhd->khd", soft.astype(BF), d_context, preferred_element_type=F32)
    d_soft = jnp.einsum("qhd,khd->hqk", d_context, values, preferred_element_type=F32)
    d_scores = (soft * (d_soft - jnp.sum(soft * d_soft, axis=-1, keepdims=True)) * SCALE).astype(BF)
    d_queries = jnp.einsum("hqk,khd->qhd", d_scores, keys, preferred_element_type=F32)
    d_keys = jnp.einsum("hqk,qhd->khd", d_scores, queries, preferred_element_type=F32)
    return d_queries, d_keys, d_values


def local(
    hidden_in,
    prefix,
    ln1_gain,
    ln1_bias,
    qkv_weight,
    q_bias,
    v_bias,
    out_weight,
    out_bias,
    ln2_gain,
    ln2_bias,
    fc1_weight,
    fc1_bias,
    fc2_weight,
    fc2_bias,
    grad_out,
    *,
    chips,
    shards,
):
    micro_count, tok_rows, width = hidden_in.shape
    ff_units = fc1_weight.shape[1]
    piece_rows = width // shards
    rows = micro_count * tok_rows
    parts = shards // (micro_count * CORES)
    ch = lax.axis_index("ch")
    core = lax.axis_index("co")
    shard = lax.axis_index("sh")
    sequence = shard // parts
    micro = sequence // CORES

    def along(value, hop):
        return lax.ppermute(value, "sh", [(i, (i + hop) % shards) for i in range(shards)])

    def plane(value, bit):
        return lax.ppermute(value, "ch", [(i, i ^ bit) for i in range(chips)])

    def swap(value):
        return lax.ppermute(value, "co", [(0, 1), (1, 0)])

    def token_pairs(turn):
        pairs = []
        for c in range(chips):
            for o in range(CORES):
                for s in range(shards):
                    m = (turn + s) % 2
                    slot = s // 2
                    z = (m * CORES + o) * parts + slot // 2
                    pairs.append(((c * CORES + o) * shards + s, (c * CORES + slot % 2) * shards + z))
        return pairs

    def tokens_in(value):
        got = [
            lax.ppermute(lax.dynamic_index_in_dim(value, (turn + shard) % 2, 0, False), ALL, token_pairs(turn))
            for turn in (0, 1)
        ]
        even = micro % 2 == 0
        return jnp.concatenate([jnp.where(even, got[0], got[1]), jnp.where(even, got[1], got[0])])

    def tokens_out(value):
        value = value.reshape(2, tok_rows, width)
        got = [
            lax.ppermute(
                lax.dynamic_index_in_dim(value, (turn + micro) % 2, 0, False),
                ALL,
                [(b, a) for a, b in token_pairs(turn)],
            )
            for turn in (0, 1)
        ]
        even = shard % 2 == 0
        return jnp.stack([jnp.where(even, got[0], got[1]), jnp.where(even, got[1], got[0])])

    def start_pieces(mine, barrier=None):
        cut = mine.shape[1] // chips
        piece = lax.dynamic_slice_in_dim(mine, ch * cut, cut, 1)
        if barrier is not None:
            piece = after(piece, barrier)
        return [along(piece, hop) for hop in range(1, shards)], piece

    def finish_pieces(mine, got, piece, barrier=None):
        height, total = mine.shape
        cut = total // chips
        if chips != 4:
            stacked = jnp.stack([piece] + got)
            everything = lax.all_gather(stacked, "ch")
            everything = jnp.take(everything, (shard - jnp.arange(shards)) % shards, axis=1)
            return everything.transpose(1, 2, 0, 3).reshape(shards * height, total)
        others = jnp.concatenate(got)
        if barrier is not None:
            others = after(others, barrier)
        from_x = plane(others, 1)
        from_y = plane(others, 2)
        tall = (shards - 1, 2, height // 2, cut)
        low_part = plane(from_x.reshape(tall)[:, 0].reshape(-1, cut), 2)
        high_part = plane(from_y.reshape(tall)[:, 1].reshape(-1, cut), 1)
        steps, hops, flips, cols, halves = [], [], [], [], []
        for half in range(2):
            for col in range(chips):
                steps.append((0, half, col))
                hops.append(0), flips.append(-1), cols.append(col), halves.append(half)
        for source, flip in ((1, 0), (2, 1), (3, 2)):
            for hop in range(1, shards):
                for half in range(2):
                    steps.append((source, 2 * (hop - 1) + half, 0))
                    hops.append(hop), flips.append(flip), cols.append(0), halves.append(half)
        for source, half in ((4, 0), (5, 1)):
            for hop in range(1, shards):
                steps.append((source, hop - 1, 0))
                hops.append(hop), flips.append(3), cols.append(0), halves.append(half)
        hops, flips, cols, halves = (np.array(v, np.int32) for v in (hops, flips, cols, halves))
        dest_rows = 2 * ((shard - hops) % shards) + halves
        dest_cols = jnp.where(flips < 0, cols, ch ^ np.maximum(flips, 0))
        return place(
            [mine, others, from_x, from_y, low_part, high_part],
            steps,
            dest_rows,
            dest_cols,
            (height // 2, cut),
            (shards * height, total),
            BF,
        )

    def reduce_grad(left_side, right_side):
        total = right_side.shape[1]
        cut = total // chips
        if chips != 4:
            grads = cross_rows(left_side, right_side).astype(BF)
            grads = grads.reshape(shards, -1, chips, cut).transpose(2, 0, 1, 3)
            mine = lax.psum_scatter(grads, "ch", scatter_dimension=0, tiled=False)
        else:
            middle_at = shards // 2

            def quarter(flip):
                block = lax.dynamic_slice_in_dim(right_side, (ch ^ flip) * cut, cut, 1)
                return cross_rows(left_side, block).astype(BF).reshape(shards, -1, cut)

            far = quarter(3)
            from_y = plane(far[:middle_at], 2)
            from_x = plane(far[middle_at:], 1)
            near_x = quarter(1)
            near_y = quarter(2)
            near_x = jnp.concatenate([near_x[:middle_at] + from_y, near_x[middle_at:]])
            near_y = jnp.concatenate([near_y[:middle_at], near_y[middle_at:] + from_x])
            sum_x = plane(near_x, 1)
            sum_y = plane(near_y, 2)
            mine = (quarter(0).astype(F32) + sum_x.astype(F32) + sum_y.astype(F32)).astype(BF)
        got = [
            along(lax.dynamic_index_in_dim(mine, (shard + hop) % shards, 0, False), hop) for hop in range(1, shards)
        ]
        final = lax.dynamic_index_in_dim(mine, shard, 0, False).astype(F32)
        for member in got:
            final = final + member.astype(F32)
        return final.astype(BF)

    def spread_grad(mine, chunk):
        height, cut = mine.shape
        if chips != 4:
            own = lax.all_gather(mine, "ch", axis=1, tiled=True)
            other = swap(own)
            pair = [jnp.where(core == 0, own, other), jnp.where(core == 0, other, own)]
            if chunk is None:
                return jnp.concatenate(pair).astype(F32)
            wide = jnp.stack([member.reshape(height, -1, chunk) for member in pair], axis=2)
            return wide.reshape(height, -1).astype(F32)
        from_x = plane(mine, 1)
        from_y = plane(mine, 2)
        low_part = plane(from_x[: height // 2], 2)
        high_part = plane(from_y[height // 2 :], 1)
        own = jnp.concatenate([mine, from_x, from_y, low_part, high_part])
        other = swap(own)
        block_cols = cut if chunk is None else min(cut, chunk)
        per = cut // block_cols
        steps, flips, halves, cores, inner = [], [], [], [], []
        for source in range(2):
            for flip in range(4):
                for half in range(2):
                    for at in range(per):
                        steps.append((source, 2 * flip + half, at))
                        flips.append(flip), halves.append(half), cores.append(source), inner.append(at)
        flips, halves, cores, inner = (np.array(v, np.int32) for v in (flips, halves, cores, inner))
        side = core ^ cores
        cols = (ch ^ flips) * per + inner
        if chunk is None:
            dest_rows, dest_cols, shape = 2 * side + halves, cols, (2 * height, chips * cut)
        else:
            step_cols = chunk // block_cols
            dest_rows = jnp.asarray(halves)
            dest_cols = ((cols // step_cols) * 2 + side) * step_cols + cols % step_cols
            shape = (height, 2 * chips * cut)
        return place([own, other], steps, dest_rows, dest_cols, (height // 2, block_cols), shape, F32)

    def take(value, axis):
        return lax.dynamic_index_in_dim(value, core, axis, False)

    qkv_mine = take(qkv_weight.reshape(piece_rows, 3 * shards, CORES, -1), 2).reshape(piece_rows, -1)
    out_mine = take(out_weight.reshape(CORES, piece_rows // CORES, width), 0)
    fc1_mine = take(fc1_weight.reshape(piece_rows, shards, CORES, -1), 2).reshape(piece_rows, -1)
    fc2_mine = take(fc2_weight.reshape(CORES, -1, width), 0)

    vectors = [ln1_gain, ln1_bias, q_bias, v_bias, out_bias, ln2_gain, ln2_bias, fc2_bias, fc1_bias]
    lengths = [v.shape[0] for v in vectors]
    edges = np.cumsum([0] + lengths)
    gathered = lax.all_gather(jnp.concatenate(vectors), "sh").astype(F32)
    vec = [gathered[:, edges[i] : edges[i + 1]] for i in range(len(vectors))]
    gain_one, shift_one, _, _, bias_out, gain_two, shift_two, bias_down, _ = [v.reshape(-1) for v in vec]
    bias_query, bias_value, bias_up = [
        take(vec[i].reshape(shards, CORES, -1), 1).reshape(-1) for i in (2, 3, 8)
    ]

    prefix_pair = [jnp.where(core == 0, a, b) for a, b in ((prefix, swap(prefix)), (swap(prefix), prefix))]
    prefix_len = jnp.concatenate(prefix_pair, axis=1).reshape(-1)[sequence]

    tokens = tokens_in(hidden_in)
    qkv_got, qkv_piece = start_pieces(qkv_mine)
    out_got, out_piece = start_pieces(out_mine, (qkv_got[0], qkv_got[1]))
    fc1_got, fc1_piece = start_pieces(fc1_mine, qkv_got[-1])
    fc2_got, fc2_piece = start_pieces(fc2_mine, fc1_got[-1])
    grads_mine = tokens_in(after(grad_out, fc1_got[-1]))

    hidden_f = tokens.astype(F32)
    normed_own = normalize(hidden_f, gain_one, shift_one).astype(BF)
    normed_one = jnp.concatenate([normed_own, swap(normed_own)])
    qkv_full = finish_pieces(qkv_mine, qkv_got, qkv_piece)
    out_full = finish_pieces(out_mine, out_got, out_piece)
    fc1_full = finish_pieces(fc1_mine, fc1_got, fc1_piece)
    fc2_full = finish_pieces(fc2_mine, fc2_got, fc2_piece)

    half_width = width // CORES
    projected = dot(normed_one, qkv_full) + jnp.concatenate([bias_query, jnp.zeros_like(bias_query), bias_value])
    projected = projected.astype(BF)
    scalars = jnp.stack([core.astype(jnp.int32), prefix_len.astype(jnp.int32)])
    if parts == 1:
        context = attend_forward(projected, scalars)
    else:
        part = shard % parts

        def to_part(value, hop):
            pairs = [(i, i // parts * parts + (i % parts + hop) % parts) for i in range(shards)]
            return lax.ppermute(value, "sh", pairs)

        def positions(which):
            at = jnp.arange(rows)
            return which * CORES * rows + jnp.concatenate([core * rows + at, (1 - core) * rows + at])

        q_four = projected[:, :half_width].reshape(CORES * rows, -1, HEAD_DIM)
        both = projected[:, half_width:]
        held = jnp.concatenate([both] + [to_part(both, hop) for hop in range(1, parts)])
        k_four = held[:, :half_width].reshape(held.shape[0], -1, HEAD_DIM)
        v_four = held[:, half_width:].reshape(held.shape[0], -1, HEAD_DIM)
        k_pos = jnp.concatenate([positions((part - hop) % parts) for hop in range(parts)])
        soft_full = spread_softmax(q_four, k_four, positions(part), k_pos, prefix_len)
        context = jnp.einsum("hqk,khd->qhd", soft_full.astype(BF), v_four, preferred_element_type=F32)
        context = context.reshape(CORES * rows, half_width).astype(BF)

    def own_sum(left_side, product):
        away = swap(product(left_side[rows:]).astype(BF))
        return product(left_side[:rows]) + away.astype(F32)

    middle = hidden_f + (own_sum(context, lambda v: dot(v, out_full)) + bias_out)
    normed_two_own = normalize(middle, gain_two, shift_two).astype(BF)
    normed_two = jnp.concatenate([normed_two_own, swap(normed_two_own)])
    pre_act = dot(normed_two, fc1_full) + bias_up
    below = 0.5 * (1.0 + lax.erf(pre_act * math.sqrt(0.5)))
    density = jnp.exp(-0.5 * pre_act * pre_act) * (1.0 / math.sqrt(2.0 * math.pi))
    activated = (pre_act * below).astype(BF)
    slope = (below + pre_act * density).astype(BF)
    result_own = middle + (own_sum(activated, lambda v: dot(v, fc2_full)) + bias_down)
    result = tokens_out(result_own.astype(BF))

    grad_rows = grads_mine.astype(F32)
    grad_both = jnp.concatenate([grads_mine, swap(grads_mine)])
    down_bias_grad = jnp.sum(grad_rows, axis=0)
    d_pre = (times_rows(grad_both, fc2_full) * slope.astype(F32)).astype(BF)
    fc2_part = reduce_grad(activated, grad_both)
    up_bias_grad = jnp.sum(d_pre, axis=0, dtype=F32)
    fc1_part = reduce_grad(normed_two, d_pre)
    d_normed_two = own_sum(d_pre, lambda v: times_rows(v, fc1_full))
    back_two = jax.vjp(normalize, middle, gain_two, shift_two)[1]
    d_middle, gain_two_grad, shift_two_grad = back_two(d_normed_two)
    d_middle = d_middle + grad_rows
    d_attn_own = d_middle.astype(BF)
    out_bias_grad = jnp.sum(d_attn_own, axis=0, dtype=F32)
    d_attn = jnp.concatenate([d_attn_own, swap(d_attn_own)])
    d_context = times_rows(d_attn, out_full).astype(BF)
    out_part = reduce_grad(context, d_attn)
    if parts == 1:
        d_queries, d_keys, d_values = attend_backward(projected, d_context, scalars)
    else:
        d_four = d_context.reshape(CORES * rows, -1, HEAD_DIM)
        d_queries, d_keys, d_values = spread_backward(q_four, k_four, v_four, d_four, soft_full)
        d_queries = d_queries.reshape(CORES * rows, half_width).astype(BF)
        d_held = jnp.concatenate([d_keys, d_values], axis=1).reshape(parts, CORES * rows, width)
        d_both = d_held[0]
        for hop in range(1, parts):
            d_both = d_both + to_part(d_held[hop].astype(BF), parts - hop).astype(F32)
        d_both = d_both.astype(BF)
        d_keys, d_values = d_both[:, :half_width], d_both[:, half_width:]
    query_bias_grad = jnp.sum(d_queries, axis=0, dtype=F32)
    value_bias_grad = jnp.sum(d_values, axis=0, dtype=F32)
    d_projected = jnp.concatenate([d_queries, d_keys, d_values], axis=1)
    qkv_part = reduce_grad(normed_one, d_projected)
    d_normed_one = own_sum(d_projected, lambda v: times_rows(v, qkv_full))
    back_one = jax.vjp(normalize, hidden_f, gain_one, shift_one)[1]
    d_inputs, gain_one_grad, shift_one_grad = back_one(d_normed_one)
    grad_in = tokens_out((d_middle + d_inputs).astype(BF))

    fc2_weight_grad = spread_grad(fc2_part, None)
    fc1_weight_grad = spread_grad(fc1_part, ff_units // (shards * CORES))
    out_weight_grad = spread_grad(out_part, None)
    qkv_weight_grad = spread_grad(qkv_part, width // (shards * CORES))

    def half_slot(value):
        value = value.reshape(shards, 1, -1)
        mask = lax.broadcasted_iota(jnp.int32, (1, CORES, 1), 1) == core
        return jnp.where(mask, value, 0.0).reshape(shards, -1)

    def full_slot(value):
        return value.reshape(shards, -1)

    packed = jnp.concatenate(
        [
            full_slot(gain_one_grad),
            full_slot(shift_one_grad),
            half_slot(query_bias_grad),
            half_slot(value_bias_grad),
            full_slot(out_bias_grad),
            full_slot(gain_two_grad),
            full_slot(shift_two_grad),
            full_slot(down_bias_grad),
            half_slot(up_bias_grad),
        ],
        axis=1,
    )
    summed = lax.dynamic_index_in_dim(lax.psum(packed, ALL), shard, 0, False)
    sums = [summed[edges[i] : edges[i + 1]] for i in range(len(vectors))]
    return (
        result,
        grad_in,
        sums[0],
        sums[1],
        qkv_weight_grad,
        sums[2],
        sums[3],
        out_weight_grad,
        sums[4],
        sums[5],
        sums[6],
        fc1_weight_grad,
        sums[8],
        fc2_weight_grad,
        sums[7],
    )


def solution(mesh):
    shards = mesh.shape["shard"]
    chips = mesh.shape["rep"] // CORES
    inner = Mesh(mesh.devices.reshape(chips, CORES, shards), ALL)
    token_spec = P(None, ALL, None)
    args = [token_spec, P(None, ("ch", "co"))]
    for dims in (1, 1, 2, 1, 1, 2, 1, 1, 1, 2, 1, 2, 1):
        args.append(P("sh", None) if dims == 2 else P("sh"))
    args.append(token_spec)
    outs = [token_spec, token_spec]
    for dims in (1, 1, 2, 1, 1, 2, 1, 1, 1, 2, 1, 2, 1):
        outs.append(P("sh", None) if dims == 2 else P("sh"))

    def run(*values):
        return local(*values, chips=chips, shards=shards)

    return jax.shard_map(run, mesh=inner, in_specs=tuple(args), out_specs=tuple(outs), check_vma=False)
```

```python
import math

import jax
import jax.numpy as jnp
import numpy as np
from jax import lax
from jax.experimental import pallas as pl
from jax.experimental.pallas import tpu as pltpu
from jax.sharding import Mesh
from jax.sharding import PartitionSpec as P

HEADS = 16
HEAD_DIM = 128
CORES = 2
EPSILON = 1e-05
MASKED = -1e30
SCALE = 1.0 / math.sqrt(HEAD_DIM)
ALL = ("ch", "co", "sh")
BF = jnp.bfloat16
F32 = jnp.float32


def normalize(values, gain_vec, shift_vec):
    centred = values - jnp.mean(values, axis=-1, keepdims=True)
    spread = jnp.mean(centred * centred, axis=-1, keepdims=True)
    return centred * lax.rsqrt(spread + EPSILON) * gain_vec + shift_vec


def dot(left_side, right_side):
    return jnp.dot(left_side, right_side, preferred_element_type=F32)


def cross_rows(left_side, right_side):
    return lax.dot_general(left_side, right_side, (((0,), (0,)), ((), ())), preferred_element_type=F32)


def times_rows(left_side, right_side):
    return lax.dot_general(left_side, right_side, (((1,), (1,)), ((), ())), preferred_element_type=F32)


def after(value, other):
    return lax.optimization_barrier((value, other))[0]


def place(sources, steps, dest_rows, dest_cols, block, out_shape, out_dtype, offset=None):
    count = len(steps)
    spans = []
    table = []
    for which in range(len(sources)):
        mine = [i for i, step in enumerate(steps) if step[0] == which]
        first, last = mine[0], mine[-1]
        spans.append((first, last + 1))
        hold = [steps[min(max(i, first), last)] for i in range(count)]
        table.append([step[1] for step in hold])
        table.append([step[2] for step in hold])
    fixed = jnp.asarray(np.array(table, np.int32))
    if offset is not None:
        mask = lax.broadcasted_iota(jnp.int32, (fixed.shape[0], 1), 0)
        fixed = fixed + jnp.where(mask == 0, offset[0], jnp.where(mask == 1, offset[1], 0))
    table = jnp.concatenate(
        [fixed, dest_rows.astype(jnp.int32)[None], dest_cols.astype(jnp.int32)[None]]
    )
    last_row = 2 * len(sources)

    def body(table_ref, *refs):
        step = pl.program_id(0)
        out_ref = refs[-1]
        for which, (first, stop) in enumerate(spans):

            @pl.when((step >= first) & (step < stop))
            def _():
                out_ref[...] = refs[which][...].astype(out_dtype)

    def in_map(which):
        return lambda i, table_ref: (table_ref[2 * which, i], table_ref[2 * which + 1, i])

    return pl.pallas_call(
        body,
        grid_spec=pltpu.PrefetchScalarGridSpec(
            num_scalar_prefetch=1,
            grid=(count,),
            in_specs=[pl.BlockSpec(block, in_map(which)) for which in range(len(sources))],
            out_specs=pl.BlockSpec(block, lambda i, table_ref: (table_ref[last_row, i], table_ref[last_row + 1, i])),
        ),
        out_shape=jax.ShapeDtypeStruct(out_shape, out_dtype),
    )(table, *sources)


def head_parts(scal_ref, q_ref, k_ref, block, rows):
    half = 2 * rows
    core = scal_ref[0]
    prefix = scal_ref[1]
    side = block // 2
    offsets = [pl.multiple_of(core * half, half), pl.multiple_of((1 - core) * half, half)]
    q_off = pl.multiple_of(offsets[side] + (block % 2) * rows, rows)
    queries = q_ref[pl.ds(q_off, rows), :]
    chunks = [(offsets[0], half, 0)]
    if side == 1:
        chunks.append((offsets[1], (block - 1) * rows, half))
    scores = []
    for k_off, count, first in chunks:
        raw = lax.dot_general(
            queries, k_ref[pl.ds(k_off, count), :], (((1,), (1,)), ((), ())), preferred_element_type=F32
        )
        raw = raw * SCALE
        if first + count > block * rows:
            q_pos = block * rows + lax.broadcasted_iota(jnp.int32, raw.shape, 0)
            k_pos = first + lax.broadcasted_iota(jnp.int32, raw.shape, 1)
            raw = jnp.where((k_pos <= q_pos) | (k_pos < prefix), raw, MASKED)
        scores.append(raw)
    top = scores[0].max(axis=-1, keepdims=True)
    for raw in scores[1:]:
        top = jnp.maximum(top, raw.max(axis=-1, keepdims=True))
    terms = [jnp.exp(raw - top) for raw in scores]
    total = terms[0].sum(axis=-1, keepdims=True)
    for term in terms[1:]:
        total = total + term.sum(axis=-1, keepdims=True)
    inverse = 1.0 / total
    return q_off, queries, [(k_off, count, term * inverse) for (k_off, count, _), term in zip(chunks, terms)]


def attend_forward_body(scal_ref, q_ref, k_ref, v_ref, out_ref):
    rows = q_ref.shape[0] // 4
    for block in range(4):
        q_off, _, parts = head_parts(scal_ref, q_ref, k_ref, block, rows)
        total = None
        for k_off, count, soft in parts:
            term = jnp.dot(soft.astype(BF), v_ref[pl.ds(k_off, count), :], preferred_element_type=F32)
            total = term if total is None else total + term
        out_ref[pl.ds(q_off, rows), :] = total.astype(BF)


def attend_backward_body(scal_ref, q_ref, k_ref, v_ref, d_ref, dq_ref, dk_ref, dv_ref, dk_acc, dv_acc):
    rows = q_ref.shape[0] // 4
    dk_acc[...] = jnp.zeros_like(dk_acc)
    dv_acc[...] = jnp.zeros_like(dv_acc)
    for block in range(4):
        q_off, queries, parts = head_parts(scal_ref, q_ref, k_ref, block, rows)
        d_out = d_ref[pl.ds(q_off, rows), :]
        d_softs = []
        row_sum = None
        for k_off, count, soft in parts:
            dv_acc[pl.ds(k_off, count), :] += lax.dot_general(
                soft.astype(BF), d_out, (((0,), (0,)), ((), ())), preferred_element_type=F32
            )
            d_soft = lax.dot_general(
                d_out, v_ref[pl.ds(k_off, count), :], (((1,), (1,)), ((), ())), preferred_element_type=F32
            )
            d_softs.append(d_soft)
            term = jnp.sum(soft * d_soft, axis=-1, keepdims=True)
            row_sum = term if row_sum is None else row_sum + term
        d_queries = None
        for (k_off, count, soft), d_soft in zip(parts, d_softs):
            d_scores = (soft * (d_soft - row_sum) * SCALE).astype(BF)
            term = jnp.dot(d_scores, k_ref[pl.ds(k_off, count), :], preferred_element_type=F32)
            d_queries = term if d_queries is None else d_queries + term
            dk_acc[pl.ds(k_off, count), :] += lax.dot_general(
                d_scores, queries, (((0,), (0,)), ((), ())), preferred_element_type=F32
            )
        dq_ref[pl.ds(q_off, rows), :] = d_queries.astype(BF)
    dk_ref[...] = dk_acc[...].astype(BF)
    dv_ref[...] = dv_acc[...].astype(BF)


def head_specs(rows, heads):
    return [pl.BlockSpec((rows, HEAD_DIM), lambda h, scal_ref, at=at: (0, at * heads + h)) for at in range(3)]


def attend_forward(projected, scalars):
    rows, width = projected.shape
    heads = width // (3 * HEAD_DIM)
    return pl.pallas_call(
        attend_forward_body,
        grid_spec=pltpu.PrefetchScalarGridSpec(
            num_scalar_prefetch=1,
            grid=(heads,),
            in_specs=head_specs(rows, heads),
            out_specs=head_specs(rows, heads)[0],
        ),
        out_shape=jax.ShapeDtypeStruct((rows, width // 3), BF),
    )(scalars, projected, projected, projected)


def attend_backward(projected, d_context, scalars):
    rows, width = projected.shape
    heads = width // (3 * HEAD_DIM)
    one = head_specs(rows, heads)[0]
    return pl.pallas_call(
        attend_backward_body,
        grid_spec=pltpu.PrefetchScalarGridSpec(
            num_scalar_prefetch=1,
            grid=(heads,),
            in_specs=head_specs(rows, heads) + [one],
            out_specs=[one, one, one],
            scratch_shapes=[pltpu.VMEM((rows, HEAD_DIM), F32), pltpu.VMEM((rows, HEAD_DIM), F32)],
        ),
        out_shape=[jax.ShapeDtypeStruct((rows, width // 3), BF)] * 3,
    )(scalars, projected, projected, projected, d_context)


def spread_softmax(queries, keys, q_pos, k_pos, prefix):
    raw = jnp.einsum("qhd,khd->hqk", queries, keys, preferred_element_type=F32) * SCALE
    visible = (k_pos[None, :] <= q_pos[:, None]) | (k_pos[None, :] < prefix)
    raw = jnp.where(visible[None], raw, MASKED)
    terms = jnp.exp(raw - jnp.max(raw, axis=-1, keepdims=True))
    return terms / jnp.sum(terms, axis=-1, keepdims=True)


def spread_backward(queries, keys, values, d_context, soft):
    d_values = jnp.einsum("hqk,qhd->khd", soft.astype(BF), d_context, preferred_element_type=F32)
    d_soft = jnp.einsum("qhd,khd->hqk", d_context, values, preferred_element_type=F32)
    d_scores = (soft * (d_soft - jnp.sum(soft * d_soft, axis=-1, keepdims=True)) * SCALE).astype(BF)
    d_queries = jnp.einsum("hqk,khd->qhd", d_scores, keys, preferred_element_type=F32)
    d_keys = jnp.einsum("hqk,qhd->khd", d_scores, queries, preferred_element_type=F32)
    return d_queries, d_keys, d_values


def local(
    hidden_in,
    prefix,
    ln1_gain,
    ln1_bias,
    qkv_weight,
    q_bias,
    v_bias,
    out_weight,
    out_bias,
    ln2_gain,
    ln2_bias,
    fc1_weight,
    fc1_bias,
    fc2_weight,
    fc2_bias,
    grad_out,
    *,
    chips,
    shards,
):
    micro_count, tok_rows, width = hidden_in.shape
    ff_units = fc1_weight.shape[1]
    piece_rows = width // shards
    rows = micro_count * tok_rows
    parts = shards // (micro_count * CORES)
    ch = lax.axis_index("ch")
    core = lax.axis_index("co")
    shard = lax.axis_index("sh")
    sequence = shard // parts
    micro = sequence // CORES

    def along(value, hop):
        return lax.ppermute(value, "sh", [(i, (i + hop) % shards) for i in range(shards)])

    def plane(value, bit):
        return lax.ppermute(value, "ch", [(i, i ^ bit) for i in range(chips)])

    def swap(value):
        return lax.ppermute(value, "co", [(0, 1), (1, 0)])

    def token_pairs(turn):
        pairs = []
        for c in range(chips):
            for o in range(CORES):
                for s in range(shards):
                    m = (turn + s) % 2
                    slot = s // 2
                    z = (m * CORES + o) * parts + slot // 2
                    pairs.append(((c * CORES + o) * shards + s, (c * CORES + slot % 2) * shards + z))
        return pairs

    def tokens_in(value):
        got = [
            lax.ppermute(lax.dynamic_index_in_dim(value, (turn + shard) % 2, 0, False), ALL, token_pairs(turn))
            for turn in (0, 1)
        ]
        even = micro % 2 == 0
        return jnp.concatenate([jnp.where(even, got[0], got[1]), jnp.where(even, got[1], got[0])])

    def tokens_out(value):
        value = value.reshape(2, tok_rows, width)
        got = [
            lax.ppermute(
                lax.dynamic_index_in_dim(value, (turn + micro) % 2, 0, False),
                ALL,
                [(b, a) for a, b in token_pairs(turn)],
            )
            for turn in (0, 1)
        ]
        even = shard % 2 == 0
        return jnp.stack([jnp.where(even, got[0], got[1]), jnp.where(even, got[1], got[0])])

    def gather_shards(piece):
        held = lax.all_gather(piece, "sh")
        return [lax.dynamic_index_in_dim(held, (shard - hop) % shards, 0, False) for hop in range(1, shards)]

    def spread_others(others):
        from_x = plane(others, 1)
        from_y = plane(others, 2)
        tall = (shards - 1, 2, others.shape[0] // (2 * (shards - 1)), others.shape[1])
        low_cut = from_x.reshape(tall)[:, 0].reshape(-1, tall[3])
        high_cut = from_y.reshape(tall)[:, 1].reshape(-1, tall[3])
        return from_x, from_y, low_cut, high_cut

    def whole_weight(source, offset, col_step, height, others, from_x, from_y, low_part, high_part):
        cut = others.shape[1]
        steps, hops, flips, cols, halves = [], [], [], [], []
        for half in range(2):
            for col in range(chips):
                steps.append((0, half, col * col_step))
                hops.append(0), flips.append(-1), cols.append(col), halves.append(half)
        for which, flip in ((1, 0), (2, 1), (3, 2)):
            for hop in range(1, shards):
                for half in range(2):
                    steps.append((which, 2 * (hop - 1) + half, 0))
                    hops.append(hop), flips.append(flip), cols.append(0), halves.append(half)
        for which, half in ((4, 0), (5, 1)):
            for hop in range(1, shards):
                steps.append((which, hop - 1, 0))
                hops.append(hop), flips.append(3), cols.append(0), halves.append(half)
        hops, flips, cols, halves = (np.array(v, np.int32) for v in (hops, flips, cols, halves))
        return place(
            [source, others, from_x, from_y, low_part, high_part],
            steps,
            2 * ((shard - hops) % shards) + halves,
            jnp.where(flips < 0, cols, ch ^ np.maximum(flips, 0)),
            (height // 2, cut),
            (shards * height, chips * cut),
            BF,
            offset,
        )

    def whole_weight_any(piece):
        everything = lax.all_gather(lax.all_gather(piece, "sh"), "ch")
        return everything.transpose(1, 2, 0, 3).reshape(-1, chips * piece.shape[1])

    def grad_block(left_side, right_side, flip, half=None):
        cut = right_side.shape[1] // chips
        block = lax.dynamic_slice_in_dim(right_side, (ch ^ flip) * cut, cut, 1)
        if half is not None:
            width_half = left_side.shape[1] // 2
            left_side = left_side[:, half * width_half : (half + 1) * width_half]
        return cross_rows(left_side, block).astype(BF)

    def sum_shards(mine):
        return lax.psum_scatter(mine, "sh", scatter_dimension=0, tiled=True)

    def sum_any(left_side, right_side):
        cut = right_side.shape[1] // chips
        grads = cross_rows(left_side, right_side).astype(BF).reshape(-1, chips, cut).transpose(1, 0, 2)
        return sum_shards(lax.psum_scatter(grads, "ch", scatter_dimension=0))

    def spread_any(mine, chunk):
        height = mine.shape[0]
        own = lax.all_gather(mine, "ch", axis=1, tiled=True)
        other = swap(own)
        pair = [jnp.where(core == 0, own, other), jnp.where(core == 0, other, own)]
        if chunk is None:
            return jnp.concatenate(pair).astype(F32)
        wide = jnp.stack([member.reshape(height, -1, chunk) for member in pair], axis=2)
        return wide.reshape(height, -1).astype(F32)

    def spread_first(mine):
        from_x = plane(mine, 1)
        from_y = plane(mine, 2)
        return mine, from_x, from_y

    def spread_second(mine, from_x, from_y):
        middle_row = mine.shape[0] // 2
        low_part = plane(from_x[:middle_row], 2)
        high_part = plane(from_y[middle_row:], 1)
        own = jnp.concatenate([mine, from_x, from_y, low_part, high_part])
        return own, swap(own)

    def spread_last(own, other, chunk):
        height, cut = own.shape[0] // 4, own.shape[1]
        block_cols = cut if chunk is None else chunk
        per = cut // block_cols
        steps, flips, cores, inner = [], [], [], []
        for source in range(2):
            for flip in range(4):
                for at in range(per):
                    steps.append((source, flip, at))
                    flips.append(flip), cores.append(source), inner.append(at)
        flips, cores, inner = (np.array(v, np.int32) for v in (flips, cores, inner))
        side = core ^ cores
        cols = (ch ^ flips) * per + inner
        if chunk is None:
            dest_rows, dest_cols, shape = side, cols, (2 * height, chips * cut)
        else:
            dest_rows, dest_cols, shape = 0 * side, cols * 2 + side, (height, 2 * chips * cut)
        return place([own, other], steps, dest_rows, dest_cols, (height, block_cols), shape, F32)

    def take(value, axis):
        return lax.dynamic_index_in_dim(value, core, axis, False)

    qkv_chunk = width // (shards * CORES)
    fc1_chunk = ff_units // (shards * CORES)

    def col_chunks(value, chunk, first, count):
        cuts = [lax.dynamic_slice_in_dim(value, ((first + i) * CORES + core) * chunk, chunk, 1) for i in range(count)]
        return cuts[0] if count == 1 else jnp.concatenate(cuts, axis=1)

    def col_piece(value, chunk):
        per = value.shape[1] // (CORES * chips * chunk)
        return col_chunks(value, chunk, ch * per, per)

    def row_piece(value):
        height, cut = value.shape[0] // CORES, value.shape[1] // chips
        return lax.dynamic_slice(value, (core * height, ch * cut), (height, cut))

    qkv_piece = col_piece(qkv_weight, qkv_chunk)
    fc1_piece = col_piece(fc1_weight, fc1_chunk)
    out_piece = row_piece(out_weight)
    fc2_piece = row_piece(fc2_weight)

    vectors = [ln1_gain, ln1_bias, q_bias, v_bias, out_bias, ln2_gain, ln2_bias, fc2_bias, fc1_bias]
    lengths = [v.shape[0] for v in vectors]
    edges = np.cumsum([0] + lengths)
    square = chips == 4
    small = jnp.concatenate(vectors)
    if square:
        qkv_others = jnp.concatenate(gather_shards(qkv_piece))
        small = after(small, qkv_others)
    ring = [small] + [along(small, hop) for hop in range(shards - 1, 0, -1)]
    gathered = lax.dynamic_slice_in_dim(jnp.stack(ring + ring), (shards - shard) % shards, shards, 0)
    vec = [gathered[:, edges[i] : edges[i + 1]].astype(F32) for i in range(len(vectors))]
    gain_one, shift_one, _, _, bias_out, gain_two, shift_two, bias_down, _ = [v.reshape(-1) for v in vec]
    bias_query, bias_value, bias_up = [
        take(vec[i].reshape(shards, CORES, -1), 1).reshape(-1) for i in (2, 3, 8)
    ]

    prefix_pair = [jnp.where(core == 0, a, b) for a, b in ((prefix, swap(prefix)), (swap(prefix), prefix))]
    prefix_len = jnp.concatenate(prefix_pair, axis=1).reshape(-1)[sequence]

    tokens = lax.optimization_barrier(tokens_in(after(hidden_in, small)))
    if square:
        out_others = jnp.concatenate(gather_shards(out_piece))
        fc1_others = jnp.concatenate(gather_shards(fc1_piece))
        fc2_others = jnp.concatenate(gather_shards(fc2_piece))
        qkv_x, qkv_y, qkv_low, qkv_high = spread_others(qkv_others)
        out_others = after(out_others, (qkv_x, qkv_y))
        out_x, out_y, out_low, out_high = spread_others(out_others)
        fc1_others = after(fc1_others, (qkv_low, qkv_high, out_others))
        fc1_x, fc1_y, fc1_low, fc1_high = spread_others(fc1_others)
        fc2_others = after(fc2_others, (fc1_low, fc1_high))
        fc2_x, fc2_y, fc2_low, fc2_high = spread_others(fc2_others)

    hidden_f = tokens.astype(F32)
    normed_own = normalize(hidden_f, gain_one, shift_one).astype(BF)
    normed_one = jnp.concatenate([normed_own, swap(normed_own)])
    none = jnp.zeros((), jnp.int32)
    if square:
        normed_one = after(normed_one, fc1_others)
        qkv_mine = col_chunks(qkv_weight, qkv_chunk, 0, 3 * shards)
        qkv_full = whole_weight(
            qkv_mine, None, 1, piece_rows, qkv_others, qkv_x, qkv_y, plane(qkv_low, 2), plane(qkv_high, 1)
        )
        out_full = whole_weight(
            out_weight, (2 * core, none), 1, piece_rows // 2, out_others, out_x, out_y, plane(out_low, 2), plane(out_high, 1)
        )
        fc1_full = whole_weight(
            fc1_weight, (none, core), 2, piece_rows, fc1_others, fc1_x, fc1_y, plane(fc1_low, 2), plane(fc1_high, 1)
        )
        fc2_full = whole_weight(
            fc2_weight,
            (2 * core, none),
            1,
            fc2_weight.shape[0] // 2,
            fc2_others,
            fc2_x,
            fc2_y,
            plane(fc2_low, 2),
            plane(fc2_high, 1),
        )
        grads_mine = tokens_in(after(grad_out, fc1_others))
    else:
        qkv_full, out_full, fc1_full, fc2_full = [
            whole_weight_any(piece) for piece in (qkv_piece, out_piece, fc1_piece, fc2_piece)
        ]
        grads_mine = tokens_in(grad_out)
    grads_mine = lax.optimization_barrier(grads_mine)

    half_width = width // CORES
    projected = dot(normed_one, qkv_full) + jnp.concatenate([bias_query, jnp.zeros_like(bias_query), bias_value])
    projected = projected.astype(BF)
    scalars = jnp.stack([core.astype(jnp.int32), prefix_len.astype(jnp.int32)])
    if parts == 1:
        context = attend_forward(projected, scalars)
    else:
        part = shard % parts

        def to_part(value, hop):
            pairs = [(i, i // parts * parts + (i % parts + hop) % parts) for i in range(shards)]
            return lax.ppermute(value, "sh", pairs)

        def positions(which):
            at = jnp.arange(rows)
            return which * CORES * rows + jnp.concatenate([core * rows + at, (1 - core) * rows + at])

        q_four = projected[:, :half_width].reshape(CORES * rows, -1, HEAD_DIM)
        both = projected[:, half_width:]
        held = jnp.concatenate([both] + [to_part(both, hop) for hop in range(1, parts)])
        k_four = held[:, :half_width].reshape(held.shape[0], -1, HEAD_DIM)
        v_four = held[:, half_width:].reshape(held.shape[0], -1, HEAD_DIM)
        k_pos = jnp.concatenate([positions((part - hop) % parts) for hop in range(parts)])
        soft_full = spread_softmax(q_four, k_four, positions(part), k_pos, prefix_len)
        context = jnp.einsum("hqk,khd->qhd", soft_full.astype(BF), v_four, preferred_element_type=F32)
        context = context.reshape(CORES * rows, half_width).astype(BF)

    if square:
        context = after(context, (fc1_low, fc1_high))

    def own_sum(left_side, product):
        away = swap(product(left_side[rows:]).astype(BF))
        return product(left_side[:rows]) + away.astype(F32)

    middle = hidden_f + (own_sum(context, lambda v: dot(v, out_full)) + bias_out)
    normed_two_own = normalize(middle, gain_two, shift_two).astype(BF)
    normed_two = jnp.concatenate([normed_two_own, swap(normed_two_own)])
    pre_act = dot(normed_two, fc1_full) + bias_up
    below = 0.5 * (1.0 + lax.erf(pre_act * math.sqrt(0.5)))
    density = jnp.exp(-0.5 * pre_act * pre_act) * (1.0 / math.sqrt(2.0 * math.pi))
    activated = (pre_act * below).astype(BF)
    slope = (below + pre_act * density).astype(BF)

    grad_rows = grads_mine.astype(F32)
    grad_both = jnp.concatenate([grads_mine, swap(grads_mine)])
    down_bias_grad = jnp.sum(grad_rows, axis=0)

    class Reduction:
        def __init__(self, left_side, right_side):
            self.sides = (left_side, right_side)
            far_low = grad_block(left_side, right_side, 3, 0)
            far_high = grad_block(left_side, right_side, 3, 1)
            self.far = (plane(far_low, 2), plane(far_high, 1))
            right_side = after(right_side, (far_low, far_high))
            self.x_high = plane(grad_block(left_side, right_side, 1, 1), 1)
            self.y_low = plane(grad_block(left_side, right_side, 2, 0), 2)
            self.near = [grad_block(left_side, right_side, 1, 0), grad_block(left_side, right_side, 2, 1)]

        def second(self, barrier=None):
            far = self.far if barrier is None else tuple(after(value, barrier) for value in self.far)
            self.sent = [self.near[0] + far[0], self.near[1] + far[1]]
            self.x_low = plane(self.sent[0], 1)
            self.y_high = plane(self.sent[1], 2)

        def third(self, barrier=None):
            x_low, y_high = self.x_low, self.y_high
            if barrier is not None:
                x_low, y_high = after(x_low, barrier), after(y_high, barrier)
            low_part = grad_block(*self.sides, 0, 0).astype(F32) + x_low.astype(F32) + self.y_low.astype(F32)
            high_part = grad_block(*self.sides, 0, 1).astype(F32) + self.x_high.astype(F32) + y_high.astype(F32)
            self.mine = jnp.concatenate([low_part.astype(BF), high_part.astype(BF)])
            return sum_shards(self.mine)

    if square:
        fc2_red = Reduction(activated, after(grad_both, (fc2_low, fc2_high)))
    d_pre = (times_rows(grad_both, fc2_full) * slope.astype(F32)).astype(BF)
    up_bias_grad = jnp.sum(d_pre, axis=0, dtype=F32)
    if square:
        fc1_red = Reduction(normed_two, d_pre)
        fc2_red.second()
        activated = after(activated, fc1_red.near)
    result_own = middle + (own_sum(activated, lambda v: dot(v, fc2_full)) + bias_down)
    result = tokens_out(result_own.astype(BF))
    d_normed_two = own_sum(d_pre, lambda v: times_rows(v, fc1_full))
    back_two = jax.vjp(normalize, middle, gain_two, shift_two)[1]
    d_middle, gain_two_grad, shift_two_grad = back_two(d_normed_two)
    d_middle = d_middle + grad_rows
    d_attn_own = d_middle.astype(BF)
    out_bias_grad = jnp.sum(d_attn_own, axis=0, dtype=F32)
    d_attn = jnp.concatenate([d_attn_own, swap(d_attn_own)])
    if square:
        fc1_red.second(fc2_red.sent)
        out_red = Reduction(context, d_attn)
    d_context = times_rows(d_attn, out_full).astype(BF)
    if square:
        d_context = after(d_context, fc1_red.sent)
    if parts == 1:
        d_queries, d_keys, d_values = attend_backward(projected, d_context, scalars)
    else:
        d_four = d_context.reshape(CORES * rows, -1, HEAD_DIM)
        d_queries, d_keys, d_values = spread_backward(q_four, k_four, v_four, d_four, soft_full)
        d_queries = d_queries.reshape(CORES * rows, half_width).astype(BF)
        d_held = jnp.concatenate([d_keys, d_values], axis=1).reshape(parts, CORES * rows, width)
        d_both = d_held[0]
        for hop in range(1, parts):
            d_both = d_both + to_part(d_held[hop].astype(BF), parts - hop).astype(F32)
        d_both = d_both.astype(BF)
        d_keys, d_values = d_both[:, :half_width], d_both[:, half_width:]
    d_projected = jnp.concatenate([d_queries, d_keys, d_values], axis=1)
    if square:
        fc2_part = fc2_red.third()
        d_projected = after(d_projected, (fc2_red.mine, result))
        qkv_red = Reduction(normed_one, d_projected)
        out_red.second()
        fc1_part = fc1_red.third(qkv_red.near)
        qkv_red.second((fc1_red.mine, out_red.sent))
        d_projected = after(d_projected, qkv_red.sent)
    query_bias_grad = jnp.sum(d_projected[:, :half_width], axis=0, dtype=F32)
    value_bias_grad = jnp.sum(d_projected[:, width:], axis=0, dtype=F32)
    d_normed_one = own_sum(d_projected, lambda v: times_rows(v, qkv_full))
    back_one = jax.vjp(normalize, hidden_f, gain_one, shift_one)[1]
    d_inputs, gain_one_grad, shift_one_grad = back_one(d_normed_one)
    grad_in_own = (d_middle + d_inputs).astype(BF)

    def half_slot(value):
        value = value.reshape(shards, 1, -1)
        mask = lax.broadcasted_iota(jnp.int32, (1, CORES, 1), 1) == core
        return jnp.where(mask, value, 0.0).reshape(shards, -1)

    def full_slot(value):
        return value.reshape(shards, -1)

    packed = jnp.concatenate(
        [
            full_slot(gain_one_grad),
            full_slot(shift_one_grad),
            half_slot(query_bias_grad),
            half_slot(value_bias_grad),
            full_slot(out_bias_grad),
            full_slot(gain_two_grad),
            full_slot(shift_two_grad),
            full_slot(down_bias_grad),
            half_slot(up_bias_grad),
        ],
        axis=1,
    )
    grad_in = tokens_out(grad_in_own)

    def sum_plane(values, bits):
        for bit in bits:
            values = values + plane(values, 1 << bit)
        return values

    def sum_line(values):
        total = lax.dynamic_index_in_dim(values, shard, 0, False)
        for hop in range(1, shards):
            total = total + along(lax.dynamic_index_in_dim(values, (shard + hop) % shards, 0, False), hop)
        return total

    packed = packed + swap(packed)
    if square:
        out_part = out_red.third((qkv_red.sent, qkv_red.x_high, qkv_red.y_low))
        fc2_first = spread_first(after(fc2_part, (qkv_red.sent, out_red.mine)))
        qkv_part = qkv_red.third(grad_in_own)
        packed = sum_plane(packed, [0])
        fc1_first = spread_first(after(fc1_part, (fc2_first[1:], qkv_red.mine, packed, grad_in)))
        fc2_pair = spread_second(*fc2_first)
        packed = sum_plane(packed, [1])
        out_first = spread_first(after(out_part, (fc1_first[1:], fc2_pair[0], packed)))
        summed = sum_line(after(packed, grad_in))
        fc1_pair = spread_second(*fc1_first)
        fc2_weight_grad = spread_last(*fc2_pair, None)
        fc1_weight_grad = spread_last(*fc1_pair, fc1_chunk)
        out_pair = spread_second(*out_first)
        qkv_first = spread_first(after(qkv_part, (out_pair[0], fc1_pair[0], fc2_weight_grad, summed)))
        out_weight_grad = spread_last(*out_pair, None)
        qkv_own, qkv_other = spread_second(*after(qkv_first, (fc1_weight_grad, out_pair[1])))
        qkv_weight_grad = spread_last(qkv_own, after(qkv_other, out_weight_grad), qkv_chunk)
    else:
        summed = sum_line(sum_plane(packed, range(chips.bit_length() - 1)))
        fc2_weight_grad = spread_any(sum_any(activated, grad_both), None)
        fc1_weight_grad = spread_any(sum_any(normed_two, d_pre), fc1_chunk)
        out_weight_grad = spread_any(sum_any(context, d_attn), None)
        qkv_weight_grad = spread_any(sum_any(normed_one, d_projected), qkv_chunk)
    sums = [summed[edges[i] : edges[i + 1]] for i in range(len(vectors))]
    return (
        result,
        grad_in,
        sums[0],
        sums[1],
        qkv_weight_grad,
        sums[2],
        sums[3],
        out_weight_grad,
        sums[4],
        sums[5],
        sums[6],
        fc1_weight_grad,
        sums[8],
        fc2_weight_grad,
        sums[7],
    )


def solution(mesh):
    shards = mesh.shape["shard"]
    chips = mesh.shape["rep"] // CORES
    inner = Mesh(mesh.devices.reshape(chips, CORES, shards), ALL)
    token_spec = P(None, ALL, None)
    args = [token_spec, P(None, ("ch", "co"))]
    for dims in (1, 1, 2, 1, 1, 2, 1, 1, 1, 2, 1, 2, 1):
        args.append(P("sh", None) if dims == 2 else P("sh"))
    args.append(token_spec)
    outs = [token_spec, token_spec]
    for dims in (1, 1, 2, 1, 1, 2, 1, 1, 1, 2, 1, 2, 1):
        outs.append(P("sh", None) if dims == 2 else P("sh"))

    def run(*values):
        return local(*values, chips=chips, shards=shards)

    return jax.shard_map(run, mesh=inner, in_specs=tuple(args), out_specs=tuple(outs), check_vma=False)
```

```python
import math

import jax
import jax.numpy as jnp
import numpy as np
from jax import lax
from jax.experimental import pallas as pl
from jax.experimental.pallas import tpu as pltpu
from jax.sharding import Mesh
from jax.sharding import PartitionSpec as P

HEADS = 16
HEAD_DIM = 128
CORES = 2
EPSILON = 1e-05
MASKED = -1e30
SCALE = 1.0 / math.sqrt(HEAD_DIM)
ALL = ("ch", "co", "sh")
BF = jnp.bfloat16
F32 = jnp.float32


def normalize(values, gain_vec, shift_vec):
    centred = values - jnp.mean(values, axis=-1, keepdims=True)
    spread = jnp.mean(centred * centred, axis=-1, keepdims=True)
    return centred * lax.rsqrt(spread + EPSILON) * gain_vec + shift_vec


def dot(left_side, right_side):
    return jnp.dot(left_side, right_side, preferred_element_type=F32)


def cross_rows(left_side, right_side):
    return lax.dot_general(left_side, right_side, (((0,), (0,)), ((), ())), preferred_element_type=F32)


def times_rows(left_side, right_side):
    return lax.dot_general(left_side, right_side, (((1,), (1,)), ((), ())), preferred_element_type=F32)


def after(value, other):
    return lax.optimization_barrier((value, other))[0]


def place(sources, steps, dest_rows, dest_cols, block, out_shape, out_dtype, offset=None):
    count = len(steps)
    spans = []
    table = []
    for which in range(len(sources)):
        mine = [i for i, step in enumerate(steps) if step[0] == which]
        first, last = mine[0], mine[-1]
        spans.append((first, last + 1))
        hold = [steps[min(max(i, first), last)] for i in range(count)]
        table.append([step[1] for step in hold])
        table.append([step[2] for step in hold])
    fixed = jnp.asarray(np.array(table, np.int32))
    if offset is not None:
        mask = lax.broadcasted_iota(jnp.int32, (fixed.shape[0], 1), 0)
        fixed = fixed + jnp.where(mask == 0, offset[0], jnp.where(mask == 1, offset[1], 0))
    table = jnp.concatenate(
        [fixed, dest_rows.astype(jnp.int32)[None], dest_cols.astype(jnp.int32)[None]]
    )
    last_row = 2 * len(sources)

    def body(table_ref, *refs):
        step = pl.program_id(0)
        out_ref = refs[-1]
        for which, (first, stop) in enumerate(spans):

            @pl.when((step >= first) & (step < stop))
            def _():
                out_ref[...] = refs[which][...].astype(out_dtype)

    def in_map(which):
        return lambda i, table_ref: (table_ref[2 * which, i], table_ref[2 * which + 1, i])

    return pl.pallas_call(
        body,
        grid_spec=pltpu.PrefetchScalarGridSpec(
            num_scalar_prefetch=1,
            grid=(count,),
            in_specs=[pl.BlockSpec(block, in_map(which)) for which in range(len(sources))],
            out_specs=pl.BlockSpec(block, lambda i, table_ref: (table_ref[last_row, i], table_ref[last_row + 1, i])),
        ),
        out_shape=jax.ShapeDtypeStruct(out_shape, out_dtype),
    )(table, *sources)


def head_parts(scal_ref, q_ref, k_ref, block, rows):
    half = 2 * rows
    core = scal_ref[0]
    prefix = scal_ref[1]
    side = block // 2
    offsets = [pl.multiple_of(core * half, half), pl.multiple_of((1 - core) * half, half)]
    q_off = pl.multiple_of(offsets[side] + (block % 2) * rows, rows)
    queries = q_ref[pl.ds(q_off, rows), :]
    chunks = [(offsets[0], half, 0)]
    if side == 1:
        chunks.append((offsets[1], (block - 1) * rows, half))
    scores = []
    for k_off, count, first in chunks:
        raw = lax.dot_general(
            queries, k_ref[pl.ds(k_off, count), :], (((1,), (1,)), ((), ())), preferred_element_type=F32
        )
        raw = raw * SCALE
        if first + count > block * rows:
            q_pos = block * rows + lax.broadcasted_iota(jnp.int32, raw.shape, 0)
            k_pos = first + lax.broadcasted_iota(jnp.int32, raw.shape, 1)
            raw = jnp.where((k_pos <= q_pos) | (k_pos < prefix), raw, MASKED)
        scores.append(raw)
    top = scores[0].max(axis=-1, keepdims=True)
    for raw in scores[1:]:
        top = jnp.maximum(top, raw.max(axis=-1, keepdims=True))
    terms = [jnp.exp(raw - top) for raw in scores]
    total = terms[0].sum(axis=-1, keepdims=True)
    for term in terms[1:]:
        total = total + term.sum(axis=-1, keepdims=True)
    inverse = 1.0 / total
    return q_off, queries, [(k_off, count, term * inverse) for (k_off, count, _), term in zip(chunks, terms)]


def attend_forward_body(scal_ref, q_ref, k_ref, v_ref, out_ref):
    rows = q_ref.shape[0] // 4
    for block in range(4):
        q_off, _, parts = head_parts(scal_ref, q_ref, k_ref, block, rows)
        total = None
        for k_off, count, soft in parts:
            term = jnp.dot(soft.astype(BF), v_ref[pl.ds(k_off, count), :], preferred_element_type=F32)
            total = term if total is None else total + term
        out_ref[pl.ds(q_off, rows), :] = total.astype(BF)


def attend_backward_body(scal_ref, q_ref, k_ref, v_ref, d_ref, dq_ref, dk_ref, dv_ref, dk_acc, dv_acc):
    rows = q_ref.shape[0] // 4
    dk_acc[...] = jnp.zeros_like(dk_acc)
    dv_acc[...] = jnp.zeros_like(dv_acc)
    for block in range(4):
        q_off, queries, parts = head_parts(scal_ref, q_ref, k_ref, block, rows)
        d_out = d_ref[pl.ds(q_off, rows), :]
        d_softs = []
        row_sum = None
        for k_off, count, soft in parts:
            dv_acc[pl.ds(k_off, count), :] += lax.dot_general(
                soft.astype(BF), d_out, (((0,), (0,)), ((), ())), preferred_element_type=F32
            )
            d_soft = lax.dot_general(
                d_out, v_ref[pl.ds(k_off, count), :], (((1,), (1,)), ((), ())), preferred_element_type=F32
            )
            d_softs.append(d_soft)
            term = jnp.sum(soft * d_soft, axis=-1, keepdims=True)
            row_sum = term if row_sum is None else row_sum + term
        d_queries = None
        for (k_off, count, soft), d_soft in zip(parts, d_softs):
            d_scores = (soft * (d_soft - row_sum) * SCALE).astype(BF)
            term = jnp.dot(d_scores, k_ref[pl.ds(k_off, count), :], preferred_element_type=F32)
            d_queries = term if d_queries is None else d_queries + term
            dk_acc[pl.ds(k_off, count), :] += lax.dot_general(
                d_scores, queries, (((0,), (0,)), ((), ())), preferred_element_type=F32
            )
        dq_ref[pl.ds(q_off, rows), :] = d_queries.astype(BF)
    dk_ref[...] = dk_acc[...].astype(BF)
    dv_ref[...] = dv_acc[...].astype(BF)


def head_specs(rows, heads):
    return [pl.BlockSpec((rows, HEAD_DIM), lambda h, scal_ref, at=at: (0, at * heads + h)) for at in range(3)]


def attend_forward(projected, scalars):
    rows, width = projected.shape
    heads = width // (3 * HEAD_DIM)
    return pl.pallas_call(
        attend_forward_body,
        grid_spec=pltpu.PrefetchScalarGridSpec(
            num_scalar_prefetch=1,
            grid=(heads,),
            in_specs=head_specs(rows, heads),
            out_specs=head_specs(rows, heads)[0],
        ),
        out_shape=jax.ShapeDtypeStruct((rows, width // 3), BF),
    )(scalars, projected, projected, projected)


def attend_backward(projected, d_context, scalars):
    rows, width = projected.shape
    heads = width // (3 * HEAD_DIM)
    one = head_specs(rows, heads)[0]
    return pl.pallas_call(
        attend_backward_body,
        grid_spec=pltpu.PrefetchScalarGridSpec(
            num_scalar_prefetch=1,
            grid=(heads,),
            in_specs=head_specs(rows, heads) + [one],
            out_specs=[one, one, one],
            scratch_shapes=[pltpu.VMEM((rows, HEAD_DIM), F32), pltpu.VMEM((rows, HEAD_DIM), F32)],
        ),
        out_shape=[jax.ShapeDtypeStruct((rows, width // 3), BF)] * 3,
    )(scalars, projected, projected, projected, d_context)


def spread_softmax(queries, keys, q_pos, k_pos, prefix):
    raw = jnp.einsum("qhd,khd->hqk", queries, keys, preferred_element_type=F32) * SCALE
    visible = (k_pos[None, :] <= q_pos[:, None]) | (k_pos[None, :] < prefix)
    raw = jnp.where(visible[None], raw, MASKED)
    terms = jnp.exp(raw - jnp.max(raw, axis=-1, keepdims=True))
    return terms / jnp.sum(terms, axis=-1, keepdims=True)


def spread_backward(queries, keys, values, d_context, soft):
    d_values = jnp.einsum("hqk,qhd->khd", soft.astype(BF), d_context, preferred_element_type=F32)
    d_soft = jnp.einsum("qhd,khd->hqk", d_context, values, preferred_element_type=F32)
    d_scores = (soft * (d_soft - jnp.sum(soft * d_soft, axis=-1, keepdims=True)) * SCALE).astype(BF)
    d_queries = jnp.einsum("hqk,khd->qhd", d_scores, keys, preferred_element_type=F32)
    d_keys = jnp.einsum("hqk,qhd->khd", d_scores, queries, preferred_element_type=F32)
    return d_queries, d_keys, d_values


def local(
    hidden_in,
    prefix,
    ln1_gain,
    ln1_bias,
    qkv_weight,
    q_bias,
    v_bias,
    out_weight,
    out_bias,
    ln2_gain,
    ln2_bias,
    fc1_weight,
    fc1_bias,
    fc2_weight,
    fc2_bias,
    grad_out,
    *,
    chips,
    shards,
):
    micro_count, tok_rows, width = hidden_in.shape
    ff_units = fc1_weight.shape[1]
    piece_rows = width // shards
    rows = micro_count * tok_rows
    parts = shards // (micro_count * CORES)
    ch = lax.axis_index("ch")
    core = lax.axis_index("co")
    shard = lax.axis_index("sh")
    sequence = shard // parts
    micro = sequence // CORES

    def along(value, hop):
        return lax.ppermute(value, "sh", [(i, (i + hop) % shards) for i in range(shards)])

    def plane(value, bit):
        return lax.ppermute(value, "ch", [(i, i ^ bit) for i in range(chips)])

    def swap(value):
        return lax.ppermute(value, "co", [(0, 1), (1, 0)])

    def token_pairs(turn):
        pairs = []
        for c in range(chips):
            for o in range(CORES):
                for s in range(shards):
                    m = (turn + s) % 2
                    slot = s // 2
                    z = (m * CORES + o) * parts + slot // 2
                    pairs.append(((c * CORES + o) * shards + s, (c * CORES + slot % 2) * shards + z))
        return pairs

    def tokens_in(value):
        got = [
            lax.ppermute(lax.dynamic_index_in_dim(value, (turn + shard) % 2, 0, False), ALL, token_pairs(turn))
            for turn in (0, 1)
        ]
        even = micro % 2 == 0
        return jnp.concatenate([jnp.where(even, got[0], got[1]), jnp.where(even, got[1], got[0])])

    def tokens_out(value):
        value = value.reshape(2, tok_rows, width)
        got = [
            lax.ppermute(
                lax.dynamic_index_in_dim(value, (turn + micro) % 2, 0, False),
                ALL,
                [(b, a) for a, b in token_pairs(turn)],
            )
            for turn in (0, 1)
        ]
        even = shard % 2 == 0
        return jnp.stack([jnp.where(even, got[0], got[1]), jnp.where(even, got[1], got[0])])

    def gather_shards(piece):
        held = lax.all_gather(piece, "sh")
        return [lax.dynamic_index_in_dim(held, (shard - hop) % shards, 0, False) for hop in range(1, shards)]

    def spread_others(others):
        from_x = plane(others, 1)
        from_y = plane(others, 2)
        tall = (shards - 1, 2, others.shape[0] // (2 * (shards - 1)), others.shape[1])
        low_cut = from_x.reshape(tall)[:, 0].reshape(-1, tall[3])
        high_cut = from_y.reshape(tall)[:, 1].reshape(-1, tall[3])
        return from_x, from_y, low_cut, high_cut

    def whole_weight(source, offset, col_step, height, others, from_x, from_y, low_part, high_part):
        cut = others.shape[1]
        steps, hops, flips, cols, halves = [], [], [], [], []
        for half in range(2):
            for col in range(chips):
                steps.append((0, half, col * col_step))
                hops.append(0), flips.append(-1), cols.append(col), halves.append(half)
        for which, flip in ((1, 0), (2, 1), (3, 2)):
            for hop in range(1, shards):
                for half in range(2):
                    steps.append((which, 2 * (hop - 1) + half, 0))
                    hops.append(hop), flips.append(flip), cols.append(0), halves.append(half)
        for which, half in ((4, 0), (5, 1)):
            for hop in range(1, shards):
                steps.append((which, hop - 1, 0))
                hops.append(hop), flips.append(3), cols.append(0), halves.append(half)
        hops, flips, cols, halves = (np.array(v, np.int32) for v in (hops, flips, cols, halves))
        return place(
            [source, others, from_x, from_y, low_part, high_part],
            steps,
            2 * ((shard - hops) % shards) + halves,
            jnp.where(flips < 0, cols, ch ^ np.maximum(flips, 0)),
            (height // 2, cut),
            (shards * height, chips * cut),
            BF,
            offset,
        )

    def whole_weight_any(piece):
        everything = lax.all_gather(lax.all_gather(piece, "sh"), "ch")
        return everything.transpose(1, 2, 0, 3).reshape(-1, chips * piece.shape[1])

    def grad_block(left_side, right_side, flip, half=None):
        cut = right_side.shape[1] // chips
        block = lax.dynamic_slice_in_dim(right_side, (ch ^ flip) * cut, cut, 1)
        if half is not None:
            width_half = left_side.shape[1] // 2
            left_side = left_side[:, half * width_half : (half + 1) * width_half]
        return cross_rows(left_side, block).astype(BF)

    def sum_shards(mine):
        return lax.psum_scatter(mine, "sh", scatter_dimension=0, tiled=True)

    def sum_any(left_side, right_side):
        cut = right_side.shape[1] // chips
        grads = cross_rows(left_side, right_side).astype(BF).reshape(-1, chips, cut).transpose(1, 0, 2)
        return sum_shards(lax.psum_scatter(grads, "ch", scatter_dimension=0))

    def spread_any(mine, chunk):
        height = mine.shape[0]
        own = lax.all_gather(mine, "ch", axis=1, tiled=True)
        other = swap(own)
        pair = [jnp.where(core == 0, own, other), jnp.where(core == 0, other, own)]
        if chunk is None:
            return jnp.concatenate(pair).astype(F32)
        wide = jnp.stack([member.reshape(height, -1, chunk) for member in pair], axis=2)
        return wide.reshape(height, -1).astype(F32)

    def spread_first(mine):
        from_x = plane(mine, 1)
        from_y = plane(mine, 2)
        return mine, from_x, from_y

    def spread_second(mine, from_x, from_y):
        middle_row = mine.shape[0] // 2
        low_part = plane(from_x[:middle_row], 2)
        high_part = plane(from_y[middle_row:], 1)
        own = jnp.concatenate([mine, from_x, from_y, low_part, high_part])
        return own, swap(own)

    def spread_last(own, other, chunk):
        height, cut = own.shape[0] // 4, own.shape[1]
        block_cols = cut if chunk is None else chunk
        per = cut // block_cols
        steps, flips, cores, inner = [], [], [], []
        for source in range(2):
            for flip in range(4):
                for at in range(per):
                    steps.append((source, flip, at))
                    flips.append(flip), cores.append(source), inner.append(at)
        flips, cores, inner = (np.array(v, np.int32) for v in (flips, cores, inner))
        side = core ^ cores
        cols = (ch ^ flips) * per + inner
        if chunk is None:
            dest_rows, dest_cols, shape = side, cols, (2 * height, chips * cut)
        else:
            dest_rows, dest_cols, shape = 0 * side, cols * 2 + side, (height, 2 * chips * cut)
        return place([own, other], steps, dest_rows, dest_cols, (height, block_cols), shape, F32)

    def take(value, axis):
        return lax.dynamic_index_in_dim(value, core, axis, False)

    qkv_chunk = width // (shards * CORES)
    fc1_chunk = ff_units // (shards * CORES)

    def col_chunks(value, chunk, first, count):
        cuts = [lax.dynamic_slice_in_dim(value, ((first + i) * CORES + core) * chunk, chunk, 1) for i in range(count)]
        return cuts[0] if count == 1 else jnp.concatenate(cuts, axis=1)

    def col_piece(value, chunk):
        per = value.shape[1] // (CORES * chips * chunk)
        return col_chunks(value, chunk, ch * per, per)

    def row_piece(value):
        height, cut = value.shape[0] // CORES, value.shape[1] // chips
        return lax.dynamic_slice(value, (core * height, ch * cut), (height, cut))

    qkv_piece = col_piece(qkv_weight, qkv_chunk)
    fc1_piece = col_piece(fc1_weight, fc1_chunk)
    out_piece = row_piece(out_weight)
    fc2_piece = row_piece(fc2_weight)

    vectors = [ln1_gain, ln1_bias, q_bias, v_bias, out_bias, ln2_gain, ln2_bias, fc2_bias, fc1_bias]
    lengths = [v.shape[0] for v in vectors]
    edges = np.cumsum([0] + lengths)
    square = chips == 4
    small = jnp.concatenate(vectors)
    ring = [small] + [along(small, hop) for hop in range(shards - 1, 0, -1)]
    qkv_piece, *ring = lax.optimization_barrier((qkv_piece, *ring))
    gathered = lax.dynamic_slice_in_dim(jnp.stack(ring + ring), (shards - shard) % shards, shards, 0)
    vec = [gathered[:, edges[i] : edges[i + 1]].astype(F32) for i in range(len(vectors))]
    gain_one, shift_one, _, _, bias_out, gain_two, shift_two, bias_down, _ = [v.reshape(-1) for v in vec]
    bias_query, bias_value, bias_up = [
        take(vec[i].reshape(shards, CORES, -1), 1).reshape(-1) for i in (2, 3, 8)
    ]

    prefix_pair = [jnp.where(core == 0, a, b) for a, b in ((prefix, swap(prefix)), (swap(prefix), prefix))]
    prefix_len = jnp.concatenate(prefix_pair, axis=1).reshape(-1)[sequence]

    tokens_from = hidden_in
    if square:
        qkv_others = jnp.concatenate(gather_shards(qkv_piece))
        tokens_from = after(hidden_in, qkv_others)
        out_got = gather_shards(out_piece)
        out_others = jnp.concatenate(out_got)
        fc1_others = jnp.concatenate(gather_shards(fc1_piece))
        fc2_got = gather_shards(after(fc2_piece, out_got[0]))
        fc2_others = jnp.concatenate(fc2_got)
        qkv_x, qkv_y, qkv_low, qkv_high = spread_others(qkv_others)
        qkv_ends = plane(qkv_low, 2), plane(qkv_high, 1)
        out_others = after(out_others, (qkv_low, qkv_high))
        out_x, out_y, out_low, out_high = spread_others(out_others)
        fc1_others = after(fc1_others, (qkv_ends, out_others))
        fc1_x, fc1_y, fc1_low, fc1_high = spread_others(fc1_others)
        fc1_ends = plane(fc1_low, 2), plane(fc1_high, 1)
        fc2_others = after(fc2_others, fc1_ends)
        fc2_x, fc2_y, fc2_low, fc2_high = spread_others(fc2_others)

    tokens = lax.optimization_barrier(tokens_in(tokens_from))
    hidden_f = tokens.astype(F32)
    normed_own = normalize(hidden_f, gain_one, shift_one).astype(BF)
    normed_one = jnp.concatenate([normed_own, swap(normed_own)])
    none = jnp.zeros((), jnp.int32)
    if square:
        qkv_mine = col_chunks(qkv_weight, qkv_chunk, 0, 3 * shards)
        qkv_full = whole_weight(
            qkv_mine, None, 1, piece_rows, qkv_others, qkv_x, qkv_y, *qkv_ends
        )
        out_full = whole_weight(
            out_weight, (2 * core, none), 1, piece_rows // 2, out_others, out_x, out_y, plane(out_low, 2), plane(out_high, 1)
        )
        fc1_full = whole_weight(
            fc1_weight, (none, core), 2, piece_rows, fc1_others, fc1_x, fc1_y, *fc1_ends
        )
        fc2_full = whole_weight(
            fc2_weight,
            (2 * core, none),
            1,
            fc2_weight.shape[0] // 2,
            fc2_others,
            fc2_x,
            fc2_y,
            plane(fc2_low, 2),
            plane(fc2_high, 1),
        )
        grads_mine = tokens_in(after(grad_out, fc2_others))
    else:
        qkv_full, out_full, fc1_full, fc2_full = [
            whole_weight_any(piece) for piece in (qkv_piece, out_piece, fc1_piece, fc2_piece)
        ]
        grads_mine = tokens_in(grad_out)
    grads_mine = lax.optimization_barrier(grads_mine)

    half_width = width // CORES
    projected = dot(normed_one, qkv_full) + jnp.concatenate([bias_query, jnp.zeros_like(bias_query), bias_value])
    projected = projected.astype(BF)
    scalars = jnp.stack([core.astype(jnp.int32), prefix_len.astype(jnp.int32)])
    if parts == 1:
        context = attend_forward(projected, scalars)
    else:
        part = shard % parts

        def to_part(value, hop):
            pairs = [(i, i // parts * parts + (i % parts + hop) % parts) for i in range(shards)]
            return lax.ppermute(value, "sh", pairs)

        def positions(which):
            at = jnp.arange(rows)
            return which * CORES * rows + jnp.concatenate([core * rows + at, (1 - core) * rows + at])

        q_four = projected[:, :half_width].reshape(CORES * rows, -1, HEAD_DIM)
        both = projected[:, half_width:]
        held = jnp.concatenate([both] + [to_part(both, hop) for hop in range(1, parts)])
        k_four = held[:, :half_width].reshape(held.shape[0], -1, HEAD_DIM)
        v_four = held[:, half_width:].reshape(held.shape[0], -1, HEAD_DIM)
        k_pos = jnp.concatenate([positions((part - hop) % parts) for hop in range(parts)])
        soft_full = spread_softmax(q_four, k_four, positions(part), k_pos, prefix_len)
        context = jnp.einsum("hqk,khd->qhd", soft_full.astype(BF), v_four, preferred_element_type=F32)
        context = context.reshape(CORES * rows, half_width).astype(BF)

    if square:
        context = after(context, fc1_ends)

    def own_sum(left_side, product):
        away = swap(product(left_side[rows:]).astype(BF))
        return product(left_side[:rows]) + away.astype(F32)

    middle = hidden_f + (own_sum(context, lambda v: dot(v, out_full)) + bias_out)
    normed_two_own = normalize(middle, gain_two, shift_two).astype(BF)
    normed_two = jnp.concatenate([normed_two_own, swap(normed_two_own)])
    grads_mine = after(grads_mine, normed_two)
    if square:
        normed_two = after(normed_two, (fc2_low, fc2_high))
    pre_act = dot(normed_two, fc1_full) + bias_up
    below = 0.5 * (1.0 + lax.erf(pre_act * math.sqrt(0.5)))
    density = jnp.exp(-0.5 * pre_act * pre_act) * (1.0 / math.sqrt(2.0 * math.pi))
    activated = (pre_act * below).astype(BF)
    slope = (below + pre_act * density).astype(BF)

    grad_rows = grads_mine.astype(F32)
    grad_both = jnp.concatenate([grads_mine, swap(grads_mine)])
    down_bias_grad = jnp.sum(grad_rows, axis=0)

    class Reduction:
        def __init__(self, left_side, right_side, barrier=()):
            self.sides = (left_side, right_side)
            far_low = grad_block(left_side, right_side, 3, 0)
            far_high = grad_block(left_side, right_side, 3, 1)
            self.far = (plane(far_low, 2), plane(far_high, 1))
            right_side = after(right_side, (far_low, far_high, *barrier))
            self.x_high = plane(grad_block(left_side, right_side, 1, 1), 1)
            self.y_low = plane(grad_block(left_side, right_side, 2, 0), 2)
            self.near = [grad_block(left_side, right_side, 1, 0), grad_block(left_side, right_side, 2, 1)]

        def second(self, barrier=None):
            far = self.far if barrier is None else tuple(after(value, barrier) for value in self.far)
            self.sent = [self.near[0] + far[0], self.near[1] + far[1]]
            self.x_low = plane(self.sent[0], 1)
            self.y_high = plane(self.sent[1], 2)

        def third(self, barrier=None):
            x_low, y_high = self.x_low, self.y_high
            if barrier is not None:
                x_low, y_high = after(x_low, barrier), after(y_high, barrier)
            low_part = grad_block(*self.sides, 0, 0).astype(F32) + x_low.astype(F32) + self.y_low.astype(F32)
            high_part = grad_block(*self.sides, 0, 1).astype(F32) + self.x_high.astype(F32) + y_high.astype(F32)
            self.mine = jnp.concatenate([low_part.astype(BF), high_part.astype(BF)])
            return sum_shards(self.mine)

    if square:
        fc2_red = Reduction(activated, after(grad_both, (fc2_low, fc2_high)))
    d_pre = (times_rows(grad_both, fc2_full) * slope.astype(F32)).astype(BF)
    up_bias_grad = jnp.sum(d_pre, axis=0, dtype=F32)
    if square:
        fc2_red.second()
        d_pre = after(d_pre, (fc2_red.sent, fc2_red.x_high, fc2_red.y_low))
        fc1_red = Reduction(normed_two, d_pre, (fc2_red.x_low, fc2_red.y_high))
        activated = after(activated, fc1_red.near)
    result_own = middle + (own_sum(activated, lambda v: dot(v, fc2_full)) + bias_down)
    result = tokens_out(result_own.astype(BF))
    if square:
        d_pre = after(d_pre, result_own)
    d_normed_two = own_sum(d_pre, lambda v: times_rows(v, fc1_full))
    back_two = jax.vjp(normalize, middle, gain_two, shift_two)[1]
    d_middle, gain_two_grad, shift_two_grad = back_two(d_normed_two)
    d_middle = d_middle + grad_rows
    d_attn_own = d_middle.astype(BF)
    out_bias_grad = jnp.sum(d_attn_own, axis=0, dtype=F32)
    d_attn = jnp.concatenate([d_attn_own, swap(d_attn_own)])
    if square:
        fc1_red.second(fc2_red.sent)
        out_red = Reduction(context, d_attn)
    d_context = times_rows(d_attn, out_full).astype(BF)
    if square:
        d_context = after(d_context, fc1_red.sent)
    if parts == 1:
        d_queries, d_keys, d_values = attend_backward(projected, d_context, scalars)
    else:
        d_four = d_context.reshape(CORES * rows, -1, HEAD_DIM)
        d_queries, d_keys, d_values = spread_backward(q_four, k_four, v_four, d_four, soft_full)
        d_queries = d_queries.reshape(CORES * rows, half_width).astype(BF)
        d_held = jnp.concatenate([d_keys, d_values], axis=1).reshape(parts, CORES * rows, width)
        d_both = d_held[0]
        for hop in range(1, parts):
            d_both = d_both + to_part(d_held[hop].astype(BF), parts - hop).astype(F32)
        d_both = d_both.astype(BF)
        d_keys, d_values = d_both[:, :half_width], d_both[:, half_width:]
    d_projected = jnp.concatenate([d_queries, d_keys, d_values], axis=1)
    if square:
        fc2_part = fc2_red.third()
        d_projected = after(d_projected, (fc2_red.mine, result, fc1_red.x_high, fc1_red.y_low))
        qkv_red = Reduction(normed_one, d_projected)
        out_red.second()
        fc1_part = fc1_red.third(qkv_red.near)
        qkv_red.second((fc1_red.mine, out_red.sent))
        d_projected = after(d_projected, qkv_red.sent)
    query_bias_grad = jnp.sum(d_projected[:, :half_width], axis=0, dtype=F32)
    value_bias_grad = jnp.sum(d_projected[:, width:], axis=0, dtype=F32)
    d_normed_one = own_sum(d_projected, lambda v: times_rows(v, qkv_full))
    back_one = jax.vjp(normalize, hidden_f, gain_one, shift_one)[1]
    d_inputs, gain_one_grad, shift_one_grad = back_one(d_normed_one)
    grad_in_own = (d_middle + d_inputs).astype(BF)

    def half_slot(value):
        value = value.reshape(shards, 1, -1)
        mask = lax.broadcasted_iota(jnp.int32, (1, CORES, 1), 1) == core
        return jnp.where(mask, value, 0.0).reshape(shards, -1)

    def full_slot(value):
        return value.reshape(shards, -1)

    packed = jnp.concatenate(
        [
            full_slot(gain_one_grad),
            full_slot(shift_one_grad),
            half_slot(query_bias_grad),
            half_slot(value_bias_grad),
            full_slot(out_bias_grad),
            full_slot(gain_two_grad),
            full_slot(shift_two_grad),
            full_slot(down_bias_grad),
            half_slot(up_bias_grad),
        ],
        axis=1,
    )
    def sum_plane(values, bits):
        for bit in bits:
            values = values + plane(values, 1 << bit)
        return values

    def sum_line(values):
        total = lax.dynamic_index_in_dim(values, shard, 0, False)
        for hop in range(1, shards):
            total = total + along(lax.dynamic_index_in_dim(values, (shard + hop) % shards, 0, False), hop)
        return total

    packed = packed + swap(packed)
    if square:
        out_part = out_red.third((qkv_red.sent, qkv_red.x_high, qkv_red.y_low))
        fc2_first = spread_first(after(fc2_part, (qkv_red.sent, out_red.mine)))
        qkv_part = qkv_red.third(grad_in_own)
        grad_in = tokens_out(after(grad_in_own, qkv_part))
        packed = sum_plane(packed, [0])
        fc1_first = spread_first(after(fc1_part, (fc2_first[1:], qkv_red.mine, packed)))
        fc2_pair = spread_second(*fc2_first)
        packed = sum_plane(packed, [1])
        out_first = spread_first(after(out_part, (fc1_first[1:], fc2_pair[0], packed)))
        summed = sum_line(after(packed, qkv_part))
        fc1_pair = spread_second(*fc1_first)
        fc2_weight_grad = spread_last(*fc2_pair, None)
        fc1_weight_grad = spread_last(*fc1_pair, fc1_chunk)
        out_pair = spread_second(*out_first)
        qkv_first = spread_first(after(qkv_part, (out_pair[0], fc1_pair[0], fc2_weight_grad)))
        out_weight_grad = spread_last(*out_pair, None)
        qkv_own, qkv_other = spread_second(*after(qkv_first, (fc1_weight_grad, out_pair[1])))
        qkv_weight_grad = spread_last(qkv_own, after(qkv_other, (out_weight_grad, grad_in)), qkv_chunk)
    else:
        grad_in = tokens_out(grad_in_own)
        summed = sum_line(sum_plane(packed, range(chips.bit_length() - 1)))
        fc2_weight_grad = spread_any(sum_any(activated, grad_both), None)
        fc1_weight_grad = spread_any(sum_any(normed_two, d_pre), fc1_chunk)
        out_weight_grad = spread_any(sum_any(context, d_attn), None)
        qkv_weight_grad = spread_any(sum_any(normed_one, d_projected), qkv_chunk)
    sums = [summed[edges[i] : edges[i + 1]] for i in range(len(vectors))]
    return (
        result,
        grad_in,
        sums[0],
        sums[1],
        qkv_weight_grad,
        sums[2],
        sums[3],
        out_weight_grad,
        sums[4],
        sums[5],
        sums[6],
        fc1_weight_grad,
        sums[8],
        fc2_weight_grad,
        sums[7],
    )


def solution(mesh):
    shards = mesh.shape["shard"]
    chips = mesh.shape["rep"] // CORES
    inner = Mesh(mesh.devices.reshape(chips, CORES, shards), ALL)
    token_spec = P(None, ALL, None)
    args = [token_spec, P(None, ("ch", "co"))]
    for dims in (1, 1, 2, 1, 1, 2, 1, 1, 1, 2, 1, 2, 1):
        args.append(P("sh", None) if dims == 2 else P("sh"))
    args.append(token_spec)
    outs = [token_spec, token_spec]
    for dims in (1, 1, 2, 1, 1, 2, 1, 1, 1, 2, 1, 2, 1):
        outs.append(P("sh", None) if dims == 2 else P("sh"))

    def run(*values):
        return local(*values, chips=chips, shards=shards)

    return jax.shard_map(run, mesh=inner, in_specs=tuple(args), out_specs=tuple(outs), check_vma=False)
```

```python
import math

import jax
import jax.numpy as jnp
import numpy as np
from jax import lax
from jax.experimental import pallas as pl
from jax.experimental.pallas import tpu as pltpu
from jax.sharding import Mesh
from jax.sharding import PartitionSpec as P

HEADS = 16
HEAD_DIM = 128
CORES = 2
EPSILON = 1e-05
MASKED = -1e30
SCALE = 1.0 / math.sqrt(HEAD_DIM)
ALL = ("ch", "co", "sh")
BF = jnp.bfloat16
F32 = jnp.float32


def normalize(values, gain_vec, shift_vec):
    centred = values - jnp.mean(values, axis=-1, keepdims=True)
    spread = jnp.mean(centred * centred, axis=-1, keepdims=True)
    return centred * lax.rsqrt(spread + EPSILON) * gain_vec + shift_vec


def dot(left_side, right_side):
    return jnp.dot(left_side, right_side, preferred_element_type=F32)


def cross_rows(left_side, right_side):
    return lax.dot_general(left_side, right_side, (((0,), (0,)), ((), ())), preferred_element_type=F32)


def times_rows(left_side, right_side):
    return lax.dot_general(left_side, right_side, (((1,), (1,)), ((), ())), preferred_element_type=F32)


def after(value, other):
    return lax.optimization_barrier((value, other))[0]


def place(sources, steps, dest_rows, dest_cols, block, out_shape, out_dtype, offset=None):
    count = len(steps)
    spans = []
    table = []
    for which in range(len(sources)):
        mine = [i for i, step in enumerate(steps) if step[0] == which]
        first, last = mine[0], mine[-1]
        spans.append((first, last + 1))
        hold = [steps[min(max(i, first), last)] for i in range(count)]
        table.append([step[1] for step in hold])
        table.append([step[2] for step in hold])
    fixed = jnp.asarray(np.array(table, np.int32))
    if offset is not None:
        mask = lax.broadcasted_iota(jnp.int32, (fixed.shape[0], 1), 0)
        fixed = fixed + jnp.where(mask == 0, offset[0], jnp.where(mask == 1, offset[1], 0))
    table = jnp.concatenate(
        [fixed, dest_rows.astype(jnp.int32)[None], dest_cols.astype(jnp.int32)[None]]
    )
    last_row = 2 * len(sources)

    def body(table_ref, *refs):
        step = pl.program_id(0)
        out_ref = refs[-1]
        for which, (first, stop) in enumerate(spans):

            @pl.when((step >= first) & (step < stop))
            def _():
                out_ref[...] = refs[which][...].astype(out_dtype)

    def in_map(which):
        return lambda i, table_ref: (table_ref[2 * which, i], table_ref[2 * which + 1, i])

    return pl.pallas_call(
        body,
        grid_spec=pltpu.PrefetchScalarGridSpec(
            num_scalar_prefetch=1,
            grid=(count,),
            in_specs=[pl.BlockSpec(block, in_map(which)) for which in range(len(sources))],
            out_specs=pl.BlockSpec(block, lambda i, table_ref: (table_ref[last_row, i], table_ref[last_row + 1, i])),
        ),
        out_shape=jax.ShapeDtypeStruct(out_shape, out_dtype),
    )(table, *sources)


def head_parts(scal_ref, q_ref, k_ref, block, rows):
    half = 2 * rows
    core = scal_ref[0]
    prefix = scal_ref[1]
    side = block // 2
    offsets = [pl.multiple_of(core * half, half), pl.multiple_of((1 - core) * half, half)]
    q_off = pl.multiple_of(offsets[side] + (block % 2) * rows, rows)
    queries = q_ref[pl.ds(q_off, rows), :]
    chunks = [(offsets[0], half, 0)]
    if side == 1:
        chunks.append((offsets[1], (block - 1) * rows, half))
    scores = []
    for k_off, count, first in chunks:
        raw = lax.dot_general(
            queries, k_ref[pl.ds(k_off, count), :], (((1,), (1,)), ((), ())), preferred_element_type=F32
        )
        raw = raw * SCALE
        if first + count > block * rows:
            q_pos = block * rows + lax.broadcasted_iota(jnp.int32, raw.shape, 0)
            k_pos = first + lax.broadcasted_iota(jnp.int32, raw.shape, 1)
            raw = jnp.where((k_pos <= q_pos) | (k_pos < prefix), raw, MASKED)
        scores.append(raw)
    top = scores[0].max(axis=-1, keepdims=True)
    for raw in scores[1:]:
        top = jnp.maximum(top, raw.max(axis=-1, keepdims=True))
    terms = [jnp.exp(raw - top) for raw in scores]
    total = terms[0].sum(axis=-1, keepdims=True)
    for term in terms[1:]:
        total = total + term.sum(axis=-1, keepdims=True)
    inverse = 1.0 / total
    return q_off, queries, [(k_off, count, term * inverse) for (k_off, count, _), term in zip(chunks, terms)]


def attend_forward_body(scal_ref, q_ref, k_ref, v_ref, out_ref):
    rows = q_ref.shape[0] // 4
    for block in range(4):
        q_off, _, parts = head_parts(scal_ref, q_ref, k_ref, block, rows)
        total = None
        for k_off, count, soft in parts:
            term = jnp.dot(soft.astype(BF), v_ref[pl.ds(k_off, count), :], preferred_element_type=F32)
            total = term if total is None else total + term
        out_ref[pl.ds(q_off, rows), :] = total.astype(BF)


def attend_backward_body(scal_ref, q_ref, k_ref, v_ref, d_ref, dq_ref, dk_ref, dv_ref, dk_acc, dv_acc):
    rows = q_ref.shape[0] // 4
    dk_acc[...] = jnp.zeros_like(dk_acc)
    dv_acc[...] = jnp.zeros_like(dv_acc)
    for block in range(4):
        q_off, queries, parts = head_parts(scal_ref, q_ref, k_ref, block, rows)
        d_out = d_ref[pl.ds(q_off, rows), :]
        d_softs = []
        row_sum = None
        for k_off, count, soft in parts:
            dv_acc[pl.ds(k_off, count), :] += lax.dot_general(
                soft.astype(BF), d_out, (((0,), (0,)), ((), ())), preferred_element_type=F32
            )
            d_soft = lax.dot_general(
                d_out, v_ref[pl.ds(k_off, count), :], (((1,), (1,)), ((), ())), preferred_element_type=F32
            )
            d_softs.append(d_soft)
            term = jnp.sum(soft * d_soft, axis=-1, keepdims=True)
            row_sum = term if row_sum is None else row_sum + term
        d_queries = None
        for (k_off, count, soft), d_soft in zip(parts, d_softs):
            d_scores = (soft * (d_soft - row_sum) * SCALE).astype(BF)
            term = jnp.dot(d_scores, k_ref[pl.ds(k_off, count), :], preferred_element_type=F32)
            d_queries = term if d_queries is None else d_queries + term
            dk_acc[pl.ds(k_off, count), :] += lax.dot_general(
                d_scores, queries, (((0,), (0,)), ((), ())), preferred_element_type=F32
            )
        dq_ref[pl.ds(q_off, rows), :] = d_queries.astype(BF)
    dk_ref[...] = dk_acc[...].astype(BF)
    dv_ref[...] = dv_acc[...].astype(BF)


def head_specs(rows, heads):
    return [pl.BlockSpec((rows, HEAD_DIM), lambda h, scal_ref, at=at: (0, at * heads + h)) for at in range(3)]


def attend_forward(projected, scalars):
    rows, width = projected.shape
    heads = width // (3 * HEAD_DIM)
    return pl.pallas_call(
        attend_forward_body,
        grid_spec=pltpu.PrefetchScalarGridSpec(
            num_scalar_prefetch=1,
            grid=(heads,),
            in_specs=head_specs(rows, heads),
            out_specs=head_specs(rows, heads)[0],
        ),
        out_shape=jax.ShapeDtypeStruct((rows, width // 3), BF),
    )(scalars, projected, projected, projected)


def attend_backward(projected, d_context, scalars):
    rows, width = projected.shape
    heads = width // (3 * HEAD_DIM)
    one = head_specs(rows, heads)[0]
    return pl.pallas_call(
        attend_backward_body,
        grid_spec=pltpu.PrefetchScalarGridSpec(
            num_scalar_prefetch=1,
            grid=(heads,),
            in_specs=head_specs(rows, heads) + [one],
            out_specs=[one, one, one],
            scratch_shapes=[pltpu.VMEM((rows, HEAD_DIM), F32), pltpu.VMEM((rows, HEAD_DIM), F32)],
        ),
        out_shape=[jax.ShapeDtypeStruct((rows, width // 3), BF)] * 3,
    )(scalars, projected, projected, projected, d_context)


def spread_softmax(queries, keys, q_pos, k_pos, prefix):
    raw = jnp.einsum("qhd,khd->hqk", queries, keys, preferred_element_type=F32) * SCALE
    visible = (k_pos[None, :] <= q_pos[:, None]) | (k_pos[None, :] < prefix)
    raw = jnp.where(visible[None], raw, MASKED)
    terms = jnp.exp(raw - jnp.max(raw, axis=-1, keepdims=True))
    return terms / jnp.sum(terms, axis=-1, keepdims=True)


def spread_backward(queries, keys, values, d_context, soft):
    d_values = jnp.einsum("hqk,qhd->khd", soft.astype(BF), d_context, preferred_element_type=F32)
    d_soft = jnp.einsum("qhd,khd->hqk", d_context, values, preferred_element_type=F32)
    d_scores = (soft * (d_soft - jnp.sum(soft * d_soft, axis=-1, keepdims=True)) * SCALE).astype(BF)
    d_queries = jnp.einsum("hqk,khd->qhd", d_scores, keys, preferred_element_type=F32)
    d_keys = jnp.einsum("hqk,qhd->khd", d_scores, queries, preferred_element_type=F32)
    return d_queries, d_keys, d_values


def local(
    hidden_in,
    prefix,
    ln1_gain,
    ln1_bias,
    qkv_weight,
    q_bias,
    v_bias,
    out_weight,
    out_bias,
    ln2_gain,
    ln2_bias,
    fc1_weight,
    fc1_bias,
    fc2_weight,
    fc2_bias,
    grad_out,
    *,
    chips,
    shards,
):
    micro_count, tok_rows, width = hidden_in.shape
    ff_units = fc1_weight.shape[1]
    piece_rows = width // shards
    rows = micro_count * tok_rows
    parts = shards // (micro_count * CORES)
    ch = lax.axis_index("ch")
    core = lax.axis_index("co")
    shard = lax.axis_index("sh")
    sequence = shard // parts
    micro = sequence // CORES

    def along(value, hop):
        return lax.ppermute(value, "sh", [(i, (i + hop) % shards) for i in range(shards)])

    def plane(value, bit):
        return lax.ppermute(value, "ch", [(i, i ^ bit) for i in range(chips)])

    def swap(value):
        return lax.ppermute(value, "co", [(0, 1), (1, 0)])

    def token_pairs(turn):
        pairs = []
        for c in range(chips):
            for o in range(CORES):
                for s in range(shards):
                    m = (turn + s) % 2
                    slot = s // 2
                    z = (m * CORES + o) * parts + slot // 2
                    pairs.append(((c * CORES + o) * shards + s, (c * CORES + slot % 2) * shards + z))
        return pairs

    def tokens_in(value):
        got = [
            lax.ppermute(lax.dynamic_index_in_dim(value, (turn + shard) % 2, 0, False), ALL, token_pairs(turn))
            for turn in (0, 1)
        ]
        even = micro % 2 == 0
        return jnp.concatenate([jnp.where(even, got[0], got[1]), jnp.where(even, got[1], got[0])])

    def tokens_out(value):
        value = value.reshape(2, tok_rows, width)
        got = [
            lax.ppermute(
                lax.dynamic_index_in_dim(value, (turn + micro) % 2, 0, False),
                ALL,
                [(b, a) for a, b in token_pairs(turn)],
            )
            for turn in (0, 1)
        ]
        even = shard % 2 == 0
        return jnp.stack([jnp.where(even, got[0], got[1]), jnp.where(even, got[1], got[0])])

    def gather_shards(piece):
        return lax.all_gather(piece, "sh")

    def others_of(held):
        return jnp.concatenate(
            [lax.dynamic_index_in_dim(held, (shard - hop) % shards, 0, False) for hop in range(1, shards)]
        )

    def spread_others(others):
        from_x = plane(others, 1)
        from_y = plane(others, 2)
        tall = (shards - 1, 2, others.shape[0] // (2 * (shards - 1)), others.shape[1])
        low_cut = from_x.reshape(tall)[:, 0].reshape(-1, tall[3])
        high_cut = from_y.reshape(tall)[:, 1].reshape(-1, tall[3])
        return from_x, from_y, low_cut, high_cut

    def whole_weight(source, offset, col_step, height, others, from_x, from_y, low_part, high_part):
        cut = others.shape[1]
        steps, hops, flips, cols, halves = [], [], [], [], []
        for half in range(2):
            for col in range(chips):
                steps.append((0, half, col * col_step))
                hops.append(0), flips.append(-1), cols.append(col), halves.append(half)
        for which, flip in ((1, 0), (2, 1), (3, 2)):
            for hop in range(1, shards):
                for half in range(2):
                    steps.append((which, 2 * (hop - 1) + half, 0))
                    hops.append(hop), flips.append(flip), cols.append(0), halves.append(half)
        for which, half in ((4, 0), (5, 1)):
            for hop in range(1, shards):
                steps.append((which, hop - 1, 0))
                hops.append(hop), flips.append(3), cols.append(0), halves.append(half)
        hops, flips, cols, halves = (np.array(v, np.int32) for v in (hops, flips, cols, halves))
        return place(
            [source, others, from_x, from_y, low_part, high_part],
            steps,
            2 * ((shard - hops) % shards) + halves,
            jnp.where(flips < 0, cols, ch ^ np.maximum(flips, 0)),
            (height // 2, cut),
            (shards * height, chips * cut),
            BF,
            offset,
        )

    def whole_weight_any(piece):
        everything = lax.all_gather(lax.all_gather(piece, "sh"), "ch")
        return everything.transpose(1, 2, 0, 3).reshape(-1, chips * piece.shape[1])

    def grad_block(left_side, right_side, flips, half):
        cut = right_side.shape[1] // chips
        blocks = [lax.dynamic_slice_in_dim(right_side, (ch ^ flip) * cut, cut, 1) for flip in flips]
        block = blocks[0] if len(flips) == 1 else jnp.concatenate(blocks, axis=1)
        width_half = left_side.shape[1] // 2
        return cross_rows(left_side[:, half * width_half : (half + 1) * width_half], block).astype(BF)

    def sum_shards(mine):
        return lax.psum_scatter(mine, "sh", scatter_dimension=0, tiled=True)

    def sum_any(left_side, right_side):
        cut = right_side.shape[1] // chips
        grads = cross_rows(left_side, right_side).astype(BF).reshape(-1, chips, cut).transpose(1, 0, 2)
        return sum_shards(lax.psum_scatter(grads, "ch", scatter_dimension=0))

    def spread_any(mine, chunk):
        height = mine.shape[0]
        own = lax.all_gather(mine, "ch", axis=1, tiled=True)
        other = swap(own)
        pair = [jnp.where(core == 0, own, other), jnp.where(core == 0, other, own)]
        if chunk is None:
            return jnp.concatenate(pair).astype(F32)
        wide = jnp.stack([member.reshape(height, -1, chunk) for member in pair], axis=2)
        return wide.reshape(height, -1).astype(F32)

    def spread_first(mine):
        from_x = plane(mine, 1)
        from_y = plane(mine, 2)
        return mine, from_x, from_y

    def spread_second(mine, from_x, from_y):
        middle_row = mine.shape[0] // 2
        low_part = plane(from_x[:middle_row], 2)
        high_part = plane(from_y[middle_row:], 1)
        own = jnp.concatenate([mine, from_x, from_y, low_part, high_part])
        return own, swap(own)

    def spread_last(own, other, chunk):
        height, cut = own.shape[0] // 4, own.shape[1]
        block_cols = cut if chunk is None else chunk
        per = cut // block_cols
        steps, flips, cores, inner = [], [], [], []
        for source in range(2):
            for flip in range(4):
                for at in range(per):
                    steps.append((source, flip, at))
                    flips.append(flip), cores.append(source), inner.append(at)
        flips, cores, inner = (np.array(v, np.int32) for v in (flips, cores, inner))
        side = core ^ cores
        cols = (ch ^ flips) * per + inner
        if chunk is None:
            dest_rows, dest_cols, shape = side, cols, (2 * height, chips * cut)
        else:
            dest_rows, dest_cols, shape = 0 * side, cols * 2 + side, (height, 2 * chips * cut)
        return place([own, other], steps, dest_rows, dest_cols, (height, block_cols), shape, F32)

    def take(value, axis):
        return lax.dynamic_index_in_dim(value, core, axis, False)

    qkv_chunk = width // (shards * CORES)
    fc1_chunk = ff_units // (shards * CORES)

    def col_chunks(value, chunk, first, count):
        cuts = [lax.dynamic_slice_in_dim(value, ((first + i) * CORES + core) * chunk, chunk, 1) for i in range(count)]
        return cuts[0] if count == 1 else jnp.concatenate(cuts, axis=1)

    def col_piece(value, chunk):
        per = value.shape[1] // (CORES * chips * chunk)
        return col_chunks(value, chunk, ch * per, per)

    def row_piece(value):
        height, cut = value.shape[0] // CORES, value.shape[1] // chips
        return lax.dynamic_slice(value, (core * height, ch * cut), (height, cut))

    qkv_piece = col_piece(qkv_weight, qkv_chunk)
    fc1_piece = col_piece(fc1_weight, fc1_chunk)
    out_piece = row_piece(out_weight)
    fc2_piece = row_piece(fc2_weight)

    vectors = [ln1_gain, ln1_bias, q_bias, v_bias, out_bias, ln2_gain, ln2_bias, fc2_bias, fc1_bias]
    lengths = [v.shape[0] for v in vectors]
    edges = np.cumsum([0] + lengths)
    square = chips == 4
    small = jnp.concatenate(vectors)
    ring = [small] + [along(small, hop) for hop in range(shards - 1, 0, -1)]
    qkv_piece, *ring = lax.optimization_barrier((qkv_piece, *ring))
    gathered = lax.dynamic_slice_in_dim(jnp.stack(ring + ring), (shards - shard) % shards, shards, 0)
    vec = [gathered[:, edges[i] : edges[i + 1]].astype(F32) for i in range(len(vectors))]
    gain_one, shift_one, _, _, bias_out, gain_two, shift_two, bias_down, _ = [v.reshape(-1) for v in vec]
    bias_query, bias_value, bias_up = [
        take(vec[i].reshape(shards, CORES, -1), 1).reshape(-1) for i in (2, 3, 8)
    ]

    prefix_pair = [jnp.where(core == 0, a, b) for a, b in ((prefix, swap(prefix)), (swap(prefix), prefix))]
    prefix_len = jnp.concatenate(prefix_pair, axis=1).reshape(-1)[sequence]

    tokens_from = hidden_in
    if square:
        qkv_others = others_of(gather_shards(qkv_piece))
        tokens_from = after(hidden_in, qkv_others)
        out_got = gather_shards(out_piece)
        fc1_got = gather_shards(fc1_piece)
        fc2_got = gather_shards(after(fc2_piece, out_got))
        qkv_x, qkv_y, qkv_low, qkv_high = spread_others(qkv_others)
        qkv_ends = plane(qkv_low, 2), plane(qkv_high, 1)
        out_others = others_of(after(out_got, (qkv_low, qkv_high)))
        out_x, out_y, out_low, out_high = spread_others(out_others)

    tokens = lax.optimization_barrier(tokens_in(tokens_from))
    hidden_f = tokens.astype(F32)
    normed_own = normalize(hidden_f, gain_one, shift_one).astype(BF)
    normed_one = jnp.concatenate([normed_own, swap(normed_own)])
    none = jnp.zeros((), jnp.int32)
    if square:
        qkv_mine = col_chunks(qkv_weight, qkv_chunk, 0, 3 * shards)
        qkv_full = whole_weight(
            qkv_mine, None, 1, piece_rows, qkv_others, qkv_x, qkv_y, *qkv_ends
        )
        out_full = whole_weight(
            out_weight, (2 * core, none), 1, piece_rows // 2, out_others, out_x, out_y, plane(out_low, 2), plane(out_high, 1)
        )
    else:
        qkv_full, out_full, fc1_full, fc2_full = [
            whole_weight_any(piece) for piece in (qkv_piece, out_piece, fc1_piece, fc2_piece)
        ]
        grads_mine = tokens_in(grad_out)

    half_width = width // CORES
    projected = dot(normed_one, qkv_full) + jnp.concatenate([bias_query, jnp.zeros_like(bias_query), bias_value])
    projected = projected.astype(BF)
    if square:
        fc1_others = others_of(after(fc1_got, (projected, out_low, out_high)))
        fc1_x, fc1_y, fc1_low, fc1_high = spread_others(fc1_others)
        fc1_ends = plane(fc1_low, 2), plane(fc1_high, 1)
        fc2_others = others_of(after(fc2_got, fc1_ends))
        fc2_x, fc2_y, fc2_low, fc2_high = spread_others(fc2_others)
        fc1_full = whole_weight(
            fc1_weight, (none, core), 2, piece_rows, fc1_others, fc1_x, fc1_y, *fc1_ends
        )
        fc2_full = whole_weight(
            fc2_weight,
            (2 * core, none),
            1,
            fc2_weight.shape[0] // 2,
            fc2_others,
            fc2_x,
            fc2_y,
            plane(fc2_low, 2),
            plane(fc2_high, 1),
        )
        grads_mine = tokens_in(after(grad_out, fc2_others))
    grads_mine = lax.optimization_barrier(grads_mine)
    scalars = jnp.stack([core.astype(jnp.int32), prefix_len.astype(jnp.int32)])
    if parts == 1:
        context = attend_forward(projected, scalars)
    else:
        part = shard % parts

        def to_part(value, hop):
            pairs = [(i, i // parts * parts + (i % parts + hop) % parts) for i in range(shards)]
            return lax.ppermute(value, "sh", pairs)

        def positions(which):
            at = jnp.arange(rows)
            return which * CORES * rows + jnp.concatenate([core * rows + at, (1 - core) * rows + at])

        q_four = projected[:, :half_width].reshape(CORES * rows, -1, HEAD_DIM)
        both = projected[:, half_width:]
        held = jnp.concatenate([both] + [to_part(both, hop) for hop in range(1, parts)])
        k_four = held[:, :half_width].reshape(held.shape[0], -1, HEAD_DIM)
        v_four = held[:, half_width:].reshape(held.shape[0], -1, HEAD_DIM)
        k_pos = jnp.concatenate([positions((part - hop) % parts) for hop in range(parts)])
        soft_full = spread_softmax(q_four, k_four, positions(part), k_pos, prefix_len)
        context = jnp.einsum("hqk,khd->qhd", soft_full.astype(BF), v_four, preferred_element_type=F32)
        context = context.reshape(CORES * rows, half_width).astype(BF)

    if square:
        context = after(context, fc1_ends)

    def own_sum(left_side, product):
        away = swap(product(left_side[rows:]).astype(BF))
        return product(left_side[:rows]) + away.astype(F32)

    middle = hidden_f + (own_sum(context, lambda v: dot(v, out_full)) + bias_out)
    normed_two_own = normalize(middle, gain_two, shift_two).astype(BF)
    normed_two = jnp.concatenate([normed_two_own, swap(normed_two_own)])
    grads_mine = after(grads_mine, normed_two)
    if square:
        normed_two = after(normed_two, (fc2_low, fc2_high))
    pre_act = dot(normed_two, fc1_full) + bias_up
    below = 0.5 * (1.0 + lax.erf(pre_act * math.sqrt(0.5)))
    density = jnp.exp(-0.5 * pre_act * pre_act) * (1.0 / math.sqrt(2.0 * math.pi))
    activated = (pre_act * below).astype(BF)
    slope = (below + pre_act * density).astype(BF)

    grad_rows = grads_mine.astype(F32)
    grad_both = jnp.concatenate([grads_mine, swap(grads_mine)])
    down_bias_grad = jnp.sum(grad_rows, axis=0)

    class Reduction:
        def __init__(self, left_side, right_side, barrier=()):
            self.sides = (left_side, right_side)
            self.cut = right_side.shape[1] // chips
            to_x = grad_block(left_side, right_side, (3, 1), 1)
            to_y = grad_block(left_side, right_side, (3, 2), 0)
            self.from_x = plane(to_x, 1)
            self.from_y = plane(to_y, 2)
            right_side = after(right_side, (to_x, to_y, *barrier))
            self.near = [grad_block(left_side, right_side, (1,), 0), grad_block(left_side, right_side, (2,), 1)]

        def second(self, barrier=()):
            from_x, from_y, *_ = lax.optimization_barrier((self.from_x, self.from_y, *barrier))
            self.sent = [self.near[0] + from_y[:, : self.cut], self.near[1] + from_x[:, : self.cut]]
            self.x_low = plane(self.sent[0], 1)
            self.y_high = plane(self.sent[1], 2)

        def third(self, barrier=()):
            x_low, y_high, *_ = lax.optimization_barrier((self.x_low, self.y_high, *barrier))
            low_part = grad_block(*self.sides, (0,), 0).astype(F32) + x_low.astype(F32)
            high_part = grad_block(*self.sides, (0,), 1).astype(F32) + y_high.astype(F32)
            low_part = low_part + self.from_y[:, self.cut :].astype(F32)
            high_part = high_part + self.from_x[:, self.cut :].astype(F32)
            self.mine = jnp.concatenate([low_part.astype(BF), high_part.astype(BF)])
            return sum_shards(self.mine)

    if square:
        fc2_red = Reduction(activated, after(grad_both, (fc2_low, fc2_high)))
    d_pre = (times_rows(grad_both, fc2_full) * slope.astype(F32)).astype(BF)
    up_bias_grad = jnp.sum(d_pre, axis=0, dtype=F32)
    if square:
        fc2_red.second()
        d_pre = after(d_pre, fc2_red.sent)
        fc1_red = Reduction(normed_two, d_pre, (fc2_red.x_low, fc2_red.y_high))
        activated = after(activated, fc1_red.near)
    result_own = middle + (own_sum(activated, lambda v: dot(v, fc2_full)) + bias_down)
    result = tokens_out(result_own.astype(BF))
    d_normed_two = own_sum(d_pre, lambda v: times_rows(v, fc1_full))
    back_two = jax.vjp(normalize, middle, gain_two, shift_two)[1]
    d_middle, gain_two_grad, shift_two_grad = back_two(d_normed_two)
    d_middle = d_middle + grad_rows
    d_attn_own = d_middle.astype(BF)
    out_bias_grad = jnp.sum(d_attn_own, axis=0, dtype=F32)
    d_attn = jnp.concatenate([d_attn_own, swap(d_attn_own)])
    if square:
        fc1_red.second((*fc2_red.sent, result_own))
        out_red = Reduction(context, d_attn)
    d_context = times_rows(d_attn, out_full).astype(BF)
    if square:
        d_context = after(d_context, fc1_red.sent)
    if parts == 1:
        d_queries, d_keys, d_values = attend_backward(projected, d_context, scalars)
    else:
        d_four = d_context.reshape(CORES * rows, -1, HEAD_DIM)
        d_queries, d_keys, d_values = spread_backward(q_four, k_four, v_four, d_four, soft_full)
        d_queries = d_queries.reshape(CORES * rows, half_width).astype(BF)
        d_held = jnp.concatenate([d_keys, d_values], axis=1).reshape(parts, CORES * rows, width)
        d_both = d_held[0]
        for hop in range(1, parts):
            d_both = d_both + to_part(d_held[hop].astype(BF), parts - hop).astype(F32)
        d_both = d_both.astype(BF)
        d_keys, d_values = d_both[:, :half_width], d_both[:, half_width:]
    d_projected = jnp.concatenate([d_queries, d_keys, d_values], axis=1)
    if square:
        fc2_part = fc2_red.third()
        d_projected = after(d_projected, (fc2_red.mine, result))
        qkv_red = Reduction(normed_one, d_projected)
        out_red.second()
        d_projected = after(d_projected, qkv_red.near)
        fc1_part = fc1_red.third((*qkv_red.near, d_projected))
        qkv_red.second((fc1_red.mine, *out_red.sent))
    query_bias_grad = jnp.sum(d_projected[:, :half_width], axis=0, dtype=F32)
    value_bias_grad = jnp.sum(d_projected[:, width:], axis=0, dtype=F32)
    d_normed_one = own_sum(d_projected, lambda v: times_rows(v, qkv_full))
    back_one = jax.vjp(normalize, hidden_f, gain_one, shift_one)[1]
    d_inputs, gain_one_grad, shift_one_grad = back_one(d_normed_one)
    grad_in_own = (d_middle + d_inputs).astype(BF)
    grad_in = tokens_out(grad_in_own)

    def half_slot(value):
        value = value.reshape(shards, 1, -1)
        mask = lax.broadcasted_iota(jnp.int32, (1, CORES, 1), 1) == core
        return jnp.where(mask, value, 0.0).reshape(shards, -1)

    def full_slot(value):
        return value.reshape(shards, -1)

    packed = jnp.concatenate(
        [
            full_slot(gain_one_grad),
            full_slot(shift_one_grad),
            half_slot(query_bias_grad),
            half_slot(value_bias_grad),
            full_slot(out_bias_grad),
            full_slot(gain_two_grad),
            full_slot(shift_two_grad),
            full_slot(down_bias_grad),
            half_slot(up_bias_grad),
        ],
        axis=1,
    )
    def sum_plane(values, bits):
        for bit in bits:
            values = values + plane(values, 1 << bit)
        return values

    def sum_line(values):
        total = lax.dynamic_index_in_dim(values, shard, 0, False)
        for hop in range(1, shards):
            total = total + along(lax.dynamic_index_in_dim(values, (shard + hop) % shards, 0, False), hop)
        return total

    packed = packed + swap(packed)
    if square:
        out_part = out_red.third((*qkv_red.sent, grad_in))
        fc2_first = spread_first(after(fc2_part, (qkv_red.sent, out_red.mine)))
        qkv_part = qkv_red.third()
        packed = sum_plane(packed, [0])
        fc1_first = spread_first(after(fc1_part, (fc2_first[1:], qkv_red.mine, packed)))
        fc2_pair = spread_second(*fc2_first)
        packed = sum_plane(packed, [1])
        out_first = spread_first(after(out_part, (fc1_first[1:], fc2_pair[0], packed)))
        summed = sum_line(after(packed, qkv_part))
        fc1_pair = spread_second(*fc1_first)
        fc2_weight_grad = spread_last(*fc2_pair, None)
        fc1_weight_grad = spread_last(*fc1_pair, fc1_chunk)
        out_pair = spread_second(*out_first)
        qkv_first = spread_first(after(qkv_part, (out_pair[0], fc1_pair[0], fc2_weight_grad)))
        out_weight_grad = spread_last(*out_pair, None)
        qkv_own, qkv_other = spread_second(*after(qkv_first, (fc1_weight_grad, out_pair[1])))
        qkv_weight_grad = spread_last(qkv_own, after(qkv_other, out_weight_grad), qkv_chunk)
    else:
        summed = sum_line(sum_plane(packed, range(chips.bit_length() - 1)))
        fc2_weight_grad = spread_any(sum_any(activated, grad_both), None)
        fc1_weight_grad = spread_any(sum_any(normed_two, d_pre), fc1_chunk)
        out_weight_grad = spread_any(sum_any(context, d_attn), None)
        qkv_weight_grad = spread_any(sum_any(normed_one, d_projected), qkv_chunk)
    sums = [summed[edges[i] : edges[i + 1]] for i in range(len(vectors))]
    return (
        result,
        grad_in,
        sums[0],
        sums[1],
        qkv_weight_grad,
        sums[2],
        sums[3],
        out_weight_grad,
        sums[4],
        sums[5],
        sums[6],
        fc1_weight_grad,
        sums[8],
        fc2_weight_grad,
        sums[7],
    )


def solution(mesh):
    shards = mesh.shape["shard"]
    chips = mesh.shape["rep"] // CORES
    inner = Mesh(mesh.devices.reshape(chips, CORES, shards), ALL)
    token_spec = P(None, ALL, None)
    args = [token_spec, P(None, ("ch", "co"))]
    for dims in (1, 1, 2, 1, 1, 2, 1, 1, 1, 2, 1, 2, 1):
        args.append(P("sh", None) if dims == 2 else P("sh"))
    args.append(token_spec)
    outs = [token_spec, token_spec]
    for dims in (1, 1, 2, 1, 1, 2, 1, 1, 1, 2, 1, 2, 1):
        outs.append(P("sh", None) if dims == 2 else P("sh"))

    def run(*values):
        return local(*values, chips=chips, shards=shards)

    return jax.shard_map(run, mesh=inner, in_specs=tuple(args), out_specs=tuple(outs), check_vma=False)
```

```python
import math

import jax
import jax.numpy as jnp
import numpy as np
from jax import lax
from jax.experimental import pallas as pl
from jax.experimental.pallas import tpu as pltpu
from jax.sharding import Mesh
from jax.sharding import PartitionSpec as P

HEADS = 16
HEAD_DIM = 128
CORES = 2
EPSILON = 1e-05
MASKED = -1e30
SCALE = 1.0 / math.sqrt(HEAD_DIM)
ALL = ("ch", "co", "sh")
BF = jnp.bfloat16
F32 = jnp.float32


def normalize(values, gain_vec, shift_vec):
    centred = values - jnp.mean(values, axis=-1, keepdims=True)
    spread = jnp.mean(centred * centred, axis=-1, keepdims=True)
    return centred * lax.rsqrt(spread + EPSILON) * gain_vec + shift_vec


def dot(left_side, right_side):
    return jnp.dot(left_side, right_side, preferred_element_type=F32)


def cross_rows(left_side, right_side):
    return lax.dot_general(left_side, right_side, (((0,), (0,)), ((), ())), preferred_element_type=F32)


def times_rows(left_side, right_side):
    return lax.dot_general(left_side, right_side, (((1,), (1,)), ((), ())), preferred_element_type=F32)


def after(value, other):
    return lax.optimization_barrier((value, other))[0]


def place(sources, steps, dest_rows, dest_cols, block, out_shape, out_dtype, offset=None):
    count = len(steps)
    spans = []
    table = []
    for which in range(len(sources)):
        mine = [i for i, step in enumerate(steps) if step[0] == which]
        first, last = mine[0], mine[-1]
        spans.append((first, last + 1))
        hold = [steps[min(max(i, first), last)] for i in range(count)]
        table.append([step[1] for step in hold])
        table.append([step[2] for step in hold])
    fixed = jnp.asarray(np.array(table, np.int32))
    if offset is not None:
        mask = lax.broadcasted_iota(jnp.int32, (fixed.shape[0], 1), 0)
        fixed = fixed + jnp.where(mask == 0, offset[0], jnp.where(mask == 1, offset[1], 0))
    table = jnp.concatenate(
        [fixed, dest_rows.astype(jnp.int32)[None], dest_cols.astype(jnp.int32)[None]]
    )
    last_row = 2 * len(sources)

    def body(table_ref, *refs):
        step = pl.program_id(0)
        out_ref = refs[-1]
        for which, (first, stop) in enumerate(spans):

            @pl.when((step >= first) & (step < stop))
            def _():
                out_ref[...] = refs[which][...].astype(out_dtype)

    def in_map(which):
        return lambda i, table_ref: (table_ref[2 * which, i], table_ref[2 * which + 1, i])

    return pl.pallas_call(
        body,
        grid_spec=pltpu.PrefetchScalarGridSpec(
            num_scalar_prefetch=1,
            grid=(count,),
            in_specs=[pl.BlockSpec(block, in_map(which)) for which in range(len(sources))],
            out_specs=pl.BlockSpec(block, lambda i, table_ref: (table_ref[last_row, i], table_ref[last_row + 1, i])),
        ),
        out_shape=jax.ShapeDtypeStruct(out_shape, out_dtype),
    )(table, *sources)


def head_parts(scal_ref, q_ref, k_ref, block, rows):
    half = 2 * rows
    core = scal_ref[0]
    prefix = scal_ref[1]
    side = block // 2
    offsets = [pl.multiple_of(core * half, half), pl.multiple_of((1 - core) * half, half)]
    q_off = pl.multiple_of(offsets[side] + (block % 2) * rows, rows)
    queries = q_ref[pl.ds(q_off, rows), :]
    chunks = [(offsets[0], half, 0)]
    if side == 1:
        chunks.append((offsets[1], (block - 1) * rows, half))
    scores = []
    for k_off, count, first in chunks:
        raw = lax.dot_general(
            queries, k_ref[pl.ds(k_off, count), :], (((1,), (1,)), ((), ())), preferred_element_type=F32
        )
        raw = raw * SCALE
        if first + count > block * rows:
            q_pos = block * rows + lax.broadcasted_iota(jnp.int32, raw.shape, 0)
            k_pos = first + lax.broadcasted_iota(jnp.int32, raw.shape, 1)
            raw = jnp.where((k_pos <= q_pos) | (k_pos < prefix), raw, MASKED)
        scores.append(raw)
    top = scores[0].max(axis=-1, keepdims=True)
    for raw in scores[1:]:
        top = jnp.maximum(top, raw.max(axis=-1, keepdims=True))
    terms = [jnp.exp(raw - top) for raw in scores]
    total = terms[0].sum(axis=-1, keepdims=True)
    for term in terms[1:]:
        total = total + term.sum(axis=-1, keepdims=True)
    inverse = 1.0 / total
    return q_off, queries, [(k_off, count, term * inverse) for (k_off, count, _), term in zip(chunks, terms)]


def attend_forward_body(scal_ref, q_ref, k_ref, v_ref, out_ref):
    rows = q_ref.shape[0] // 4
    for block in range(4):
        q_off, _, parts = head_parts(scal_ref, q_ref, k_ref, block, rows)
        total = None
        for k_off, count, soft in parts:
            term = jnp.dot(soft.astype(BF), v_ref[pl.ds(k_off, count), :], preferred_element_type=F32)
            total = term if total is None else total + term
        out_ref[pl.ds(q_off, rows), :] = total.astype(BF)


def attend_backward_body(scal_ref, q_ref, k_ref, v_ref, d_ref, dq_ref, dk_ref, dv_ref, dk_acc, dv_acc):
    rows = q_ref.shape[0] // 4
    dk_acc[...] = jnp.zeros_like(dk_acc)
    dv_acc[...] = jnp.zeros_like(dv_acc)
    for block in range(4):
        q_off, queries, parts = head_parts(scal_ref, q_ref, k_ref, block, rows)
        d_out = d_ref[pl.ds(q_off, rows), :]
        d_softs = []
        row_sum = None
        for k_off, count, soft in parts:
            dv_acc[pl.ds(k_off, count), :] += lax.dot_general(
                soft.astype(BF), d_out, (((0,), (0,)), ((), ())), preferred_element_type=F32
            )
            d_soft = lax.dot_general(
                d_out, v_ref[pl.ds(k_off, count), :], (((1,), (1,)), ((), ())), preferred_element_type=F32
            )
            d_softs.append(d_soft)
            term = jnp.sum(soft * d_soft, axis=-1, keepdims=True)
            row_sum = term if row_sum is None else row_sum + term
        d_queries = None
        for (k_off, count, soft), d_soft in zip(parts, d_softs):
            d_scores = (soft * (d_soft - row_sum) * SCALE).astype(BF)
            term = jnp.dot(d_scores, k_ref[pl.ds(k_off, count), :], preferred_element_type=F32)
            d_queries = term if d_queries is None else d_queries + term
            dk_acc[pl.ds(k_off, count), :] += lax.dot_general(
                d_scores, queries, (((0,), (0,)), ((), ())), preferred_element_type=F32
            )
        dq_ref[pl.ds(q_off, rows), :] = d_queries.astype(BF)
    dk_ref[...] = dk_acc[...].astype(BF)
    dv_ref[...] = dv_acc[...].astype(BF)


def head_specs(rows, heads):
    return [pl.BlockSpec((rows, HEAD_DIM), lambda h, scal_ref, at=at: (0, at * heads + h)) for at in range(3)]


def attend_forward(projected, scalars):
    rows, width = projected.shape
    heads = width // (3 * HEAD_DIM)
    return pl.pallas_call(
        attend_forward_body,
        grid_spec=pltpu.PrefetchScalarGridSpec(
            num_scalar_prefetch=1,
            grid=(heads,),
            in_specs=head_specs(rows, heads),
            out_specs=head_specs(rows, heads)[0],
        ),
        out_shape=jax.ShapeDtypeStruct((rows, width // 3), BF),
    )(scalars, projected, projected, projected)


def attend_backward(projected, d_context, scalars):
    rows, width = projected.shape
    heads = width // (3 * HEAD_DIM)
    one = head_specs(rows, heads)[0]
    return pl.pallas_call(
        attend_backward_body,
        grid_spec=pltpu.PrefetchScalarGridSpec(
            num_scalar_prefetch=1,
            grid=(heads,),
            in_specs=head_specs(rows, heads) + [one],
            out_specs=[one, one, one],
            scratch_shapes=[pltpu.VMEM((rows, HEAD_DIM), F32), pltpu.VMEM((rows, HEAD_DIM), F32)],
        ),
        out_shape=[jax.ShapeDtypeStruct((rows, width // 3), BF)] * 3,
    )(scalars, projected, projected, projected, d_context)


def spread_softmax(queries, keys, q_pos, k_pos, prefix):
    raw = jnp.einsum("qhd,khd->hqk", queries, keys, preferred_element_type=F32) * SCALE
    visible = (k_pos[None, :] <= q_pos[:, None]) | (k_pos[None, :] < prefix)
    raw = jnp.where(visible[None], raw, MASKED)
    terms = jnp.exp(raw - jnp.max(raw, axis=-1, keepdims=True))
    return terms / jnp.sum(terms, axis=-1, keepdims=True)


def spread_backward(queries, keys, values, d_context, soft):
    d_values = jnp.einsum("hqk,qhd->khd", soft.astype(BF), d_context, preferred_element_type=F32)
    d_soft = jnp.einsum("qhd,khd->hqk", d_context, values, preferred_element_type=F32)
    d_scores = (soft * (d_soft - jnp.sum(soft * d_soft, axis=-1, keepdims=True)) * SCALE).astype(BF)
    d_queries = jnp.einsum("hqk,khd->qhd", d_scores, keys, preferred_element_type=F32)
    d_keys = jnp.einsum("hqk,qhd->khd", d_scores, queries, preferred_element_type=F32)
    return d_queries, d_keys, d_values


def local(
    hidden_in,
    prefix,
    ln1_gain,
    ln1_bias,
    qkv_weight,
    q_bias,
    v_bias,
    out_weight,
    out_bias,
    ln2_gain,
    ln2_bias,
    fc1_weight,
    fc1_bias,
    fc2_weight,
    fc2_bias,
    grad_out,
    *,
    chips,
    shards,
):
    micro_count, tok_rows, width = hidden_in.shape
    ff_units = fc1_weight.shape[1]
    piece_rows = width // shards
    rows = micro_count * tok_rows
    parts = shards // (micro_count * CORES)
    ch = lax.axis_index("ch")
    core = lax.axis_index("co")
    shard = lax.axis_index("sh")
    sequence = shard // parts
    micro = sequence // CORES

    def along(value, hop):
        return lax.ppermute(value, "sh", [(i, (i + hop) % shards) for i in range(shards)])

    def plane(value, bit):
        return lax.ppermute(value, "ch", [(i, i ^ bit) for i in range(chips)])

    def swap(value):
        return lax.ppermute(value, "co", [(0, 1), (1, 0)])

    def token_pairs(turn):
        pairs = []
        for c in range(chips):
            for o in range(CORES):
                for s in range(shards):
                    m = (turn + s) % 2
                    slot = s // 2
                    z = (m * CORES + o) * parts + slot // 2
                    pairs.append(((c * CORES + o) * shards + s, (c * CORES + slot % 2) * shards + z))
        return pairs

    def tokens_in(value, barrier=()):
        got = [
            lax.ppermute(lax.dynamic_index_in_dim(value, (turn + shard) % 2, 0, False), ALL, token_pairs(turn))
            for turn in (0, 1)
        ]
        got = lax.optimization_barrier((*got, *barrier))
        even = micro % 2 == 0
        return jnp.concatenate([jnp.where(even, got[0], got[1]), jnp.where(even, got[1], got[0])])

    def tokens_out(value):
        value = value.reshape(2, tok_rows, width)
        got = [
            lax.ppermute(
                lax.dynamic_index_in_dim(value, (turn + micro) % 2, 0, False),
                ALL,
                [(b, a) for a, b in token_pairs(turn)],
            )
            for turn in (0, 1)
        ]
        even = shard % 2 == 0
        return jnp.stack([jnp.where(even, got[0], got[1]), jnp.where(even, got[1], got[0])])

    def gather_shards(piece):
        return lax.all_gather(piece, "sh")

    def others_of(held):
        return jnp.concatenate(
            [lax.dynamic_index_in_dim(held, (shard - hop) % shards, 0, False) for hop in range(1, shards)]
        )

    def spread_others(others, barrier=()):
        from_x = plane(others, 1)
        from_y = plane(others, 2)
        from_x, from_y, *_ = lax.optimization_barrier((from_x, from_y, *barrier))
        tall = (shards - 1, 2, others.shape[0] // (2 * (shards - 1)), others.shape[1])
        low_cut = from_x.reshape(tall)[:, 0].reshape(-1, tall[3])
        high_cut = from_y.reshape(tall)[:, 1].reshape(-1, tall[3])
        return from_x, from_y, low_cut, high_cut

    def whole_weight(source, offset, col_step, height, others, from_x, from_y, low_part, high_part):
        cut = others.shape[1]
        steps, hops, flips, cols, halves = [], [], [], [], []
        for half in range(2):
            for col in range(chips):
                steps.append((0, half, col * col_step))
                hops.append(0), flips.append(-1), cols.append(col), halves.append(half)
        for which, flip in ((1, 0), (2, 1), (3, 2)):
            for hop in range(1, shards):
                for half in range(2):
                    steps.append((which, 2 * (hop - 1) + half, 0))
                    hops.append(hop), flips.append(flip), cols.append(0), halves.append(half)
        for which, half in ((4, 0), (5, 1)):
            for hop in range(1, shards):
                steps.append((which, hop - 1, 0))
                hops.append(hop), flips.append(3), cols.append(0), halves.append(half)
        hops, flips, cols, halves = (np.array(v, np.int32) for v in (hops, flips, cols, halves))
        return place(
            [source, others, from_x, from_y, low_part, high_part],
            steps,
            2 * ((shard - hops) % shards) + halves,
            jnp.where(flips < 0, cols, ch ^ np.maximum(flips, 0)),
            (height // 2, cut),
            (shards * height, chips * cut),
            BF,
            offset,
        )

    def whole_weight_any(piece):
        everything = lax.all_gather(lax.all_gather(piece, "sh"), "ch")
        return everything.transpose(1, 2, 0, 3).reshape(-1, chips * piece.shape[1])

    def grad_block(left_side, right_side, flips, half):
        cut = right_side.shape[1] // chips
        blocks = [lax.dynamic_slice_in_dim(right_side, (ch ^ flip) * cut, cut, 1) for flip in flips]
        block = blocks[0] if len(flips) == 1 else jnp.concatenate(blocks, axis=1)
        width_half = left_side.shape[1] // 2
        return cross_rows(left_side[:, half * width_half : (half + 1) * width_half], block).astype(BF)

    def sum_shards(mine):
        return lax.psum_scatter(mine, "sh", scatter_dimension=0, tiled=True)

    def sum_any(left_side, right_side):
        cut = right_side.shape[1] // chips
        grads = cross_rows(left_side, right_side).astype(BF).reshape(-1, chips, cut).transpose(1, 0, 2)
        return sum_shards(lax.psum_scatter(grads, "ch", scatter_dimension=0))

    def spread_any(mine, chunk):
        height = mine.shape[0]
        own = lax.all_gather(mine, "ch", axis=1, tiled=True)
        other = swap(own)
        pair = [jnp.where(core == 0, own, other), jnp.where(core == 0, other, own)]
        if chunk is None:
            return jnp.concatenate(pair).astype(F32)
        wide = jnp.stack([member.reshape(height, -1, chunk) for member in pair], axis=2)
        return wide.reshape(height, -1).astype(F32)

    def spread_first(mine):
        from_x = plane(mine, 1)
        from_y = plane(mine, 2)
        return mine, from_x, from_y

    def spread_second(mine, from_x, from_y):
        middle_row = mine.shape[0] // 2
        low_part = plane(from_x[:middle_row], 2)
        high_part = plane(from_y[middle_row:], 1)
        own = jnp.concatenate([mine, from_x, from_y, low_part, high_part])
        return own, swap(own)

    def spread_last(own, other, chunk):
        height, cut = own.shape[0] // 4, own.shape[1]
        block_cols = cut if chunk is None else chunk
        per = cut // block_cols
        steps, flips, cores, inner = [], [], [], []
        for source in range(2):
            for flip in range(4):
                for at in range(per):
                    steps.append((source, flip, at))
                    flips.append(flip), cores.append(source), inner.append(at)
        flips, cores, inner = (np.array(v, np.int32) for v in (flips, cores, inner))
        side = core ^ cores
        cols = (ch ^ flips) * per + inner
        if chunk is None:
            dest_rows, dest_cols, shape = side, cols, (2 * height, chips * cut)
        else:
            dest_rows, dest_cols, shape = 0 * side, cols * 2 + side, (height, 2 * chips * cut)
        return place([own, other], steps, dest_rows, dest_cols, (height, block_cols), shape, F32)

    def take(value, axis):
        return lax.dynamic_index_in_dim(value, core, axis, False)

    qkv_chunk = width // (shards * CORES)
    fc1_chunk = ff_units // (shards * CORES)

    def col_chunks(value, chunk, first, count):
        cuts = [lax.dynamic_slice_in_dim(value, ((first + i) * CORES + core) * chunk, chunk, 1) for i in range(count)]
        return cuts[0] if count == 1 else jnp.concatenate(cuts, axis=1)

    def col_piece(value, chunk):
        per = value.shape[1] // (CORES * chips * chunk)
        return col_chunks(value, chunk, ch * per, per)

    def row_piece(value):
        height, cut = value.shape[0] // CORES, value.shape[1] // chips
        return lax.dynamic_slice(value, (core * height, ch * cut), (height, cut))

    qkv_piece = col_piece(qkv_weight, qkv_chunk)
    fc1_piece = col_piece(fc1_weight, fc1_chunk)
    out_piece = row_piece(out_weight)
    fc2_piece = row_piece(fc2_weight)

    vectors = [ln1_gain, ln1_bias, q_bias, v_bias, out_bias, ln2_gain, ln2_bias, fc2_bias, fc1_bias]
    lengths = [v.shape[0] for v in vectors]
    edges = np.cumsum([0] + lengths)
    square = chips == 4
    small = jnp.concatenate(vectors)
    ring = [small] + [along(small, hop) for hop in range(shards - 1, 0, -1)]
    qkv_piece, tokens, *ring = lax.optimization_barrier((qkv_piece, tokens_in(hidden_in), *ring))
    gathered = lax.dynamic_slice_in_dim(jnp.stack(ring + ring), (shards - shard) % shards, shards, 0)
    vec = [gathered[:, edges[i] : edges[i + 1]].astype(F32) for i in range(len(vectors))]
    gain_one, shift_one, _, _, bias_out, gain_two, shift_two, bias_down, _ = [v.reshape(-1) for v in vec]
    bias_query, bias_value, bias_up = [
        take(vec[i].reshape(shards, CORES, -1), 1).reshape(-1) for i in (2, 3, 8)
    ]

    prefix_pair = [jnp.where(core == 0, a, b) for a, b in ((prefix, swap(prefix)), (swap(prefix), prefix))]
    prefix_len = jnp.concatenate(prefix_pair, axis=1).reshape(-1)[sequence]

    if square:
        qkv_others = others_of(gather_shards(qkv_piece))
        out_got = gather_shards(out_piece)
        fc1_got = gather_shards(fc1_piece)
        fc2_got = gather_shards(after(fc2_piece, out_got))
        qkv_x, qkv_y, qkv_low, qkv_high = spread_others(qkv_others)
        qkv_ends = plane(qkv_low, 2), plane(qkv_high, 1)
        out_others = others_of(after(out_got, (qkv_low, qkv_high)))
        out_x, out_y, out_low, out_high = spread_others(out_others)

    hidden_f = tokens.astype(F32)
    normed_own = normalize(hidden_f, gain_one, shift_one).astype(BF)
    normed_one = jnp.concatenate([normed_own, swap(normed_own)])
    none = jnp.zeros((), jnp.int32)
    if square:
        qkv_mine = col_chunks(qkv_weight, qkv_chunk, 0, 3 * shards)
        qkv_full = whole_weight(
            qkv_mine, None, 1, piece_rows, qkv_others, qkv_x, qkv_y, *qkv_ends
        )
        out_full = whole_weight(
            out_weight, (2 * core, none), 1, piece_rows // 2, out_others, out_x, out_y, plane(out_low, 2), plane(out_high, 1)
        )
    else:
        qkv_full, out_full, fc1_full, fc2_full = [
            whole_weight_any(piece) for piece in (qkv_piece, out_piece, fc1_piece, fc2_piece)
        ]
        grads_mine = tokens_in(grad_out)

    half_width = width // CORES
    projected = dot(normed_one, qkv_full) + jnp.concatenate([bias_query, jnp.zeros_like(bias_query), bias_value])
    projected = projected.astype(BF)
    if square:
        fc1_others = others_of(after(fc1_got, (projected, out_low, out_high)))
    scalars = jnp.stack([core.astype(jnp.int32), prefix_len.astype(jnp.int32)])
    if parts == 1:
        context = attend_forward(projected, scalars)
    else:
        part = shard % parts

        def to_part(value, hop):
            pairs = [(i, i // parts * parts + (i % parts + hop) % parts) for i in range(shards)]
            return lax.ppermute(value, "sh", pairs)

        def positions(which):
            at = jnp.arange(rows)
            return which * CORES * rows + jnp.concatenate([core * rows + at, (1 - core) * rows + at])

        q_four = projected[:, :half_width].reshape(CORES * rows, -1, HEAD_DIM)
        both = projected[:, half_width:]
        held = jnp.concatenate([both] + [to_part(both, hop) for hop in range(1, parts)])
        k_four = held[:, :half_width].reshape(held.shape[0], -1, HEAD_DIM)
        v_four = held[:, half_width:].reshape(held.shape[0], -1, HEAD_DIM)
        k_pos = jnp.concatenate([positions((part - hop) % parts) for hop in range(parts)])
        soft_full = spread_softmax(q_four, k_four, positions(part), k_pos, prefix_len)
        context = jnp.einsum("hqk,khd->qhd", soft_full.astype(BF), v_four, preferred_element_type=F32)
        context = context.reshape(CORES * rows, half_width).astype(BF)

    if square:
        fc1_x, fc1_y, fc1_low, fc1_high = spread_others(fc1_others, (context,))
        fc1_ends = plane(fc1_low, 2), plane(fc1_high, 1)
        fc2_others = others_of(after(fc2_got, fc1_ends))
        fc2_x, fc2_y, fc2_low, fc2_high = spread_others(fc2_others)
        fc1_full = whole_weight(
            fc1_weight, (none, core), 2, piece_rows, fc1_others, fc1_x, fc1_y, *fc1_ends
        )
        fc2_full = whole_weight(
            fc2_weight,
            (2 * core, none),
            1,
            fc2_weight.shape[0] // 2,
            fc2_others,
            fc2_x,
            fc2_y,
            plane(fc2_low, 2),
            plane(fc2_high, 1),
        )
        grads_mine = tokens_in(after(grad_out, fc2_others))
    grads_mine = lax.optimization_barrier(grads_mine)

    def own_sum(left_side, product):
        away = swap(product(left_side[rows:]).astype(BF))
        return product(left_side[:rows]) + away.astype(F32)

    middle = hidden_f + (own_sum(context, lambda v: dot(v, out_full)) + bias_out)
    if square:
        middle = after(middle, (fc1_low, fc1_high, fc2_got))
    normed_two_own = normalize(middle, gain_two, shift_two).astype(BF)
    normed_two = jnp.concatenate([normed_two_own, swap(normed_two_own)])
    grads_mine = after(grads_mine, normed_two)
    pre_act = dot(normed_two, fc1_full) + bias_up
    below = 0.5 * (1.0 + lax.erf(pre_act * math.sqrt(0.5)))
    density = jnp.exp(-0.5 * pre_act * pre_act) * (1.0 / math.sqrt(2.0 * math.pi))
    activated = (pre_act * below).astype(BF)
    slope = (below + pre_act * density).astype(BF)

    grad_rows = grads_mine.astype(F32)
    grad_both = jnp.concatenate([grads_mine, swap(grads_mine)])
    down_bias_grad = jnp.sum(grad_rows, axis=0)

    class Reduction:
        def __init__(self, left_side, right_side, barrier=()):
            self.sides = (left_side, right_side)
            self.cut = right_side.shape[1] // chips
            to_x = grad_block(left_side, right_side, (3, 1), 1)
            to_y = grad_block(left_side, right_side, (3, 2), 0)
            self.from_x = plane(to_x, 1)
            self.from_y = plane(to_y, 2)
            right_side = after(right_side, (to_x, to_y, *barrier))
            self.near = [grad_block(left_side, right_side, (1,), 0), grad_block(left_side, right_side, (2,), 1)]

        def second(self, barrier=()):
            from_x, from_y, *_ = lax.optimization_barrier((self.from_x, self.from_y, *barrier))
            self.sent = [self.near[0] + from_y[:, : self.cut], self.near[1] + from_x[:, : self.cut]]
            self.x_low = plane(self.sent[0], 1)
            self.y_high = plane(self.sent[1], 2)

        def third(self, barrier=()):
            x_low, y_high, *_ = lax.optimization_barrier((self.x_low, self.y_high, *barrier))
            low_part = grad_block(*self.sides, (0,), 0).astype(F32) + x_low.astype(F32)
            high_part = grad_block(*self.sides, (0,), 1).astype(F32) + y_high.astype(F32)
            low_part = low_part + self.from_y[:, self.cut :].astype(F32)
            high_part = high_part + self.from_x[:, self.cut :].astype(F32)
            self.mine = jnp.concatenate([low_part.astype(BF), high_part.astype(BF)])
            return sum_shards(self.mine)

    if square:
        fc2_red = Reduction(activated, after(grad_both, (fc2_low, fc2_high)))
    d_pre = (times_rows(grad_both, fc2_full) * slope.astype(F32)).astype(BF)
    up_bias_grad = jnp.sum(d_pre, axis=0, dtype=F32)
    if square:
        fc2_red.second()
        d_pre = after(d_pre, fc2_red.sent)
        fc1_red = Reduction(normed_two, d_pre, (fc2_red.x_low, fc2_red.y_high))
        activated = after(activated, fc1_red.near)
    result_own = middle + (own_sum(activated, lambda v: dot(v, fc2_full)) + bias_down)
    result = tokens_out(result_own.astype(BF))
    d_normed_two = own_sum(d_pre, lambda v: times_rows(v, fc1_full))
    back_two = jax.vjp(normalize, middle, gain_two, shift_two)[1]
    d_middle, gain_two_grad, shift_two_grad = back_two(d_normed_two)
    d_middle = d_middle + grad_rows
    d_attn_own = d_middle.astype(BF)
    out_bias_grad = jnp.sum(d_attn_own, axis=0, dtype=F32)
    d_attn = jnp.concatenate([d_attn_own, swap(d_attn_own)])
    if square:
        fc1_red.second((*fc2_red.sent, result_own))
        out_red = Reduction(context, d_attn)
    d_context = times_rows(d_attn, out_full).astype(BF)
    if square:
        d_context = after(d_context, fc1_red.sent)
    if parts == 1:
        d_queries, d_keys, d_values = attend_backward(projected, d_context, scalars)
    else:
        d_four = d_context.reshape(CORES * rows, -1, HEAD_DIM)
        d_queries, d_keys, d_values = spread_backward(q_four, k_four, v_four, d_four, soft_full)
        d_queries = d_queries.reshape(CORES * rows, half_width).astype(BF)
        d_held = jnp.concatenate([d_keys, d_values], axis=1).reshape(parts, CORES * rows, width)
        d_both = d_held[0]
        for hop in range(1, parts):
            d_both = d_both + to_part(d_held[hop].astype(BF), parts - hop).astype(F32)
        d_both = d_both.astype(BF)
        d_keys, d_values = d_both[:, :half_width], d_both[:, half_width:]
    d_projected = jnp.concatenate([d_queries, d_keys, d_values], axis=1)
    if square:
        fc2_part = fc2_red.third()
        d_projected = after(d_projected, fc2_red.mine)
        qkv_red = Reduction(normed_one, d_projected)
        out_red.second()
        d_projected = after(d_projected, qkv_red.near)
        fc1_part = fc1_red.third((*qkv_red.near, d_projected))
        qkv_red.second((fc1_red.mine, *out_red.sent))
    query_bias_grad = jnp.sum(d_projected[:, :half_width], axis=0, dtype=F32)
    value_bias_grad = jnp.sum(d_projected[:, width:], axis=0, dtype=F32)
    d_normed_one = own_sum(d_projected, lambda v: times_rows(v, qkv_full))
    back_one = jax.vjp(normalize, hidden_f, gain_one, shift_one)[1]
    d_inputs, gain_one_grad, shift_one_grad = back_one(d_normed_one)
    grad_in_own = (d_middle + d_inputs).astype(BF)
    grad_in = tokens_out(grad_in_own)

    def half_slot(value):
        value = value.reshape(shards, 1, -1)
        mask = lax.broadcasted_iota(jnp.int32, (1, CORES, 1), 1) == core
        return jnp.where(mask, value, 0.0).reshape(shards, -1)

    def full_slot(value):
        return value.reshape(shards, -1)

    packed = jnp.concatenate(
        [
            full_slot(gain_one_grad),
            full_slot(shift_one_grad),
            half_slot(query_bias_grad),
            half_slot(value_bias_grad),
            full_slot(out_bias_grad),
            full_slot(gain_two_grad),
            full_slot(shift_two_grad),
            full_slot(down_bias_grad),
            half_slot(up_bias_grad),
        ],
        axis=1,
    )
    def sum_plane(values, bits):
        for bit in bits:
            values = values + plane(values, 1 << bit)
        return values

    def sum_line(values):
        total = lax.dynamic_index_in_dim(values, shard, 0, False)
        for hop in range(1, shards):
            total = total + along(lax.dynamic_index_in_dim(values, (shard + hop) % shards, 0, False), hop)
        return total

    packed = packed + swap(packed)
    if square:
        out_part = out_red.third((*qkv_red.sent, result))
        fc2_first = spread_first(after(fc2_part, (qkv_red.sent, out_red.mine)))
        qkv_part = qkv_red.third()
        packed = sum_plane(packed, [0])
        fc1_first = spread_first(after(fc1_part, (fc2_first[1:], qkv_red.mine, packed, grad_in)))
        fc2_pair = spread_second(*fc2_first)
        packed = sum_plane(packed, [1])
        out_first = spread_first(after(out_part, (fc1_first[1:], fc2_pair[0], packed)))
        summed = sum_line(after(packed, qkv_part))
        fc1_pair = spread_second(*fc1_first)
        fc2_weight_grad = spread_last(*fc2_pair, None)
        fc1_weight_grad = spread_last(*fc1_pair, fc1_chunk)
        out_pair = spread_second(*out_first)
        qkv_first = spread_first(after(qkv_part, (out_pair[0], fc1_pair[0], fc2_weight_grad)))
        out_weight_grad = spread_last(*out_pair, None)
        qkv_own, qkv_other = spread_second(*after(qkv_first, (fc1_weight_grad, out_pair[1])))
        qkv_weight_grad = spread_last(qkv_own, after(qkv_other, out_weight_grad), qkv_chunk)
    else:
        summed = sum_line(sum_plane(packed, range(chips.bit_length() - 1)))
        fc2_weight_grad = spread_any(sum_any(activated, grad_both), None)
        fc1_weight_grad = spread_any(sum_any(normed_two, d_pre), fc1_chunk)
        out_weight_grad = spread_any(sum_any(context, d_attn), None)
        qkv_weight_grad = spread_any(sum_any(normed_one, d_projected), qkv_chunk)
    sums = [summed[edges[i] : edges[i + 1]] for i in range(len(vectors))]
    return (
        result,
        grad_in,
        sums[0],
        sums[1],
        qkv_weight_grad,
        sums[2],
        sums[3],
        out_weight_grad,
        sums[4],
        sums[5],
        sums[6],
        fc1_weight_grad,
        sums[8],
        fc2_weight_grad,
        sums[7],
    )


def solution(mesh):
    shards = mesh.shape["shard"]
    chips = mesh.shape["rep"] // CORES
    inner = Mesh(mesh.devices.reshape(chips, CORES, shards), ALL)
    token_spec = P(None, ALL, None)
    args = [token_spec, P(None, ("ch", "co"))]
    for dims in (1, 1, 2, 1, 1, 2, 1, 1, 1, 2, 1, 2, 1):
        args.append(P("sh", None) if dims == 2 else P("sh"))
    args.append(token_spec)
    outs = [token_spec, token_spec]
    for dims in (1, 1, 2, 1, 1, 2, 1, 1, 1, 2, 1, 2, 1):
        outs.append(P("sh", None) if dims == 2 else P("sh"))

    def run(*values):
        return local(*values, chips=chips, shards=shards)

    return jax.shard_map(run, mesh=inner, in_specs=tuple(args), out_specs=tuple(outs), check_vma=False)
```

```python
import math

import jax
import jax.numpy as jnp
import numpy as np
from jax import lax
from jax.experimental import pallas as pl
from jax.experimental.pallas import tpu as pltpu
from jax.sharding import Mesh
from jax.sharding import PartitionSpec as P

HEADS = 16
HEAD_DIM = 128
CORES = 2
EPSILON = 1e-05
MASKED = -1e30
SCALE = 1.0 / math.sqrt(HEAD_DIM)
ALL = ("ch", "co", "sh")
BF = jnp.bfloat16
F32 = jnp.float32


def normalize(values, gain_vec, shift_vec):
    centred = values - jnp.mean(values, axis=-1, keepdims=True)
    spread = jnp.mean(centred * centred, axis=-1, keepdims=True)
    return centred * lax.rsqrt(spread + EPSILON) * gain_vec + shift_vec


def dot(left_side, right_side):
    return jnp.dot(left_side, right_side, preferred_element_type=F32)


def cross_rows(left_side, right_side):
    return lax.dot_general(left_side, right_side, (((0,), (0,)), ((), ())), preferred_element_type=F32)


def times_rows(left_side, right_side):
    return lax.dot_general(left_side, right_side, (((1,), (1,)), ((), ())), preferred_element_type=F32)


def after(value, other):
    return lax.optimization_barrier((value, other))[0]


def place(sources, steps, dest_rows, dest_cols, block, out_shape, out_dtype, offset=None):
    count = len(steps)
    spans = []
    table = []
    for which in range(len(sources)):
        mine = [i for i, step in enumerate(steps) if step[0] == which]
        first, last = mine[0], mine[-1]
        spans.append((first, last + 1))
        hold = [steps[min(max(i, first), last)] for i in range(count)]
        table.append([step[1] for step in hold])
        table.append([step[2] for step in hold])
    fixed = jnp.asarray(np.array(table, np.int32))
    if offset is not None:
        mask = lax.broadcasted_iota(jnp.int32, (fixed.shape[0], 1), 0)
        fixed = fixed + jnp.where(mask == 0, offset[0], jnp.where(mask == 1, offset[1], 0))
    table = jnp.concatenate(
        [fixed, dest_rows.astype(jnp.int32)[None], dest_cols.astype(jnp.int32)[None]]
    )
    last_row = 2 * len(sources)

    def body(table_ref, *refs):
        step = pl.program_id(0)
        out_ref = refs[-1]
        for which, (first, stop) in enumerate(spans):

            @pl.when((step >= first) & (step < stop))
            def _():
                out_ref[...] = refs[which][...].astype(out_dtype)

    def in_map(which):
        return lambda i, table_ref: (table_ref[2 * which, i], table_ref[2 * which + 1, i])

    return pl.pallas_call(
        body,
        grid_spec=pltpu.PrefetchScalarGridSpec(
            num_scalar_prefetch=1,
            grid=(count,),
            in_specs=[pl.BlockSpec(block, in_map(which)) for which in range(len(sources))],
            out_specs=pl.BlockSpec(block, lambda i, table_ref: (table_ref[last_row, i], table_ref[last_row + 1, i])),
        ),
        out_shape=jax.ShapeDtypeStruct(out_shape, out_dtype),
    )(table, *sources)


def head_parts(scal_ref, q_ref, k_ref, block, rows):
    half = 2 * rows
    core = scal_ref[0]
    prefix = scal_ref[1]
    side = block // 2
    offsets = [pl.multiple_of(core * half, half), pl.multiple_of((1 - core) * half, half)]
    q_off = pl.multiple_of(offsets[side] + (block % 2) * rows, rows)
    queries = q_ref[pl.ds(q_off, rows), :]
    chunks = [(offsets[0], half, 0)]
    if side == 1:
        chunks.append((offsets[1], (block - 1) * rows, half))
    scores = []
    for k_off, count, first in chunks:
        raw = lax.dot_general(
            queries, k_ref[pl.ds(k_off, count), :], (((1,), (1,)), ((), ())), preferred_element_type=F32
        )
        raw = raw * SCALE
        if first + count > block * rows:
            q_pos = block * rows + lax.broadcasted_iota(jnp.int32, raw.shape, 0)
            k_pos = first + lax.broadcasted_iota(jnp.int32, raw.shape, 1)
            raw = jnp.where((k_pos <= q_pos) | (k_pos < prefix), raw, MASKED)
        scores.append(raw)
    top = scores[0].max(axis=-1, keepdims=True)
    for raw in scores[1:]:
        top = jnp.maximum(top, raw.max(axis=-1, keepdims=True))
    terms = [jnp.exp(raw - top) for raw in scores]
    total = terms[0].sum(axis=-1, keepdims=True)
    for term in terms[1:]:
        total = total + term.sum(axis=-1, keepdims=True)
    inverse = 1.0 / total
    return q_off, queries, [(k_off, count, term * inverse) for (k_off, count, _), term in zip(chunks, terms)]


def attend_forward_body(scal_ref, q_ref, k_ref, v_ref, out_ref):
    rows = q_ref.shape[0] // 4
    for block in range(4):
        q_off, _, parts = head_parts(scal_ref, q_ref, k_ref, block, rows)
        total = None
        for k_off, count, soft in parts:
            term = jnp.dot(soft.astype(BF), v_ref[pl.ds(k_off, count), :], preferred_element_type=F32)
            total = term if total is None else total + term
        out_ref[pl.ds(q_off, rows), :] = total.astype(BF)


def attend_backward_body(scal_ref, q_ref, k_ref, v_ref, d_ref, dq_ref, dk_ref, dv_ref, dk_acc, dv_acc):
    rows = q_ref.shape[0] // 4
    dk_acc[...] = jnp.zeros_like(dk_acc)
    dv_acc[...] = jnp.zeros_like(dv_acc)
    for block in range(4):
        q_off, queries, parts = head_parts(scal_ref, q_ref, k_ref, block, rows)
        d_out = d_ref[pl.ds(q_off, rows), :]
        d_softs = []
        row_sum = None
        for k_off, count, soft in parts:
            dv_acc[pl.ds(k_off, count), :] += lax.dot_general(
                soft.astype(BF), d_out, (((0,), (0,)), ((), ())), preferred_element_type=F32
            )
            d_soft = lax.dot_general(
                d_out, v_ref[pl.ds(k_off, count), :], (((1,), (1,)), ((), ())), preferred_element_type=F32
            )
            d_softs.append(d_soft)
            term = jnp.sum(soft * d_soft, axis=-1, keepdims=True)
            row_sum = term if row_sum is None else row_sum + term
        d_queries = None
        for (k_off, count, soft), d_soft in zip(parts, d_softs):
            d_scores = (soft * (d_soft - row_sum) * SCALE).astype(BF)
            term = jnp.dot(d_scores, k_ref[pl.ds(k_off, count), :], preferred_element_type=F32)
            d_queries = term if d_queries is None else d_queries + term
            dk_acc[pl.ds(k_off, count), :] += lax.dot_general(
                d_scores, queries, (((0,), (0,)), ((), ())), preferred_element_type=F32
            )
        dq_ref[pl.ds(q_off, rows), :] = d_queries.astype(BF)
    dk_ref[...] = dk_acc[...].astype(BF)
    dv_ref[...] = dv_acc[...].astype(BF)


def head_specs(rows, heads):
    return [pl.BlockSpec((rows, HEAD_DIM), lambda h, scal_ref, at=at: (0, at * heads + h)) for at in range(3)]


def attend_forward(projected, scalars):
    rows, width = projected.shape
    heads = width // (3 * HEAD_DIM)
    return pl.pallas_call(
        attend_forward_body,
        grid_spec=pltpu.PrefetchScalarGridSpec(
            num_scalar_prefetch=1,
            grid=(heads,),
            in_specs=head_specs(rows, heads),
            out_specs=head_specs(rows, heads)[0],
        ),
        out_shape=jax.ShapeDtypeStruct((rows, width // 3), BF),
    )(scalars, projected, projected, projected)


def attend_backward(projected, d_context, scalars):
    rows, width = projected.shape
    heads = width // (3 * HEAD_DIM)
    one = head_specs(rows, heads)[0]
    return pl.pallas_call(
        attend_backward_body,
        grid_spec=pltpu.PrefetchScalarGridSpec(
            num_scalar_prefetch=1,
            grid=(heads,),
            in_specs=head_specs(rows, heads) + [one],
            out_specs=[one, one, one],
            scratch_shapes=[pltpu.VMEM((rows, HEAD_DIM), F32), pltpu.VMEM((rows, HEAD_DIM), F32)],
        ),
        out_shape=[jax.ShapeDtypeStruct((rows, width // 3), BF)] * 3,
    )(scalars, projected, projected, projected, d_context)


def spread_softmax(queries, keys, q_pos, k_pos, prefix):
    raw = jnp.einsum("qhd,khd->hqk", queries, keys, preferred_element_type=F32) * SCALE
    visible = (k_pos[None, :] <= q_pos[:, None]) | (k_pos[None, :] < prefix)
    raw = jnp.where(visible[None], raw, MASKED)
    terms = jnp.exp(raw - jnp.max(raw, axis=-1, keepdims=True))
    return terms / jnp.sum(terms, axis=-1, keepdims=True)


def spread_backward(queries, keys, values, d_context, soft):
    d_values = jnp.einsum("hqk,qhd->khd", soft.astype(BF), d_context, preferred_element_type=F32)
    d_soft = jnp.einsum("qhd,khd->hqk", d_context, values, preferred_element_type=F32)
    d_scores = (soft * (d_soft - jnp.sum(soft * d_soft, axis=-1, keepdims=True)) * SCALE).astype(BF)
    d_queries = jnp.einsum("hqk,khd->qhd", d_scores, keys, preferred_element_type=F32)
    d_keys = jnp.einsum("hqk,qhd->khd", d_scores, queries, preferred_element_type=F32)
    return d_queries, d_keys, d_values


def local(
    hidden_in,
    prefix,
    ln1_gain,
    ln1_bias,
    qkv_weight,
    q_bias,
    v_bias,
    out_weight,
    out_bias,
    ln2_gain,
    ln2_bias,
    fc1_weight,
    fc1_bias,
    fc2_weight,
    fc2_bias,
    grad_out,
    *,
    chips,
    shards,
):
    micro_count, tok_rows, width = hidden_in.shape
    ff_units = fc1_weight.shape[1]
    piece_rows = width // shards
    rows = micro_count * tok_rows
    parts = shards // (micro_count * CORES)
    ch = lax.axis_index("ch")
    core = lax.axis_index("co")
    shard = lax.axis_index("sh")
    sequence = shard // parts
    micro = sequence // CORES

    def along(value, hop):
        return lax.ppermute(value, "sh", [(i, (i + hop) % shards) for i in range(shards)])

    def plane(value, bit):
        return lax.ppermute(value, "ch", [(i, i ^ bit) for i in range(chips)])

    def swap(value):
        return lax.ppermute(value, "co", [(0, 1), (1, 0)])

    def token_pairs(turn):
        pairs = []
        for c in range(chips):
            for o in range(CORES):
                for s in range(shards):
                    m = (turn + s) % 2
                    slot = s // 2
                    z = (m * CORES + o) * parts + slot // 2
                    pairs.append(((c * CORES + o) * shards + s, (c * CORES + slot % 2) * shards + z))
        return pairs

    def tokens_in(value, barrier=()):
        got = [
            lax.ppermute(lax.dynamic_index_in_dim(value, (turn + shard) % 2, 0, False), ALL, token_pairs(turn))
            for turn in (0, 1)
        ]
        got = lax.optimization_barrier((*got, *barrier))
        even = micro % 2 == 0
        return jnp.concatenate([jnp.where(even, got[0], got[1]), jnp.where(even, got[1], got[0])])

    def tokens_out(value):
        value = value.reshape(2, tok_rows, width)
        got = [
            lax.ppermute(
                lax.dynamic_index_in_dim(value, (turn + micro) % 2, 0, False),
                ALL,
                [(b, a) for a, b in token_pairs(turn)],
            )
            for turn in (0, 1)
        ]
        even = shard % 2 == 0
        return jnp.stack([jnp.where(even, got[0], got[1]), jnp.where(even, got[1], got[0])])

    def gather_shards(piece):
        return lax.all_gather(piece, "sh")

    def others_of(held):
        return jnp.concatenate(
            [lax.dynamic_index_in_dim(held, (shard - hop) % shards, 0, False) for hop in range(1, shards)]
        )

    def spread_others(others, barrier=()):
        from_x = plane(others, 1)
        from_y = plane(others, 2)
        from_x, from_y, *_ = lax.optimization_barrier((from_x, from_y, *barrier))
        tall = (shards - 1, 2, others.shape[0] // (2 * (shards - 1)), others.shape[1])
        low_cut = from_x.reshape(tall)[:, 0].reshape(-1, tall[3])
        high_cut = from_y.reshape(tall)[:, 1].reshape(-1, tall[3])
        return from_x, from_y, low_cut, high_cut

    def whole_weight(source, offset, col_step, height, others, from_x, from_y, low_part, high_part):
        cut = others.shape[1]
        steps, hops, flips, cols, halves = [], [], [], [], []
        for half in range(2):
            for col in range(chips):
                steps.append((0, half, col * col_step))
                hops.append(0), flips.append(-1), cols.append(col), halves.append(half)
        for which, flip in ((1, 0), (2, 1), (3, 2)):
            for hop in range(1, shards):
                for half in range(2):
                    steps.append((which, 2 * (hop - 1) + half, 0))
                    hops.append(hop), flips.append(flip), cols.append(0), halves.append(half)
        for which, half in ((4, 0), (5, 1)):
            for hop in range(1, shards):
                steps.append((which, hop - 1, 0))
                hops.append(hop), flips.append(3), cols.append(0), halves.append(half)
        hops, flips, cols, halves = (np.array(v, np.int32) for v in (hops, flips, cols, halves))
        return place(
            [source, others, from_x, from_y, low_part, high_part],
            steps,
            2 * ((shard - hops) % shards) + halves,
            jnp.where(flips < 0, cols, ch ^ np.maximum(flips, 0)),
            (height // 2, cut),
            (shards * height, chips * cut),
            BF,
            offset,
        )

    def whole_weight_any(piece):
        everything = lax.all_gather(lax.all_gather(piece, "sh"), "ch")
        return everything.transpose(1, 2, 0, 3).reshape(-1, chips * piece.shape[1])

    def grad_block(left_side, right_side, flips, half):
        cut = right_side.shape[1] // chips
        blocks = [lax.dynamic_slice_in_dim(right_side, (ch ^ flip) * cut, cut, 1) for flip in flips]
        block = blocks[0] if len(flips) == 1 else jnp.concatenate(blocks, axis=1)
        width_half = left_side.shape[1] // 2
        return cross_rows(left_side[:, half * width_half : (half + 1) * width_half], block).astype(BF)

    def sum_shards(mine):
        return lax.psum_scatter(mine, "sh", scatter_dimension=0, tiled=True)

    def sum_any(left_side, right_side):
        cut = right_side.shape[1] // chips
        grads = cross_rows(left_side, right_side).astype(BF).reshape(-1, chips, cut).transpose(1, 0, 2)
        return sum_shards(lax.psum_scatter(grads, "ch", scatter_dimension=0))

    def spread_any(mine, chunk):
        height = mine.shape[0]
        own = lax.all_gather(mine, "ch", axis=1, tiled=True)
        other = swap(own)
        pair = [jnp.where(core == 0, own, other), jnp.where(core == 0, other, own)]
        if chunk is None:
            return jnp.concatenate(pair).astype(F32)
        wide = jnp.stack([member.reshape(height, -1, chunk) for member in pair], axis=2)
        return wide.reshape(height, -1).astype(F32)

    def spread_first(mine):
        from_x = plane(mine, 1)
        from_y = plane(mine, 2)
        return mine, from_x, from_y

    def spread_second(mine, from_x, from_y):
        middle_row = mine.shape[0] // 2
        low_part = plane(from_x[:middle_row], 2)
        high_part = plane(from_y[middle_row:], 1)
        own = jnp.concatenate([mine, from_x, from_y, low_part, high_part])
        return own, swap(own)

    def spread_last(own, other, chunk):
        height, cut = own.shape[0] // 4, own.shape[1]
        block_cols = cut if chunk is None else chunk
        per = cut // block_cols
        steps, flips, cores, inner = [], [], [], []
        for source in range(2):
            for flip in range(4):
                for at in range(per):
                    steps.append((source, flip, at))
                    flips.append(flip), cores.append(source), inner.append(at)
        flips, cores, inner = (np.array(v, np.int32) for v in (flips, cores, inner))
        side = core ^ cores
        cols = (ch ^ flips) * per + inner
        if chunk is None:
            dest_rows, dest_cols, shape = side, cols, (2 * height, chips * cut)
        else:
            dest_rows, dest_cols, shape = 0 * side, cols * 2 + side, (height, 2 * chips * cut)
        return place([own, other], steps, dest_rows, dest_cols, (height, block_cols), shape, F32)

    def take(value, axis):
        return lax.dynamic_index_in_dim(value, core, axis, False)

    qkv_chunk = width // (shards * CORES)
    fc1_chunk = ff_units // (shards * CORES)

    def col_chunks(value, chunk, first, count):
        cuts = [lax.dynamic_slice_in_dim(value, ((first + i) * CORES + core) * chunk, chunk, 1) for i in range(count)]
        return cuts[0] if count == 1 else jnp.concatenate(cuts, axis=1)

    def col_piece(value, chunk):
        per = value.shape[1] // (CORES * chips * chunk)
        return col_chunks(value, chunk, ch * per, per)

    def row_piece(value):
        height, cut = value.shape[0] // CORES, value.shape[1] // chips
        return lax.dynamic_slice(value, (core * height, ch * cut), (height, cut))

    qkv_piece = col_piece(qkv_weight, qkv_chunk)
    fc1_piece = col_piece(fc1_weight, fc1_chunk)
    out_piece = row_piece(out_weight)
    fc2_piece = row_piece(fc2_weight)

    vectors = [ln1_gain, ln1_bias, q_bias, v_bias, out_bias, ln2_gain, ln2_bias, fc2_bias, fc1_bias]
    lengths = [v.shape[0] for v in vectors]
    edges = np.cumsum([0] + lengths)
    square = chips == 4
    small = jnp.concatenate(vectors)
    ring = [small] + [along(small, hop) for hop in range(shards - 1, 0, -1)]
    qkv_piece, tokens, *ring = lax.optimization_barrier((qkv_piece, tokens_in(hidden_in), *ring))
    gathered = lax.dynamic_slice_in_dim(jnp.stack(ring + ring), (shards - shard) % shards, shards, 0)
    vec = [gathered[:, edges[i] : edges[i + 1]].astype(F32) for i in range(len(vectors))]
    gain_one, shift_one, _, _, bias_out, gain_two, shift_two, bias_down, _ = [v.reshape(-1) for v in vec]
    bias_query, bias_value, bias_up = [
        take(vec[i].reshape(shards, CORES, -1), 1).reshape(-1) for i in (2, 3, 8)
    ]

    prefix_pair = [jnp.where(core == 0, a, b) for a, b in ((prefix, swap(prefix)), (swap(prefix), prefix))]
    prefix_len = jnp.concatenate(prefix_pair, axis=1).reshape(-1)[sequence]

    if square:
        qkv_others = others_of(gather_shards(qkv_piece))
        out_got = gather_shards(out_piece)
        fc1_got = gather_shards(fc1_piece)
        fc2_got = gather_shards(after(fc2_piece, out_got))
        qkv_x, qkv_y, qkv_low, qkv_high = spread_others(qkv_others)
        qkv_ends = plane(qkv_low, 2), plane(qkv_high, 1)
        out_others = others_of(after(out_got, (qkv_low, qkv_high)))
        out_x, out_y, out_low, out_high = spread_others(out_others)
        out_ends = plane(out_low, 2), plane(out_high, 1)

    hidden_f = tokens.astype(F32)
    normed_own = normalize(hidden_f, gain_one, shift_one).astype(BF)
    normed_one = jnp.concatenate([normed_own, swap(normed_own)])
    none = jnp.zeros((), jnp.int32)
    if square:
        qkv_mine = col_chunks(qkv_weight, qkv_chunk, 0, 3 * shards)
        qkv_full = whole_weight(
            qkv_mine, None, 1, piece_rows, qkv_others, qkv_x, qkv_y, *qkv_ends
        )
        out_full = whole_weight(
            out_weight, (2 * core, none), 1, piece_rows // 2, out_others, out_x, out_y, *out_ends
        )
    else:
        qkv_full, out_full, fc1_full, fc2_full = [
            whole_weight_any(piece) for piece in (qkv_piece, out_piece, fc1_piece, fc2_piece)
        ]
        grads_mine = tokens_in(grad_out)

    half_width = width // CORES
    projected = dot(normed_one, qkv_full) + jnp.concatenate([bias_query, jnp.zeros_like(bias_query), bias_value])
    projected = projected.astype(BF)
    if square:
        fc1_others = others_of(after(fc1_got, (projected, *out_ends)))
    scalars = jnp.stack([core.astype(jnp.int32), prefix_len.astype(jnp.int32)])
    if parts == 1:
        context = attend_forward(projected, scalars)
    else:
        part = shard % parts

        def to_part(value, hop):
            pairs = [(i, i // parts * parts + (i % parts + hop) % parts) for i in range(shards)]
            return lax.ppermute(value, "sh", pairs)

        def positions(which):
            at = jnp.arange(rows)
            return which * CORES * rows + jnp.concatenate([core * rows + at, (1 - core) * rows + at])

        q_four = projected[:, :half_width].reshape(CORES * rows, -1, HEAD_DIM)
        both = projected[:, half_width:]
        held = jnp.concatenate([both] + [to_part(both, hop) for hop in range(1, parts)])
        k_four = held[:, :half_width].reshape(held.shape[0], -1, HEAD_DIM)
        v_four = held[:, half_width:].reshape(held.shape[0], -1, HEAD_DIM)
        k_pos = jnp.concatenate([positions((part - hop) % parts) for hop in range(parts)])
        soft_full = spread_softmax(q_four, k_four, positions(part), k_pos, prefix_len)
        context = jnp.einsum("hqk,khd->qhd", soft_full.astype(BF), v_four, preferred_element_type=F32)
        context = context.reshape(CORES * rows, half_width).astype(BF)

    if square:
        fc1_x, fc1_y, fc1_low, fc1_high = spread_others(fc1_others, (context,))
        fc1_ends = plane(fc1_low, 2), plane(fc1_high, 1)
        fc2_others = others_of(after(fc2_got, fc1_ends))
        fc2_x, fc2_y, fc2_low, fc2_high = spread_others(fc2_others)
        fc1_full = whole_weight(
            fc1_weight, (none, core), 2, piece_rows, fc1_others, fc1_x, fc1_y, *fc1_ends
        )
        fc2_full = whole_weight(
            fc2_weight,
            (2 * core, none),
            1,
            fc2_weight.shape[0] // 2,
            fc2_others,
            fc2_x,
            fc2_y,
            plane(fc2_low, 2),
            plane(fc2_high, 1),
        )
        grads_mine = tokens_in(after(grad_out, fc2_others))
    grads_mine = lax.optimization_barrier(grads_mine)

    def own_sum(left_side, product):
        away = swap(product(left_side[rows:]).astype(BF))
        return product(left_side[:rows]) + away.astype(F32)

    middle = hidden_f + (own_sum(context, lambda v: dot(v, out_full)) + bias_out)
    if square:
        middle = after(middle, (fc1_low, fc1_high, fc2_got))
    normed_two_own = normalize(middle, gain_two, shift_two).astype(BF)
    normed_two = jnp.concatenate([normed_two_own, swap(normed_two_own)])
    grads_mine = after(grads_mine, normed_two)
    pre_act = dot(normed_two, fc1_full) + bias_up
    below = 0.5 * (1.0 + lax.erf(pre_act * math.sqrt(0.5)))
    density = jnp.exp(-0.5 * pre_act * pre_act) * (1.0 / math.sqrt(2.0 * math.pi))
    activated = (pre_act * below).astype(BF)
    slope = (below + pre_act * density).astype(BF)

    grad_rows = grads_mine.astype(F32)
    grad_both = jnp.concatenate([grads_mine, swap(grads_mine)])
    down_bias_grad = jnp.sum(grad_rows, axis=0)

    class Reduction:
        def __init__(self, left_side, right_side, barrier=()):
            self.sides = (left_side, right_side)
            self.cut = right_side.shape[1] // chips
            to_x = grad_block(left_side, right_side, (3, 1), 1)
            to_y = grad_block(left_side, right_side, (3, 2), 0)
            self.from_x = plane(to_x, 1)
            self.from_y = plane(to_y, 2)
            right_side = after(right_side, (to_x, to_y, *barrier))
            self.near = [grad_block(left_side, right_side, (1,), 0), grad_block(left_side, right_side, (2,), 1)]

        def second(self, barrier=()):
            from_x, from_y, *_ = lax.optimization_barrier((self.from_x, self.from_y, *barrier))
            self.sent = [self.near[0] + from_y[:, : self.cut], self.near[1] + from_x[:, : self.cut]]
            self.x_low = plane(self.sent[0], 1)
            self.y_high = plane(self.sent[1], 2)

        def third(self, barrier=()):
            x_low, y_high, *_ = lax.optimization_barrier((self.x_low, self.y_high, *barrier))
            low_part = grad_block(*self.sides, (0,), 0).astype(F32) + x_low.astype(F32)
            high_part = grad_block(*self.sides, (0,), 1).astype(F32) + y_high.astype(F32)
            low_part = low_part + self.from_y[:, self.cut :].astype(F32)
            high_part = high_part + self.from_x[:, self.cut :].astype(F32)
            self.mine = jnp.concatenate([low_part.astype(BF), high_part.astype(BF)])
            return sum_shards(self.mine)

    if square:
        fc2_red = Reduction(activated, after(grad_both, (fc2_low, fc2_high)))
    d_pre = (times_rows(grad_both, fc2_full) * slope.astype(F32)).astype(BF)
    up_bias_grad = jnp.sum(d_pre, axis=0, dtype=F32)
    if square:
        fc2_red.second()
        d_pre = after(d_pre, fc2_red.sent)
        fc1_red = Reduction(normed_two, d_pre, (fc2_red.x_low, fc2_red.y_high))
        activated = after(activated, fc1_red.near)
    result_own = middle + (own_sum(activated, lambda v: dot(v, fc2_full)) + bias_down)
    result = tokens_out(result_own.astype(BF))
    d_normed_two = own_sum(d_pre, lambda v: times_rows(v, fc1_full))
    back_two = jax.vjp(normalize, middle, gain_two, shift_two)[1]
    d_middle, gain_two_grad, shift_two_grad = back_two(d_normed_two)
    d_middle = d_middle + grad_rows
    d_attn_own = d_middle.astype(BF)
    out_bias_grad = jnp.sum(d_attn_own, axis=0, dtype=F32)
    d_attn = jnp.concatenate([d_attn_own, swap(d_attn_own)])
    if square:
        fc1_red.second((*fc2_red.sent, result_own))
        out_red = Reduction(context, d_attn)
    d_context = times_rows(d_attn, out_full).astype(BF)
    if square:
        d_context = after(d_context, fc1_red.sent)
    if parts == 1:
        d_queries, d_keys, d_values = attend_backward(projected, d_context, scalars)
    else:
        d_four = d_context.reshape(CORES * rows, -1, HEAD_DIM)
        d_queries, d_keys, d_values = spread_backward(q_four, k_four, v_four, d_four, soft_full)
        d_queries = d_queries.reshape(CORES * rows, half_width).astype(BF)
        d_held = jnp.concatenate([d_keys, d_values], axis=1).reshape(parts, CORES * rows, width)
        d_both = d_held[0]
        for hop in range(1, parts):
            d_both = d_both + to_part(d_held[hop].astype(BF), parts - hop).astype(F32)
        d_both = d_both.astype(BF)
        d_keys, d_values = d_both[:, :half_width], d_both[:, half_width:]
    d_projected = jnp.concatenate([d_queries, d_keys, d_values], axis=1)
    if square:
        fc2_part = fc2_red.third()
        d_projected = after(d_projected, fc2_red.mine)
        qkv_red = Reduction(normed_one, d_projected)
        out_red.second()
        d_projected = after(d_projected, qkv_red.near)
        fc1_part = fc1_red.third((*qkv_red.near, d_projected, result))
        qkv_red.second((fc1_red.mine, *out_red.sent))
    query_bias_grad = jnp.sum(d_projected[:, :half_width], axis=0, dtype=F32)
    value_bias_grad = jnp.sum(d_projected[:, width:], axis=0, dtype=F32)
    d_normed_one = own_sum(d_projected, lambda v: times_rows(v, qkv_full))
    back_one = jax.vjp(normalize, hidden_f, gain_one, shift_one)[1]
    d_inputs, gain_one_grad, shift_one_grad = back_one(d_normed_one)
    grad_in_own = (d_middle + d_inputs).astype(BF)
    grad_in = tokens_out(grad_in_own)

    def half_slot(value):
        value = value.reshape(shards, 1, -1)
        mask = lax.broadcasted_iota(jnp.int32, (1, CORES, 1), 1) == core
        return jnp.where(mask, value, 0.0).reshape(shards, -1)

    def full_slot(value):
        return value.reshape(shards, -1)

    packed = jnp.concatenate(
        [
            full_slot(gain_one_grad),
            full_slot(shift_one_grad),
            half_slot(query_bias_grad),
            half_slot(value_bias_grad),
            full_slot(out_bias_grad),
            full_slot(gain_two_grad),
            full_slot(shift_two_grad),
            full_slot(down_bias_grad),
            half_slot(up_bias_grad),
        ],
        axis=1,
    )
    def sum_plane(values, bits):
        for bit in bits:
            values = values + plane(values, 1 << bit)
        return values

    def sum_line(values):
        total = lax.dynamic_index_in_dim(values, shard, 0, False)
        for hop in range(1, shards):
            total = total + along(lax.dynamic_index_in_dim(values, (shard + hop) % shards, 0, False), hop)
        return total

    packed = packed + swap(packed)
    if square:
        out_part = out_red.third((*qkv_red.sent, grad_in))
        fc2_first = spread_first(after(fc2_part, (qkv_red.sent, out_red.mine)))
        qkv_part = qkv_red.third()
        packed = sum_plane(packed, [0])
        fc1_first = spread_first(after(fc1_part, (fc2_first[1:], qkv_red.mine, packed)))
        fc2_pair = spread_second(*fc2_first)
        packed = sum_plane(packed, [1])
        out_first = spread_first(after(out_part, (fc1_first[1:], fc2_pair[0], packed)))
        summed = sum_line(after(packed, qkv_part))
        fc1_pair = spread_second(*fc1_first)
        fc2_weight_grad = spread_last(*fc2_pair, None)
        fc1_weight_grad = spread_last(*fc1_pair, fc1_chunk)
        out_pair = spread_second(*out_first)
        qkv_first = spread_first(after(qkv_part, (out_pair[0], fc1_pair[0], fc2_weight_grad)))
        out_weight_grad = spread_last(*out_pair, None)
        qkv_own, qkv_other = spread_second(*after(qkv_first, (fc1_weight_grad, out_pair[1])))
        qkv_weight_grad = spread_last(qkv_own, after(qkv_other, out_weight_grad), qkv_chunk)
    else:
        summed = sum_line(sum_plane(packed, range(chips.bit_length() - 1)))
        fc2_weight_grad = spread_any(sum_any(activated, grad_both), None)
        fc1_weight_grad = spread_any(sum_any(normed_two, d_pre), fc1_chunk)
        out_weight_grad = spread_any(sum_any(context, d_attn), None)
        qkv_weight_grad = spread_any(sum_any(normed_one, d_projected), qkv_chunk)
    sums = [summed[edges[i] : edges[i + 1]] for i in range(len(vectors))]
    return (
        result,
        grad_in,
        sums[0],
        sums[1],
        qkv_weight_grad,
        sums[2],
        sums[3],
        out_weight_grad,
        sums[4],
        sums[5],
        sums[6],
        fc1_weight_grad,
        sums[8],
        fc2_weight_grad,
        sums[7],
    )


def solution(mesh):
    shards = mesh.shape["shard"]
    chips = mesh.shape["rep"] // CORES
    inner = Mesh(mesh.devices.reshape(chips, CORES, shards), ALL)
    token_spec = P(None, ALL, None)
    args = [token_spec, P(None, ("ch", "co"))]
    for dims in (1, 1, 2, 1, 1, 2, 1, 1, 1, 2, 1, 2, 1):
        args.append(P("sh", None) if dims == 2 else P("sh"))
    args.append(token_spec)
    outs = [token_spec, token_spec]
    for dims in (1, 1, 2, 1, 1, 2, 1, 1, 1, 2, 1, 2, 1):
        outs.append(P("sh", None) if dims == 2 else P("sh"))

    def run(*values):
        return local(*values, chips=chips, shards=shards)

    return jax.shard_map(run, mesh=inner, in_specs=tuple(args), out_specs=tuple(outs), check_vma=False)
```

```python
import math

import jax
import jax.numpy as jnp
import numpy as np
from jax import lax
from jax.experimental import pallas as pl
from jax.experimental.pallas import tpu as pltpu
from jax.sharding import Mesh
from jax.sharding import PartitionSpec as P

HEADS = 16
HEAD_DIM = 128
CORES = 2
EPSILON = 1e-05
MASKED = -1e30
SCALE = 1.0 / math.sqrt(HEAD_DIM)
ALL = ("ch", "co", "sh")
BF = jnp.bfloat16
F32 = jnp.float32


def normalize(values, gain_vec, shift_vec):
    centred = values - jnp.mean(values, axis=-1, keepdims=True)
    spread = jnp.mean(centred * centred, axis=-1, keepdims=True)
    return centred * lax.rsqrt(spread + EPSILON) * gain_vec + shift_vec


def dot(left_side, right_side):
    return jnp.dot(left_side, right_side, preferred_element_type=F32)


def cross_rows(left_side, right_side):
    return lax.dot_general(left_side, right_side, (((0,), (0,)), ((), ())), preferred_element_type=F32)


def times_rows(left_side, right_side):
    return lax.dot_general(left_side, right_side, (((1,), (1,)), ((), ())), preferred_element_type=F32)


def after(value, other):
    return lax.optimization_barrier((value, other))[0]


def place(sources, steps, dest_rows, dest_cols, block, out_shape, out_dtype, offset=None):
    count = len(steps)
    spans = []
    table = []
    for which in range(len(sources)):
        mine = [i for i, step in enumerate(steps) if step[0] == which]
        first, last = mine[0], mine[-1]
        spans.append((first, last + 1))
        hold = [steps[min(max(i, first), last)] for i in range(count)]
        table.append([step[1] for step in hold])
        table.append([step[2] for step in hold])
    fixed = jnp.asarray(np.array(table, np.int32))
    if offset is not None:
        mask = lax.broadcasted_iota(jnp.int32, (fixed.shape[0], 1), 0)
        fixed = fixed + jnp.where(mask == 0, offset[0], jnp.where(mask == 1, offset[1], 0))
    table = jnp.concatenate(
        [fixed, dest_rows.astype(jnp.int32)[None], dest_cols.astype(jnp.int32)[None]]
    )
    last_row = 2 * len(sources)

    def body(table_ref, *refs):
        step = pl.program_id(0)
        out_ref = refs[-1]
        for which, (first, stop) in enumerate(spans):

            @pl.when((step >= first) & (step < stop))
            def _():
                out_ref[...] = refs[which][...].astype(out_dtype)

    def in_map(which):
        return lambda i, table_ref: (table_ref[2 * which, i], table_ref[2 * which + 1, i])

    return pl.pallas_call(
        body,
        grid_spec=pltpu.PrefetchScalarGridSpec(
            num_scalar_prefetch=1,
            grid=(count,),
            in_specs=[pl.BlockSpec(block, in_map(which)) for which in range(len(sources))],
            out_specs=pl.BlockSpec(block, lambda i, table_ref: (table_ref[last_row, i], table_ref[last_row + 1, i])),
        ),
        out_shape=jax.ShapeDtypeStruct(out_shape, out_dtype),
    )(table, *sources)


def head_parts(scal_ref, q_ref, k_ref, block, rows):
    half = 2 * rows
    core = scal_ref[0]
    prefix = scal_ref[1]
    side = block // 2
    offsets = [pl.multiple_of(core * half, half), pl.multiple_of((1 - core) * half, half)]
    q_off = pl.multiple_of(offsets[side] + (block % 2) * rows, rows)
    queries = q_ref[pl.ds(q_off, rows), :]
    chunks = [(offsets[0], half, 0)]
    if side == 1:
        chunks.append((offsets[1], (block - 1) * rows, half))
    scores = []
    for k_off, count, first in chunks:
        raw = lax.dot_general(
            queries, k_ref[pl.ds(k_off, count), :], (((1,), (1,)), ((), ())), preferred_element_type=F32
        )
        raw = raw * SCALE
        if first + count > block * rows:
            q_pos = block * rows + lax.broadcasted_iota(jnp.int32, raw.shape, 0)
            k_pos = first + lax.broadcasted_iota(jnp.int32, raw.shape, 1)
            raw = jnp.where((k_pos <= q_pos) | (k_pos < prefix), raw, MASKED)
        scores.append(raw)
    top = scores[0].max(axis=-1, keepdims=True)
    for raw in scores[1:]:
        top = jnp.maximum(top, raw.max(axis=-1, keepdims=True))
    terms = [jnp.exp(raw - top) for raw in scores]
    total = terms[0].sum(axis=-1, keepdims=True)
    for term in terms[1:]:
        total = total + term.sum(axis=-1, keepdims=True)
    inverse = 1.0 / total
    return q_off, queries, [(k_off, count, term * inverse) for (k_off, count, _), term in zip(chunks, terms)]


def attend_forward_body(scal_ref, q_ref, k_ref, v_ref, out_ref):
    rows = q_ref.shape[0] // 4
    for block in range(4):
        q_off, _, parts = head_parts(scal_ref, q_ref, k_ref, block, rows)
        total = None
        for k_off, count, soft in parts:
            term = jnp.dot(soft.astype(BF), v_ref[pl.ds(k_off, count), :], preferred_element_type=F32)
            total = term if total is None else total + term
        out_ref[pl.ds(q_off, rows), :] = total.astype(BF)


def attend_backward_body(scal_ref, q_ref, k_ref, v_ref, d_ref, dq_ref, dk_ref, dv_ref, dk_acc, dv_acc):
    rows = q_ref.shape[0] // 4
    dk_acc[...] = jnp.zeros_like(dk_acc)
    dv_acc[...] = jnp.zeros_like(dv_acc)
    for block in range(4):
        q_off, queries, parts = head_parts(scal_ref, q_ref, k_ref, block, rows)
        d_out = d_ref[pl.ds(q_off, rows), :]
        d_softs = []
        row_sum = None
        for k_off, count, soft in parts:
            dv_acc[pl.ds(k_off, count), :] += lax.dot_general(
                soft.astype(BF), d_out, (((0,), (0,)), ((), ())), preferred_element_type=F32
            )
            d_soft = lax.dot_general(
                d_out, v_ref[pl.ds(k_off, count), :], (((1,), (1,)), ((), ())), preferred_element_type=F32
            )
            d_softs.append(d_soft)
            term = jnp.sum(soft * d_soft, axis=-1, keepdims=True)
            row_sum = term if row_sum is None else row_sum + term
        d_queries = None
        for (k_off, count, soft), d_soft in zip(parts, d_softs):
            d_scores = (soft * (d_soft - row_sum) * SCALE).astype(BF)
            term = jnp.dot(d_scores, k_ref[pl.ds(k_off, count), :], preferred_element_type=F32)
            d_queries = term if d_queries is None else d_queries + term
            dk_acc[pl.ds(k_off, count), :] += lax.dot_general(
                d_scores, queries, (((0,), (0,)), ((), ())), preferred_element_type=F32
            )
        dq_ref[pl.ds(q_off, rows), :] = d_queries.astype(BF)
    dk_ref[...] = dk_acc[...].astype(BF)
    dv_ref[...] = dv_acc[...].astype(BF)


def head_specs(rows, heads):
    return [pl.BlockSpec((rows, HEAD_DIM), lambda h, scal_ref, at=at: (0, at * heads + h)) for at in range(3)]


def attend_forward(projected, scalars):
    rows, width = projected.shape
    heads = width // (3 * HEAD_DIM)
    return pl.pallas_call(
        attend_forward_body,
        grid_spec=pltpu.PrefetchScalarGridSpec(
            num_scalar_prefetch=1,
            grid=(heads,),
            in_specs=head_specs(rows, heads),
            out_specs=head_specs(rows, heads)[0],
        ),
        out_shape=jax.ShapeDtypeStruct((rows, width // 3), BF),
    )(scalars, projected, projected, projected)


def attend_backward(projected, d_context, scalars):
    rows, width = projected.shape
    heads = width // (3 * HEAD_DIM)
    one = head_specs(rows, heads)[0]
    return pl.pallas_call(
        attend_backward_body,
        grid_spec=pltpu.PrefetchScalarGridSpec(
            num_scalar_prefetch=1,
            grid=(heads,),
            in_specs=head_specs(rows, heads) + [one],
            out_specs=[one, one, one],
            scratch_shapes=[pltpu.VMEM((rows, HEAD_DIM), F32), pltpu.VMEM((rows, HEAD_DIM), F32)],
        ),
        out_shape=[jax.ShapeDtypeStruct((rows, width // 3), BF)] * 3,
    )(scalars, projected, projected, projected, d_context)


def spread_softmax(queries, keys, q_pos, k_pos, prefix):
    raw = jnp.einsum("qhd,khd->hqk", queries, keys, preferred_element_type=F32) * SCALE
    visible = (k_pos[None, :] <= q_pos[:, None]) | (k_pos[None, :] < prefix)
    raw = jnp.where(visible[None], raw, MASKED)
    terms = jnp.exp(raw - jnp.max(raw, axis=-1, keepdims=True))
    return terms / jnp.sum(terms, axis=-1, keepdims=True)


def spread_backward(queries, keys, values, d_context, soft):
    d_values = jnp.einsum("hqk,qhd->khd", soft.astype(BF), d_context, preferred_element_type=F32)
    d_soft = jnp.einsum("qhd,khd->hqk", d_context, values, preferred_element_type=F32)
    d_scores = (soft * (d_soft - jnp.sum(soft * d_soft, axis=-1, keepdims=True)) * SCALE).astype(BF)
    d_queries = jnp.einsum("hqk,khd->qhd", d_scores, keys, preferred_element_type=F32)
    d_keys = jnp.einsum("hqk,qhd->khd", d_scores, queries, preferred_element_type=F32)
    return d_queries, d_keys, d_values


def local(
    hidden_in,
    prefix,
    ln1_gain,
    ln1_bias,
    qkv_weight,
    q_bias,
    v_bias,
    out_weight,
    out_bias,
    ln2_gain,
    ln2_bias,
    fc1_weight,
    fc1_bias,
    fc2_weight,
    fc2_bias,
    grad_out,
    *,
    chips,
    shards,
):
    micro_count, tok_rows, width = hidden_in.shape
    ff_units = fc1_weight.shape[1]
    piece_rows = width // shards
    rows = micro_count * tok_rows
    parts = shards // (micro_count * CORES)
    ch = lax.axis_index("ch")
    core = lax.axis_index("co")
    shard = lax.axis_index("sh")
    sequence = shard // parts
    micro = sequence // CORES

    def along(value, hop):
        return lax.ppermute(value, "sh", [(i, (i + hop) % shards) for i in range(shards)])

    def plane(value, bit):
        return lax.ppermute(value, "ch", [(i, i ^ bit) for i in range(chips)])

    def swap(value):
        return lax.ppermute(value, "co", [(0, 1), (1, 0)])

    def token_pairs(turn):
        pairs = []
        for c in range(chips):
            for o in range(CORES):
                for s in range(shards):
                    m = (turn + s) % 2
                    slot = s // 2
                    z = (m * CORES + o) * parts + slot // 2
                    pairs.append(((c * CORES + o) * shards + s, (c * CORES + slot % 2) * shards + z))
        return pairs

    def tokens_in(value, barrier=()):
        got = [
            lax.ppermute(lax.dynamic_index_in_dim(value, (turn + shard) % 2, 0, False), ALL, token_pairs(turn))
            for turn in (0, 1)
        ]
        got = lax.optimization_barrier((*got, *barrier))
        even = micro % 2 == 0
        return jnp.concatenate([jnp.where(even, got[0], got[1]), jnp.where(even, got[1], got[0])])

    def tokens_out(value):
        value = value.reshape(2, tok_rows, width)
        got = [
            lax.ppermute(
                lax.dynamic_index_in_dim(value, (turn + micro) % 2, 0, False),
                ALL,
                [(b, a) for a, b in token_pairs(turn)],
            )
            for turn in (0, 1)
        ]
        even = shard % 2 == 0
        return jnp.stack([jnp.where(even, got[0], got[1]), jnp.where(even, got[1], got[0])])

    def gather_shards(piece):
        return lax.all_gather(piece, "sh")

    def others_of(held):
        return jnp.concatenate(
            [lax.dynamic_index_in_dim(held, (shard - hop) % shards, 0, False) for hop in range(1, shards)]
        )

    def spread_others(others, barrier=()):
        from_x = plane(others, 1)
        from_y = plane(others, 2)
        from_x, from_y, *_ = lax.optimization_barrier((from_x, from_y, *barrier))
        tall = (shards - 1, 2, others.shape[0] // (2 * (shards - 1)), others.shape[1])
        low_cut = from_x.reshape(tall)[:, 0].reshape(-1, tall[3])
        high_cut = from_y.reshape(tall)[:, 1].reshape(-1, tall[3])
        return from_x, from_y, low_cut, high_cut

    def whole_weight(source, offset, col_step, height, others, from_x, from_y, low_part, high_part):
        cut = others.shape[1]
        steps, hops, flips, cols, halves = [], [], [], [], []
        for half in range(2):
            for col in range(chips):
                steps.append((0, half, col * col_step))
                hops.append(0), flips.append(-1), cols.append(col), halves.append(half)
        for which, flip in ((1, 0), (2, 1), (3, 2)):
            for hop in range(1, shards):
                for half in range(2):
                    steps.append((which, 2 * (hop - 1) + half, 0))
                    hops.append(hop), flips.append(flip), cols.append(0), halves.append(half)
        for which, half in ((4, 0), (5, 1)):
            for hop in range(1, shards):
                steps.append((which, hop - 1, 0))
                hops.append(hop), flips.append(3), cols.append(0), halves.append(half)
        hops, flips, cols, halves = (np.array(v, np.int32) for v in (hops, flips, cols, halves))
        return place(
            [source, others, from_x, from_y, low_part, high_part],
            steps,
            2 * ((shard - hops) % shards) + halves,
            jnp.where(flips < 0, cols, ch ^ np.maximum(flips, 0)),
            (height // 2, cut),
            (shards * height, chips * cut),
            BF,
            offset,
        )

    def whole_weight_any(piece):
        everything = lax.all_gather(lax.all_gather(piece, "sh"), "ch")
        return everything.transpose(1, 2, 0, 3).reshape(-1, chips * piece.shape[1])

    def grad_block(left_side, right_side, flips, half):
        cut = right_side.shape[1] // chips
        blocks = [lax.dynamic_slice_in_dim(right_side, (ch ^ flip) * cut, cut, 1) for flip in flips]
        block = blocks[0] if len(flips) == 1 else jnp.concatenate(blocks, axis=1)
        width_half = left_side.shape[1] // 2
        return cross_rows(left_side[:, half * width_half : (half + 1) * width_half], block).astype(BF)

    def sum_shards(mine):
        return lax.psum_scatter(mine, "sh", scatter_dimension=0, tiled=True)

    def sum_any(left_side, right_side):
        cut = right_side.shape[1] // chips
        grads = cross_rows(left_side, right_side).astype(BF).reshape(-1, chips, cut).transpose(1, 0, 2)
        return sum_shards(lax.psum_scatter(grads, "ch", scatter_dimension=0))

    def spread_any(mine, chunk):
        height = mine.shape[0]
        own = lax.all_gather(mine, "ch", axis=1, tiled=True)
        other = swap(own)
        pair = [jnp.where(core == 0, own, other), jnp.where(core == 0, other, own)]
        if chunk is None:
            return jnp.concatenate(pair).astype(F32)
        wide = jnp.stack([member.reshape(height, -1, chunk) for member in pair], axis=2)
        return wide.reshape(height, -1).astype(F32)

    def spread_first(mine):
        from_x = plane(mine, 1)
        from_y = plane(mine, 2)
        return mine, from_x, from_y

    def spread_second(mine, from_x, from_y):
        middle_row = mine.shape[0] // 2
        low_part = plane(from_x[:middle_row], 2)
        high_part = plane(from_y[middle_row:], 1)
        own = jnp.concatenate([mine, from_x, from_y, low_part, high_part])
        return own, swap(own)

    def spread_last(own, other, chunk):
        height, cut = own.shape[0] // 4, own.shape[1]
        block_cols = cut if chunk is None else chunk
        per = cut // block_cols
        steps, flips, cores, inner = [], [], [], []
        for source in range(2):
            for flip in range(4):
                for at in range(per):
                    steps.append((source, flip, at))
                    flips.append(flip), cores.append(source), inner.append(at)
        flips, cores, inner = (np.array(v, np.int32) for v in (flips, cores, inner))
        side = core ^ cores
        cols = (ch ^ flips) * per + inner
        if chunk is None:
            dest_rows, dest_cols, shape = side, cols, (2 * height, chips * cut)
        else:
            dest_rows, dest_cols, shape = 0 * side, cols * 2 + side, (height, 2 * chips * cut)
        return place([own, other], steps, dest_rows, dest_cols, (height, block_cols), shape, F32)

    def take(value, axis):
        return lax.dynamic_index_in_dim(value, core, axis, False)

    qkv_chunk = width // (shards * CORES)
    fc1_chunk = ff_units // (shards * CORES)

    def col_chunks(value, chunk, first, count):
        cuts = [lax.dynamic_slice_in_dim(value, ((first + i) * CORES + core) * chunk, chunk, 1) for i in range(count)]
        return cuts[0] if count == 1 else jnp.concatenate(cuts, axis=1)

    def col_piece(value, chunk):
        per = value.shape[1] // (CORES * chips * chunk)
        return col_chunks(value, chunk, ch * per, per)

    def row_piece(value):
        height, cut = value.shape[0] // CORES, value.shape[1] // chips
        return lax.dynamic_slice(value, (core * height, ch * cut), (height, cut))

    qkv_piece = col_piece(qkv_weight, qkv_chunk)
    fc1_piece = col_piece(fc1_weight, fc1_chunk)
    out_piece = row_piece(out_weight)
    fc2_piece = row_piece(fc2_weight)

    vectors = [ln1_gain, ln1_bias, q_bias, v_bias, out_bias, ln2_gain, ln2_bias, fc2_bias, fc1_bias]
    lengths = [v.shape[0] for v in vectors]
    edges = np.cumsum([0] + lengths)
    square = chips == 4
    small = jnp.concatenate(vectors)
    ring = [small] + [along(small, hop) for hop in range(shards - 1, 0, -1)]
    qkv_piece, tokens, *ring = lax.optimization_barrier((qkv_piece, tokens_in(hidden_in), *ring))
    gathered = lax.dynamic_slice_in_dim(jnp.stack(ring + ring), (shards - shard) % shards, shards, 0)
    vec = [gathered[:, edges[i] : edges[i + 1]].astype(F32) for i in range(len(vectors))]
    gain_one, shift_one, _, _, bias_out, gain_two, shift_two, bias_down, _ = [v.reshape(-1) for v in vec]
    bias_query, bias_value, bias_up = [
        take(vec[i].reshape(shards, CORES, -1), 1).reshape(-1) for i in (2, 3, 8)
    ]

    prefix_pair = [jnp.where(core == 0, a, b) for a, b in ((prefix, swap(prefix)), (swap(prefix), prefix))]
    prefix_len = jnp.concatenate(prefix_pair, axis=1).reshape(-1)[sequence]

    if square:
        qkv_others = others_of(gather_shards(qkv_piece))
        out_got = gather_shards(out_piece)
        fc1_got = gather_shards(fc1_piece)
        fc2_got = gather_shards(after(fc2_piece, out_got))
        qkv_x, qkv_y, qkv_low, qkv_high = spread_others(qkv_others)
        qkv_ends = plane(qkv_low, 2), plane(qkv_high, 1)
        out_others = others_of(after(out_got, (qkv_low, qkv_high)))
        out_x, out_y, out_low, out_high = spread_others(out_others)
        out_ends = plane(out_low, 2), plane(out_high, 1)

    hidden_f = tokens.astype(F32)
    normed_own = normalize(hidden_f, gain_one, shift_one).astype(BF)
    normed_one = jnp.concatenate([normed_own, swap(normed_own)])
    none = jnp.zeros((), jnp.int32)
    if square:
        qkv_mine = col_chunks(qkv_weight, qkv_chunk, 0, 3 * shards)
        qkv_full = whole_weight(
            qkv_mine, None, 1, piece_rows, qkv_others, qkv_x, qkv_y, *qkv_ends
        )
        out_full = whole_weight(
            out_weight, (2 * core, none), 1, piece_rows // 2, out_others, out_x, out_y, *out_ends
        )
    else:
        qkv_full, out_full, fc1_full, fc2_full = [
            whole_weight_any(piece) for piece in (qkv_piece, out_piece, fc1_piece, fc2_piece)
        ]
        grads_mine = tokens_in(grad_out)

    half_width = width // CORES
    projected = dot(normed_one, qkv_full) + jnp.concatenate([bias_query, jnp.zeros_like(bias_query), bias_value])
    projected = projected.astype(BF)
    if square:
        fc1_others = others_of(after(fc1_got, (projected, *out_ends)))
    scalars = jnp.stack([core.astype(jnp.int32), prefix_len.astype(jnp.int32)])
    if parts == 1:
        context = attend_forward(projected, scalars)
    else:
        part = shard % parts

        def to_part(value, hop):
            pairs = [(i, i // parts * parts + (i % parts + hop) % parts) for i in range(shards)]
            return lax.ppermute(value, "sh", pairs)

        def positions(which):
            at = jnp.arange(rows)
            return which * CORES * rows + jnp.concatenate([core * rows + at, (1 - core) * rows + at])

        q_four = projected[:, :half_width].reshape(CORES * rows, -1, HEAD_DIM)
        both = projected[:, half_width:]
        held = jnp.concatenate([both] + [to_part(both, hop) for hop in range(1, parts)])
        k_four = held[:, :half_width].reshape(held.shape[0], -1, HEAD_DIM)
        v_four = held[:, half_width:].reshape(held.shape[0], -1, HEAD_DIM)
        k_pos = jnp.concatenate([positions((part - hop) % parts) for hop in range(parts)])
        soft_full = spread_softmax(q_four, k_four, positions(part), k_pos, prefix_len)
        context = jnp.einsum("hqk,khd->qhd", soft_full.astype(BF), v_four, preferred_element_type=F32)
        context = context.reshape(CORES * rows, half_width).astype(BF)

    if square:
        fc1_x, fc1_y, fc1_low, fc1_high = spread_others(fc1_others, (context,))
        fc1_ends = plane(fc1_low, 2), plane(fc1_high, 1)
        fc2_others = others_of(after(fc2_got, fc1_ends))
        fc2_x, fc2_y, fc2_low, fc2_high = spread_others(fc2_others)
        fc1_full = whole_weight(
            fc1_weight, (none, core), 2, piece_rows, fc1_others, fc1_x, fc1_y, *fc1_ends
        )
        fc2_full = whole_weight(
            fc2_weight,
            (2 * core, none),
            1,
            fc2_weight.shape[0] // 2,
            fc2_others,
            fc2_x,
            fc2_y,
            plane(fc2_low, 2),
            plane(fc2_high, 1),
        )
        grads_mine = tokens_in(after(grad_out, fc2_others))
    grads_mine = lax.optimization_barrier(grads_mine)

    def own_sum(left_side, product):
        away = swap(product(left_side[rows:]).astype(BF))
        return product(left_side[:rows]) + away.astype(F32)

    middle = hidden_f + (own_sum(context, lambda v: dot(v, out_full)) + bias_out)
    if square:
        middle = after(middle, (fc1_low, fc1_high, fc2_got))
    normed_two_own = normalize(middle, gain_two, shift_two).astype(BF)
    normed_two = jnp.concatenate([normed_two_own, swap(normed_two_own)])
    grads_mine = after(grads_mine, normed_two)
    pre_act = dot(normed_two, fc1_full) + bias_up
    below = 0.5 * (1.0 + lax.erf(pre_act * math.sqrt(0.5)))
    density = jnp.exp(-0.5 * pre_act * pre_act) * (1.0 / math.sqrt(2.0 * math.pi))
    activated = (pre_act * below).astype(BF)
    slope = (below + pre_act * density).astype(BF)

    grad_rows = grads_mine.astype(F32)
    grad_both = jnp.concatenate([grads_mine, swap(grads_mine)])
    down_bias_grad = jnp.sum(grad_rows, axis=0)

    class Reduction:
        def __init__(self, left_side, right_side, barrier=()):
            self.sides = (left_side, right_side)
            self.cut = right_side.shape[1] // chips
            to_x = grad_block(left_side, right_side, (3, 1), 1)
            to_y = grad_block(left_side, right_side, (3, 2), 0)
            self.from_x = plane(to_x, 1)
            self.from_y = plane(to_y, 2)
            right_side = after(right_side, (to_x, to_y, *barrier))
            self.near = [grad_block(left_side, right_side, (1,), 0), grad_block(left_side, right_side, (2,), 1)]

        def second(self, barrier=()):
            from_x, from_y, *_ = lax.optimization_barrier((self.from_x, self.from_y, *barrier))
            self.sent = [self.near[0] + from_y[:, : self.cut], self.near[1] + from_x[:, : self.cut]]
            self.x_low = plane(self.sent[0], 1)
            self.y_high = plane(self.sent[1], 2)

        def third(self, barrier=()):
            x_low, y_high, *_ = lax.optimization_barrier((self.x_low, self.y_high, *barrier))
            low_part = grad_block(*self.sides, (0,), 0).astype(F32) + x_low.astype(F32)
            high_part = grad_block(*self.sides, (0,), 1).astype(F32) + y_high.astype(F32)
            low_part = low_part + self.from_y[:, self.cut :].astype(F32)
            high_part = high_part + self.from_x[:, self.cut :].astype(F32)
            self.mine = jnp.concatenate([low_part.astype(BF), high_part.astype(BF)])
            return sum_shards(self.mine)

    if square:
        fc2_red = Reduction(activated, after(grad_both, (fc2_low, fc2_high)))
    d_pre = (times_rows(grad_both, fc2_full) * slope.astype(F32)).astype(BF)
    up_bias_grad = jnp.sum(d_pre, axis=0, dtype=F32)
    if square:
        fc2_red.second()
        d_pre = after(d_pre, fc2_red.sent)
        fc1_red = Reduction(normed_two, d_pre, (fc2_red.x_low, fc2_red.y_high))
        activated = after(activated, fc1_red.near)
    result_own = middle + (own_sum(activated, lambda v: dot(v, fc2_full)) + bias_down)
    result = tokens_out(result_own.astype(BF))
    d_normed_two = own_sum(d_pre, lambda v: times_rows(v, fc1_full))
    back_two = jax.vjp(normalize, middle, gain_two, shift_two)[1]
    d_middle, gain_two_grad, shift_two_grad = back_two(d_normed_two)
    d_middle = d_middle + grad_rows
    d_attn_own = d_middle.astype(BF)
    out_bias_grad = jnp.sum(d_attn_own, axis=0, dtype=F32)
    d_attn = jnp.concatenate([d_attn_own, swap(d_attn_own)])
    if square:
        fc1_red.second((*fc2_red.sent, result_own))
        out_red = Reduction(context, d_attn)
    d_context = times_rows(d_attn, out_full).astype(BF)
    if square:
        d_context = after(d_context, fc1_red.sent)
    if parts == 1:
        d_queries, d_keys, d_values = attend_backward(projected, d_context, scalars)
    else:
        d_four = d_context.reshape(CORES * rows, -1, HEAD_DIM)
        d_queries, d_keys, d_values = spread_backward(q_four, k_four, v_four, d_four, soft_full)
        d_queries = d_queries.reshape(CORES * rows, half_width).astype(BF)
        d_held = jnp.concatenate([d_keys, d_values], axis=1).reshape(parts, CORES * rows, width)
        d_both = d_held[0]
        for hop in range(1, parts):
            d_both = d_both + to_part(d_held[hop].astype(BF), parts - hop).astype(F32)
        d_both = d_both.astype(BF)
        d_keys, d_values = d_both[:, :half_width], d_both[:, half_width:]
    d_projected = jnp.concatenate([d_queries, d_keys, d_values], axis=1)
    if square:
        fc2_part = fc2_red.third()
        d_projected = after(d_projected, fc2_red.mine)
        qkv_red = Reduction(normed_one, d_projected)
        out_red.second()
        d_projected = after(d_projected, qkv_red.near)
        fc1_part = fc1_red.third((*qkv_red.near, d_projected, result))
        qkv_red.second((fc1_red.mine, *out_red.sent))
    query_bias_grad = jnp.sum(d_projected[:, :half_width], axis=0, dtype=F32)
    value_bias_grad = jnp.sum(d_projected[:, width:], axis=0, dtype=F32)
    d_normed_one = own_sum(d_projected, lambda v: times_rows(v, qkv_full))
    back_one = jax.vjp(normalize, hidden_f, gain_one, shift_one)[1]
    d_inputs, gain_one_grad, shift_one_grad = back_one(d_normed_one)
    grad_in_own = (d_middle + d_inputs).astype(BF)
    grad_in = tokens_out(grad_in_own)

    def half_slot(value):
        value = value.reshape(shards, 1, -1)
        mask = lax.broadcasted_iota(jnp.int32, (1, CORES, 1), 1) == core
        return jnp.where(mask, value, 0.0).reshape(shards, -1)

    def full_slot(value):
        return value.reshape(shards, -1)

    packed = jnp.concatenate(
        [
            full_slot(gain_one_grad),
            full_slot(shift_one_grad),
            half_slot(query_bias_grad),
            half_slot(value_bias_grad),
            full_slot(out_bias_grad),
            full_slot(gain_two_grad),
            full_slot(shift_two_grad),
            full_slot(down_bias_grad),
            half_slot(up_bias_grad),
        ],
        axis=1,
    )
    def sum_plane(values, bits):
        for bit in bits:
            values = values + plane(values, 1 << bit)
        return values

    def sum_line(values):
        total = lax.dynamic_index_in_dim(values, shard, 0, False)
        for hop in range(1, shards):
            total = total + along(lax.dynamic_index_in_dim(values, (shard + hop) % shards, 0, False), hop)
        return total

    packed = packed + swap(packed)
    if square:
        out_part = out_red.third(qkv_red.sent)
        fc2_first = spread_first(after(fc2_part, (qkv_red.sent, out_red.mine)))
        qkv_part = qkv_red.third((grad_in,))
        packed = sum_plane(packed, [0])
        fc1_first = spread_first(after(fc1_part, (fc2_first[1:], qkv_red.mine, packed)))
        fc2_pair = spread_second(*fc2_first)
        packed = sum_plane(packed, [1])
        out_first = spread_first(after(out_part, (fc1_first[1:], fc2_pair[0], packed)))
        summed = sum_line(after(packed, qkv_part))
        fc1_pair = spread_second(*fc1_first)
        fc2_weight_grad = spread_last(*fc2_pair, None)
        fc1_weight_grad = spread_last(*fc1_pair, fc1_chunk)
        out_pair = spread_second(*out_first)
        qkv_first = spread_first(after(qkv_part, (out_pair[0], fc1_pair[0], fc2_weight_grad)))
        out_weight_grad = spread_last(*out_pair, None)
        qkv_own, qkv_other = spread_second(*after(qkv_first, (fc1_weight_grad, out_pair[1])))
        qkv_weight_grad = spread_last(qkv_own, after(qkv_other, out_weight_grad), qkv_chunk)
    else:
        summed = sum_line(sum_plane(packed, range(chips.bit_length() - 1)))
        fc2_weight_grad = spread_any(sum_any(activated, grad_both), None)
        fc1_weight_grad = spread_any(sum_any(normed_two, d_pre), fc1_chunk)
        out_weight_grad = spread_any(sum_any(context, d_attn), None)
        qkv_weight_grad = spread_any(sum_any(normed_one, d_projected), qkv_chunk)
    sums = [summed[edges[i] : edges[i + 1]] for i in range(len(vectors))]
    return (
        result,
        grad_in,
        sums[0],
        sums[1],
        qkv_weight_grad,
        sums[2],
        sums[3],
        out_weight_grad,
        sums[4],
        sums[5],
        sums[6],
        fc1_weight_grad,
        sums[8],
        fc2_weight_grad,
        sums[7],
    )


def solution(mesh):
    shards = mesh.shape["shard"]
    chips = mesh.shape["rep"] // CORES
    inner = Mesh(mesh.devices.reshape(chips, CORES, shards), ALL)
    token_spec = P(None, ALL, None)
    args = [token_spec, P(None, ("ch", "co"))]
    for dims in (1, 1, 2, 1, 1, 2, 1, 1, 1, 2, 1, 2, 1):
        args.append(P("sh", None) if dims == 2 else P("sh"))
    args.append(token_spec)
    outs = [token_spec, token_spec]
    for dims in (1, 1, 2, 1, 1, 2, 1, 1, 1, 2, 1, 2, 1):
        outs.append(P("sh", None) if dims == 2 else P("sh"))

    def run(*values):
        return local(*values, chips=chips, shards=shards)

    return jax.shard_map(run, mesh=inner, in_specs=tuple(args), out_specs=tuple(outs), check_vma=False)
```
